256 devices in a mesh: leaf: 64 (over y, z, core), probe: 4 (over x).
Axes of the slice: x: 4, y: 4, z: 8, core: 2. Of those that a mesh axis runs over, the one named last changes fastest.
Arguments:
- coords: float32 [3, 262144], P(None, 'leaf')
- site_order: int32 [1024, 256], P('leaf'), may hold values from 0 to 255, each once within a row
- leaf_pairs: int32 [2, 6144], P(None, 'leaf'), may hold values from 0 to 1023, as said below
- pair_count: int32 [64], P('leaf'), may hold values from 31 to 96, as said below
- probes: float32 [64, 262144], P('probe', 'leaf'), may hold values from -16 to 16
Outputs:
- solution: float32 [64, 262144], P('probe', 'leaf')
- residual: float32 [64, 262144], P('probe', 'leaf')
The draws below stay inside these ranges and needn't reach their ends.
Inputs may be any that keep to these rules, and one draw needn't show every extreme that they name: `leaf_pairs`: each leaf index owns 96 slots; its first pair_count slots hold distinct pairs (i, j) with i among that index's own 16 leaves and i <= j <= i + 5, j < 1024, every own leaf listed with itself once and with the next leaf where there is one; the later slots hold the index's first leaf twice. `pair_count`: pairs listed for each leaf index; some index lists 96 in every draw. Each row of site_order lists 0 to 255 once.
All inputs are finite; a program needn't handle non-finite values.
Results may differ from the reference program's by a relative error of at most 0.0003.
Values sent between devices are 32-bit elements; how exact they have to be, the bound alone decides.
No kernel may reach another device: no remote copies, remote signals or barrier semaphores. Data moves between devices by JAX's collectives and lax.ppermute only.
A program may use at most 64 MiB of HBM per device.

```python
import math
import jax
import jax.numpy as jnp
from jax import lax

LEAF = 256
REACH = 5
PROBES = 64
ITERS = 2
LEAF_DEV = 16
LEAVES = 1024
SITES = 262144


UNIT = 0.025


SIDE = 0.5


def slab_layout(key):
    groups = LEAVES // LEAF_DEV
    k_wide, k_dense, k_force = jax.random.split(jax.random.fold_in(key, 7), 3)
    widths = jax.random.randint(k_wide, (LEAVES,), 2, REACH + 1)
    flagged = jax.random.randint(k_dense, (groups,), 0, 8) == 0
    forced = jax.random.randint(k_force, (), 0, groups - 1)
    leaf_ids = jnp.arange(LEAVES)
    owner = leaf_ids // LEAF_DEV
    follow = (leaf_ids >= (forced + 1) * LEAF_DEV) & (leaf_ids < (forced + 1) * LEAF_DEV + REACH - 1)
    crowded = flagged[owner] | (owner == forced) | follow
    widths = jnp.where(crowded, 1, widths)
    ends = jnp.cumsum(widths)
    start_offsets = ends - widths
    return (widths, start_offsets, ends)


def pair_table(key):
    widths, start_offsets, ends = slab_layout(key)
    groups = LEAVES // LEAF_DEV
    slots = LEAF_DEV * (REACH + 1)
    leaf_ids = jnp.arange(LEAVES)
    offsets = jnp.arange(REACH + 1)
    partner = leaf_ids[:, None] + offsets[None, :]
    inside = partner < LEAVES
    capped = jnp.minimum(partner, LEAVES - 1)
    near = start_offsets[capped] - ends[:, None] < REACH
    valid = (inside & ((offsets[None, :] == 0) | near)).reshape(groups, slots)
    rows = jnp.broadcast_to(leaf_ids[:, None], partner.shape).reshape(groups, slots)
    cols = capped.reshape(groups, slots)
    sorted_rank = jnp.argsort(1 - valid.astype(jnp.int32), axis=1, stable=True)
    rows = jnp.take_along_axis(rows, sorted_rank, axis=1)
    cols = jnp.take_along_axis(cols, sorted_rank, axis=1)
    count = jnp.sum(valid.astype(jnp.int32), axis=1)
    live = jnp.arange(slots)[None, :] < count[:, None]
    first = (jnp.arange(groups) * LEAF_DEV)[:, None]
    rows = jnp.where(live, rows, first)
    cols = jnp.where(live, cols, first)
    return (jnp.stack([rows.reshape(-1), cols.reshape(-1)]).astype(jnp.int32), count.astype(jnp.int32))


def draw_leaf_pairs(key, part):
    return pair_table(key)[0]


def draw_pair_count(key, part):
    return pair_table(key)[1]


def draw_coords(key, part):
    widths, start_offsets, ends = slab_layout(key)
    k_along, k_across = jax.random.split(jax.random.fold_in(key, 11))
    along = jax.random.uniform(k_along, (LEAVES, LEAF), jnp.float32)
    first = (start_offsets[:, None].astype(jnp.float32) + widths[:, None].astype(jnp.float32) * along) * UNIT
    across = jax.random.uniform(k_across, (2, LEAVES, LEAF), jnp.float32) * SIDE
    return jnp.concatenate([first[None], across], axis=0).reshape(3, SITES).astype(jnp.float32)


def draw_probes(key, part):
    k_base, k_row, k_leaf = jax.random.split(jax.random.fold_in(key, 13), 3)
    base = jnp.clip(jax.random.normal(k_base, (PROBES, LEAVES, LEAF), jnp.float32), -4.0, 4.0)
    row_scale = jnp.exp(jax.random.uniform(k_row, (PROBES, 1, 1), jnp.float32, -1.15, 1.15))
    leaf_scale = jnp.exp(jax.random.uniform(k_leaf, (1, LEAVES, 1), jnp.float32, -1.15, 1.15))
    rising = jnp.exp(0.55 * jnp.arange(LEAVES, dtype=jnp.float32) / LEAVES)[None, :, None]
    values = jnp.clip(base * row_scale * leaf_scale * rising, -16.0, 16.0)
    return values.reshape(PROBES, SITES).astype(jnp.float32)


def setup_inputs(seed: int = 0) -> dict:
    streams_of = jax.random.split(jax.random.key(seed), 6)
    return {
        "coords": draw_coords(jax.random.fold_in(streams_of[5], 71), 0),
        "site_order": jax.vmap(lambda own: jax.random.permutation(own, LEAF))(jax.random.split(streams_of[1], LEAVES)).reshape((LEAVES, LEAF)).astype(jnp.int32),
        "leaf_pairs": draw_leaf_pairs(jax.random.fold_in(streams_of[5], 71), 0),
        "pair_count": draw_pair_count(jax.random.fold_in(streams_of[5], 71), 0),
        "probes": draw_probes(jax.random.fold_in(streams_of[5], 71), 0),
    }


UNIT = 0.025
LENGTH = 0.12
NUGGET = 0.5
UPPER_LIMIT = lax.Precision.HIGHEST

def kernel_tiles(left, right):
    diff = left[:, :, :, None] - right[:, :, None, :]
    dist = jnp.sqrt(lax.optimization_barrier(jnp.sum(diff * diff, axis=0)))
    taper = REACH * UNIT
    scaled = dist * (math.sqrt(3.0) / LENGTH)
    remain = jnp.maximum(1.0 - dist / taper, 0.0)
    return (1.0 + scaled) * jnp.exp(-scaled) * remain ** 4 * (1.0 + 4.0 * dist / taper)

def apply_operator(points, leaf_pairs, pair_count, field):
    groups = pair_count.shape[0]
    slots = leaf_pairs.shape[1] // groups

    def one_group(group, grand_total):

        def one_pair(index, acc):
            slot = group * slots + index
            row = leaf_pairs[0, slot]
            col = leaf_pairs[1, slot]
            tile = kernel_tiles(points[:, row][:, None], points[:, col][:, None])[0]
            to_row = jnp.dot(field[:, col], tile.T, precision=UPPER_LIMIT)
            column_target = jnp.dot(field[:, row], tile, precision=UPPER_LIMIT)
            column_target = jnp.where(row != col, column_target, jnp.zeros_like(column_target))
            acc = acc.at[:, row].add(to_row)
            return acc.at[:, col].add(column_target)
        return lax.fori_loop(0, pair_count[group], one_pair, grand_total)
    summed = lax.fori_loop(0, groups, one_group, jnp.zeros_like(field))
    return NUGGET * field + summed

def reference(coords, site_order, leaf_pairs, pair_count, probes):
    points = jnp.take_along_axis(coords.reshape(3, LEAVES, LEAF), site_order[None], axis=2)
    right = probes.reshape(PROBES, LEAVES, LEAF)
    solution = jnp.zeros_like(right)
    residual = right
    direction = right
    norm_now = lax.optimization_barrier(jnp.sum(residual * residual, axis=(1, 2)))
    for step in range(ITERS):
        image = apply_operator(points, leaf_pairs, pair_count, direction)
        alpha = norm_now / lax.optimization_barrier(jnp.sum(direction * image, axis=(1, 2)))
        solution = solution + alpha[:, None, None] * direction
        residual = residual - alpha[:, None, None] * image
        if step + 1 < ITERS:
            norm_next = lax.optimization_barrier(jnp.sum(residual * residual, axis=(1, 2)))
            direction = residual + (norm_next / norm_now)[:, None, None] * direction
            norm_now = norm_next
    return (solution.reshape(PROBES, SITES), residual.reshape(PROBES, SITES))
```

```python
import functools
import math

import jax
import jax.numpy as jnp
from jax import lax
from jax.experimental import pallas as pl
from jax.experimental.pallas import tpu as pltpu
from jax.sharding import PartitionSpec as P

REACH = 5
STEPS = REACH + 1
UNIT = 0.025
LENGTH = 0.12
NUGGET = 0.5
W = 256
TAPER = REACH * UNIT
DECAY = math.sqrt(3.0) * TAPER / LENGTH
LOG2E = math.log2(math.e)
CHUNK = 16
FLOOR_INV = 1e18


def split2(x):
    hi = x.astype(jnp.bfloat16)
    lo = (x - hi.astype(jnp.float32)).astype(jnp.bfloat16)
    return hi, lo


def split3(x):
    hi = x.astype(jnp.bfloat16)
    rest = x - hi.astype(jnp.float32)
    mid = rest.astype(jnp.bfloat16)
    lo = (rest - mid.astype(jnp.float32)).astype(jnp.bfloat16)
    return hi, mid, lo


def load_values(v_ref, src_ref, leaves, first):
    for k in range(leaves):
        hi, lo = split2(src_ref[:, k * W : (k + 1) * W])
        v_ref[first + k] = jnp.concatenate([hi, lo], axis=0)


def place_points(pts_ref, coords_ref, order_ref, leaves, first):
    sub = lax.broadcasted_iota(jnp.int32, (W, W), 0)
    for k in range(leaves):
        sel = (sub == order_ref[k : k + 1, :]).astype(jnp.float32).astype(jnp.bfloat16)
        hi, mid, lo = split3(coords_ref[:, k * W : (k + 1) * W])
        dot = functools.partial(jnp.dot, preferred_element_type=jnp.float32)
        got = dot(hi, sel) + dot(mid, sel) + dot(lo, sel)
        pts_ref[first + k, 0:3, :] = got * (1.0 / TAPER)


def spread_rows(bc_ref, pts_ref, leaf):
    cols = jnp.transpose(pts_ref[leaf])
    for c in range(3):
        bc_ref[c] = jnp.broadcast_to(cols[:, c : c + 1], (W, 128))


def make_tile(t_ref, bc_ref, other, scale):
    f0 = scale
    f1 = scale * (4.0 + DECAY)
    f2 = scale * (4.0 * DECAY)
    b = [jnp.broadcast_to(other[c : c + 1, :], (CHUNK, W)) for c in range(3)]
    for k in range(W // CHUNK):
        rows = slice(k * CHUNK, (k + 1) * CHUNK)
        u = None
        for c in range(3):
            a = bc_ref[c, rows, :]
            d = jnp.concatenate([a, a], axis=1) - b[c]
            u = d * d if u is None else u + d * d
        u = jnp.minimum(u, 1.0)
        q = u * jnp.minimum(lax.rsqrt(u), FLOOR_INV)
        t = 1.0 - q
        t = t * t
        t = t * t
        e = jnp.exp2(q * (-DECAY * LOG2E))
        x = (q * f1 + f0 + u * f2) * (t * e)
        hi, lo = split2(x)
        t_ref[rows, 0:W] = hi
        t_ref[rows, W : 2 * W] = lo


def use_tile(t_ref, v_ref, acc_ref, i, j):
    hi = t_ref[:, 0:W]
    lo = t_ref[:, W : 2 * W]
    dot = functools.partial(lax.dot_general, preferred_element_type=jnp.float32)
    nt = (((1,), (1,)), ((), ()))
    nn = (((1,), (0,)), ((), ()))
    n = acc_ref.shape[1]
    vj = v_ref[j]
    vi = v_ref[i]
    p = dot(vj, hi, nt)
    acc_ref[i] += p[:n] + p[n:] + dot(vj[:n], lo, nt)
    p = dot(vi, hi, nn)
    acc_ref[j] += p[:n] + p[n:] + dot(vi[:n], lo, nn)


def list_weights(flag_ref, pairs_ref, count_ref, base_ref, leaf_dev):
    def clear(s, _):
        flag_ref[s] = 0.0
        return 0

    lax.fori_loop(0, leaf_dev * STEPS, clear, 0)

    def put(s, _):
        row = pairs_ref[0, s] - base_ref[0]
        step = pairs_ref[1, s] - pairs_ref[0, s]
        flag_ref[row * STEPS + step] = jnp.where(step == 0, 0.5, 1.0)
        return 0

    lax.fori_loop(0, count_ref[0], put, 0)


def first_kernel(
    i0, i1, leaf_dev, with_prev, pairs_ref, count_ref, base_ref, coords_ref, order_ref, b_ref, *rest
):
    rest = list(rest)
    halo = i1 + REACH > leaf_dev
    if halo:
        hc_ref, ho_ref, hb_ref = rest[:3]
        rest = rest[3:]
    if with_prev:
        prev_ref = rest.pop(0)
    tiles_ref, acc_ref, flag_ref, pts_ref, bc_ref, v_ref = rest
    list_weights(flag_ref, pairs_ref, count_ref, base_ref, leaf_dev)
    load_values(v_ref, b_ref, leaf_dev, 0)
    place_points(pts_ref, coords_ref, order_ref, leaf_dev, 0)
    if halo:
        load_values(v_ref, hb_ref, REACH, leaf_dev)
        place_points(pts_ref, hc_ref, ho_ref, REACH, leaf_dev)
    if with_prev:
        acc_ref[...] = prev_ref[...]
    else:
        acc_ref[...] = jnp.zeros_like(acc_ref)

    def one_leaf(i, _):
        spread_rows(bc_ref, pts_ref, i)

        def one_step(d, _):
            j = i + d
            t_ref = tiles_ref.at[(i - i0) * STEPS + d]
            make_tile(t_ref, bc_ref, pts_ref[j], flag_ref[i * STEPS + d])
            use_tile(t_ref, v_ref, acc_ref, i, j)
            return 0

        return lax.fori_loop(0, STEPS, one_step, 0)

    lax.fori_loop(i0, i1, one_leaf, 0)


def second_kernel(i0, i1, leaf_dev, with_prev, tiles_ref, w_ref, *rest):
    rest = list(rest)
    halo = i1 + REACH > leaf_dev
    if halo:
        hw_ref = rest.pop(0)
    if with_prev:
        prev_ref = rest.pop(0)
    acc_ref, v_ref = rest
    load_values(v_ref, w_ref, leaf_dev, 0)
    if halo:
        load_values(v_ref, hw_ref, REACH, leaf_dev)
    if with_prev:
        acc_ref[...] = prev_ref[...]
    else:
        acc_ref[...] = jnp.zeros_like(acc_ref)

    def one_leaf(i, _):
        def one_step(d, _):
            use_tile(tiles_ref.at[(i - i0) * STEPS + d], v_ref, acc_ref, i, i + d)
            return 0

        return lax.fori_loop(0, STEPS, one_step, 0)

    lax.fori_loop(i0, i1, one_leaf, 0)


VM = pl.BlockSpec(memory_space=pltpu.VMEM)
SM = pl.BlockSpec(memory_space=pltpu.SMEM)


def first_call(i0, i1, leaf_dev, n, smem, own, halo, prev):
    extent = leaf_dev + REACH
    tiles = (i1 - i0) * STEPS
    ops = [*smem, *own, *halo, *([] if prev is None else [prev])]
    return pl.pallas_call(
        functools.partial(first_kernel, i0, i1, leaf_dev, prev is not None),
        out_shape=(
            jax.ShapeDtypeStruct((tiles, W, 2 * W), jnp.bfloat16),
            jax.ShapeDtypeStruct((extent, n, W), jnp.float32),
        ),
        in_specs=[SM] * len(smem) + [VM] * (len(ops) - len(smem)),
        out_specs=(VM, VM),
        scratch_shapes=[
            pltpu.SMEM((leaf_dev * STEPS,), jnp.float32),
            pltpu.VMEM((extent, 8, W), jnp.float32),
            pltpu.VMEM((3, W, 128), jnp.float32),
            pltpu.VMEM((extent, 2 * n, W), jnp.bfloat16),
        ],
        compiler_params=pltpu.CompilerParams(vmem_limit_bytes=40 << 20),
        cost_estimate=pl.CostEstimate(flops=tiles << 26, transcendentals=tiles << 17, bytes_accessed=tiles << 18),
        name=f"evaluate_{i0}",
    )(*ops)


def second_call(i0, i1, leaf_dev, n, tiles, own, halo, prev):
    extent = leaf_dev + REACH
    ops = [tiles, own, *halo, *([] if prev is None else [prev])]
    return pl.pallas_call(
        functools.partial(second_kernel, i0, i1, leaf_dev, prev is not None),
        out_shape=jax.ShapeDtypeStruct((extent, n, W), jnp.float32),
        in_specs=[VM] * len(ops),
        out_specs=VM,
        scratch_shapes=[pltpu.VMEM((extent, 2 * n, W), jnp.bfloat16)],
        compiler_params=pltpu.CompilerParams(vmem_limit_bytes=40 << 20),
        cost_estimate=pl.CostEstimate(flops=tiles.shape[0] << 26, transcendentals=0, bytes_accessed=tiles.size * 2),
        name=f"apply_{i0}",
    )(*ops)


def shift(value, by):
    length = lax.axis_size("leaf")
    return lax.ppermute(value, "leaf", [(i, i + by) for i in range(length) if 0 <= i + by < length])


def sum_over_leaf(value):
    length = lax.axis_size("leaf")
    value = value + lax.ppermute(value, "leaf", [(i, i ^ 1) for i in range(length)])
    copies = jnp.broadcast_to(value, (length // 2, *value.shape))
    groups = [[i for i in range(length) if i % 2 == c] for c in range(2)]
    got = lax.all_to_all(
        copies, "leaf", split_axis=0, concat_axis=0, tiled=True, axis_index_groups=groups
    )
    return jnp.sum(got, axis=0)


def to_rows(acc):
    return jnp.moveaxis(acc, 1, 0).reshape(acc.shape[1], -1)


def body(coords, site_order, leaf_pairs, pair_count, probes):
    leaf_dev, width = site_order.shape
    n = probes.shape[0]
    edge = REACH * width
    base = (lax.axis_index("leaf") * leaf_dev).astype(jnp.int32).reshape(1)
    packed = jnp.concatenate(
        [probes[:, :edge], coords[:, :edge], site_order[:REACH].reshape(1, edge).astype(jnp.float32)]
    )
    arrived = shift(packed, -1)
    halo = (arrived[n : n + 3], arrived[n + 3].reshape(REACH, width).astype(jnp.int32), arrived[:n])
    smem = (leaf_pairs, pair_count, base)
    own = (coords, site_order, probes)
    cut0, cut1 = leaf_dev // 2, leaf_dev - REACH

    def operator(run, far, field):
        t0, acc = run(0, cut0, (), None)
        t1, acc = run(cut1, leaf_dev, far, acc)
        back = shift(to_rows(acc[leaf_dev:]), 1)
        part_far = acc[leaf_dev:]
        t2, acc = run(cut0, cut1, (), acc)
        part_own = to_rows(acc[:leaf_dev])
        return (t0, t1, t2), part_own, part_far, back

    def run_first(i0, i1, far, prev):
        return first_call(i0, i1, leaf_dev, n, smem, own, far, prev)

    tiles, part, _, back = operator(run_first, halo, probes)
    image = NUGGET * probes + part
    image = jnp.concatenate([image[:, :edge] + back, image[:, edge:]], axis=1)
    image_far = shift(image[:, :edge], -1)
    by_start = {0: tiles[0], cut1: tiles[1], cut0: tiles[2]}

    def run_second(i0, i1, far, prev):
        return None, second_call(i0, i1, leaf_dev, n, by_start[i0], image, far, prev)

    _, part2, part2_far, back2 = operator(run_second, (image_far,), image)
    image2_here = NUGGET * image + part2
    far_dot = jnp.sum(jnp.moveaxis(part2_far, 1, 0) * image_far.reshape(n, REACH, width), axis=(1, 2))
    sums = jnp.stack(
        [
            jnp.sum(probes * probes, axis=1),
            jnp.sum(probes * image, axis=1),
            jnp.sum(image * image, axis=1),
            jnp.sum(image * image2_here, axis=1) + far_dot,
        ]
    )
    rr, bw, ww, wz = sum_over_leaf(sums)
    image2 = jnp.concatenate([image2_here[:, :edge] + back2, image2_here[:, edge:]], axis=1)
    alpha = rr / bw
    rr1 = rr - 2.0 * alpha * bw + alpha * alpha * ww
    beta = rr1 / rr
    g = 1.0 + beta
    curve = g * g * bw - 2.0 * g * alpha * ww + alpha * alpha * wz
    alpha1 = rr1 / curve
    c = lambda x: x[:, None]
    direction1 = c(g) * probes - c(alpha) * image
    image1 = c(g) * image - c(alpha) * image2
    solution = c(alpha) * probes + c(alpha1) * direction1
    residual = probes - c(alpha) * image - c(alpha1) * image1
    return solution, residual


def solution(mesh):
    in_specs = (P(None, "leaf"), P("leaf", None), P(None, "leaf"), P("leaf"), P("probe", "leaf"))
    out_specs = (P("probe", "leaf"), P("probe", "leaf"))
    return jax.shard_map(body, mesh=mesh, in_specs=in_specs, out_specs=out_specs, check_vma=False)
```

```python
import functools
import math

import jax
import jax.numpy as jnp
from jax import lax
from jax.experimental import pallas as pl
from jax.experimental.pallas import tpu as pltpu
from jax.sharding import PartitionSpec as P

REACH = 5
STEPS = REACH + 1
UNIT = 0.025
LENGTH = 0.12
NUGGET = 0.5
W = 256
TAPER = REACH * UNIT
DECAY = math.sqrt(3.0) * TAPER / LENGTH
LOG2E = math.log2(math.e)
CHUNK = 16
HALF = W // 2
FLOOR_INV = 1e18


def split2(x):
    hi = x.astype(jnp.bfloat16)
    lo = (x - hi.astype(jnp.float32)).astype(jnp.bfloat16)
    return hi, lo


def split3(x):
    hi = x.astype(jnp.bfloat16)
    rest = x - hi.astype(jnp.float32)
    mid = rest.astype(jnp.bfloat16)
    lo = (rest - mid.astype(jnp.float32)).astype(jnp.bfloat16)
    return hi, mid, lo


def load_values(v_ref, src_ref, leaves, first):
    n = v_ref.shape[1] // 2
    for k in range(leaves):
        hi, lo = split2(src_ref[0:n, k * W : (k + 1) * W])
        v_ref[first + k] = jnp.concatenate([hi, lo], axis=0)


def prepare_kernel(
    pairs_ref, count_ref, base_ref, coords_hbm, order_hbm, b_hbm,
    listed_ref, pts_ref, cols_ref, v_ref, edge_ref, coords_ref, order_ref, b_ref, sems,
):
    copies = [
        pltpu.make_async_copy(coords_hbm, coords_ref, sems.at[0]),
        pltpu.make_async_copy(order_hbm, order_ref, sems.at[1]),
        pltpu.make_async_copy(b_hbm, b_ref, sems.at[2]),
    ]
    for copy in copies:
        copy.start()
    slots = pairs_ref.shape[1]
    row = pairs_ref[0:1, :]
    place = (row - base_ref[0]) * STEPS + pairs_ref[1:2, :] - row
    live = lax.broadcasted_iota(jnp.int32, (1, slots), 1) < count_ref[0]
    place = jnp.where(live, place, -1)
    hit = lax.broadcasted_iota(jnp.int32, (slots, slots), 0) == place
    found = jnp.sum(hit.astype(jnp.float32), axis=1, keepdims=True)
    listed_ref[...] = jnp.broadcast_to(found, (slots, HALF))
    for copy in copies:
        copy.wait()
    leaves = order_ref.shape[0]
    n = b_ref.shape[0]
    sub = lax.broadcasted_iota(jnp.int32, (W, W), 0)
    dot = functools.partial(jnp.dot, preferred_element_type=jnp.float32)
    for k in range(leaves):
        at = slice(k * W, (k + 1) * W)
        sel = (sub == order_ref[k : k + 1, :]).astype(jnp.float32).astype(jnp.bfloat16)
        hi, mid, lo = split3(coords_ref[:, at] * (1.0 / TAPER))
        zero = jnp.zeros((5, W), jnp.float32)
        parts = [dot(p, sel) for p in (hi, mid, lo)]
        got = parts[0] + parts[1] + parts[2]
        pts_ref[k, 0:3, :] = got
        stack = jnp.concatenate([z for p in parts for z in (p, zero)], axis=0)
        cols_ref[k] = jnp.transpose(stack).astype(jnp.bfloat16)
        if k < REACH:
            edge_ref[0:n, at] = b_ref[:, at]
            edge_ref[n : n + 3, at] = got
    load_values(v_ref, b_ref, leaves, 0)


def spread_rows(bc_ref, cols):
    r = lax.broadcasted_iota(jnp.int32, (24, 3 * HALF), 0)
    c = lax.broadcasted_iota(jnp.int32, (24, 3 * HALF), 1)
    sel = ((r & 7) == (c >> 7)).astype(jnp.float32).astype(jnp.bfloat16)
    bc_ref[...] = jnp.dot(cols, sel, preferred_element_type=jnp.float32)


def make_tile(t_ref, bc_ref, other, listed, same):
    f0 = jnp.broadcast_to(listed, (CHUNK, HALF))
    coef = {}
    for weight in (0.5, 1.0) if same else (1.0,):
        f = f0 * weight if weight != 1.0 else f0
        coef[weight] = (f, f * (4.0 + DECAY), f * (4.0 * DECAY))
    b = [
        [jnp.broadcast_to(other[c : c + 1, h * HALF : (h + 1) * HALF], (CHUNK, HALF)) for c in range(3)]
        for h in range(2)
    ]
    for k in range(W // CHUNK):
        rows = slice(k * CHUNK, (k + 1) * CHUNK)
        lower = k * CHUNK >= HALF
        for h in range(2):
            at = slice(h * HALF, (h + 1) * HALF)
            at_lo = slice(W + h * HALF, W + (h + 1) * HALF)
            if same and lower and h == 0:
                t_ref[rows, at] = jnp.zeros((CHUNK, HALF), jnp.bfloat16)
                t_ref[rows, at_lo] = jnp.zeros((CHUNK, HALF), jnp.bfloat16)
                continue
            g0, g1, g2 = coef[0.5 if same and lower == bool(h) else 1.0]
            u = None
            for c in range(3):
                d = bc_ref[rows, c * HALF : (c + 1) * HALF] - b[h][c]
                u = d * d if u is None else u + d * d
            u = jnp.minimum(u, 1.0)
            q = u * jnp.minimum(lax.rsqrt(u), FLOOR_INV)
            t = 1.0 - q
            t = t * t
            t = t * t
            e = jnp.exp2(q * (-DECAY * LOG2E))
            x = (q * g1 + g0 + u * g2) * (t * e)
            hi, lo = split2(x)
            t_ref[rows, at] = hi
            t_ref[rows, at_lo] = lo


def products(t_ref, vi, vj):
    hi = t_ref[:, 0:W]
    lo = t_ref[:, W : 2 * W]
    dot = functools.partial(lax.dot_general, preferred_element_type=jnp.float32)
    nt = (((1,), (1,)), ((), ()))
    nn = (((1,), (0,)), ((), ()))
    n = vi.shape[0] // 2
    p = dot(vj, hi, nt)
    to_row = p[:n] + p[n:] + dot(vj[:n], lo, nt)
    p = dot(vi, hi, nn)
    to_col = p[:n] + p[n:] + dot(vi[:n], lo, nn)
    return to_row, to_col


def evaluate_kernel(i0, i1, leaf_dev, listed_ref, pts_ref, cols_ref, v_ref, *rest):
    rest = list(rest)
    shift_by = 0
    if i1 + REACH > leaf_dev:
        edge_ref = rest.pop(0)
        prev_ref = rest.pop(0)
        tiles_ref, acc_ref, bc_ref, pts_all, v_all = rest
        n = v_ref.shape[1] // 2
        own = leaf_dev - i0
        pts_all[0:own] = pts_ref[i0:leaf_dev]
        v_all[0:own] = v_ref[i0:leaf_dev]
        for k in range(REACH):
            pts_all[own + k, 0:3, :] = edge_ref[n : n + 3, k * W : (k + 1) * W]
        load_values(v_all, edge_ref, REACH, own)
        pts_ref, v_ref = pts_all, v_all
        shift_by = i0
    else:
        if i0:
            prev_ref = rest.pop(0)
        tiles_ref, acc_ref, bc_ref = rest
    if i0:
        acc_ref[...] = prev_ref[...]
    else:
        acc_ref[...] = jnp.zeros_like(acc_ref)
    tiles_ref[0] = jnp.zeros_like(tiles_ref[0])

    def last_of(i):
        to_row, to_col = products(tiles_ref.at[(i - i0) * STEPS], v_ref[i - 1 - shift_by], v_ref[i - 1 + REACH - shift_by])
        acc_ref[i - 1] += to_row
        acc_ref[i - 1 + REACH] += to_col

    def one_leaf(i, _):
        slot = (i - i0) * STEPS
        spread_rows(bc_ref, cols_ref[i])
        vi = v_ref[i - shift_by]

        def make(d):
            j = i + d - shift_by
            listed = listed_ref[pl.ds(i * STEPS + d, 1), :]
            make_tile(tiles_ref.at[slot + (1 + d)], bc_ref, pts_ref.at[j], listed, d == 0)

        make(0)
        before = jnp.maximum(i - 1, i0)
        to_row, to_col = products(
            tiles_ref.at[slot], v_ref[before - shift_by], v_ref[before + REACH - shift_by]
        )
        acc_ref[before] += to_row
        acc_ref[before + REACH] += to_col
        total = None
        for d in range(REACH):
            make(d + 1)
            to_row, to_col = products(tiles_ref.at[slot + (1 + d)], vi, v_ref[i + d - shift_by])
            total = to_row if total is None else total + to_row
            acc_ref[i + d] += to_col
        acc_ref[i] += total
        return 0

    lax.fori_loop(i0, i1, one_leaf, 0)
    last_of(i1)


def apply_kernel(i0, i1, leaf_dev, tiles_ref, w_ref, *rest):
    rest = list(rest)
    if i1 + REACH > leaf_dev:
        far_ref = rest.pop(0)
    if i0:
        prev_ref = rest.pop(0)
    acc_ref, v_ref = rest
    load_values(v_ref, w_ref, leaf_dev, 0)
    if i1 + REACH > leaf_dev:
        load_values(v_ref, far_ref, REACH, leaf_dev)
    if i0:
        acc_ref[...] = prev_ref[...]
    else:
        acc_ref[...] = jnp.zeros_like(acc_ref)

    def one_leaf(i, _):
        slot = (i - i0) * STEPS
        vi = v_ref[i]
        total = None
        for d in range(STEPS):
            to_row, to_col = products(tiles_ref.at[slot + (1 + d)], vi, v_ref[i + d])
            total = to_row if total is None else total + to_row
            acc_ref[i + d] += to_col
        acc_ref[i] += total
        return 0

    lax.fori_loop(i0, i1, one_leaf, 0)


VM = pl.BlockSpec(memory_space=pltpu.VMEM)
SM = pl.BlockSpec(memory_space=pltpu.SMEM)
ANY = pl.BlockSpec(memory_space=pl.ANY)
PARAMS = pltpu.CompilerParams(vmem_limit_bytes=8 << 20)


def prepare_call(pairs, count, base, coords, order, b):
    leaves = order.shape[0]
    n = b.shape[0]
    return pl.pallas_call(
        prepare_kernel,
        out_shape=(
            jax.ShapeDtypeStruct((pairs.shape[1], HALF), jnp.float32),
            jax.ShapeDtypeStruct((leaves, 8, W), jnp.float32),
            jax.ShapeDtypeStruct((leaves, W, 24), jnp.bfloat16),
            jax.ShapeDtypeStruct((leaves, 2 * n, W), jnp.bfloat16),
            jax.ShapeDtypeStruct((n + 3, REACH * W), jnp.float32),
        ),
        in_specs=[VM, SM, SM, ANY, ANY, ANY],
        out_specs=(VM,) * 5,
        scratch_shapes=[
            pltpu.VMEM(coords.shape, jnp.float32),
            pltpu.VMEM(order.shape, jnp.int32),
            pltpu.VMEM(b.shape, jnp.float32),
            pltpu.SemaphoreType.DMA((3,)),
        ],
        compiler_params=PARAMS,
        name="prepare",
    )(pairs, count, base, coords, order, b)


def evaluate_call(i0, i1, leaf_dev, n, prepared, far, prev):
    extent = leaf_dev + REACH
    tiles = (i1 - i0) * STEPS
    ops = [*prepared, *far, *([] if prev is None else [prev])]
    scratch = [pltpu.VMEM((W, 3 * HALF), jnp.float32)]
    if far:
        held = leaf_dev - i0 + REACH
        scratch += [pltpu.VMEM((held, 8, W), jnp.float32), pltpu.VMEM((held, 2 * n, W), jnp.bfloat16)]
    return pl.pallas_call(
        functools.partial(evaluate_kernel, i0, i1, leaf_dev),
        out_shape=(
            jax.ShapeDtypeStruct((tiles + 1, W, 2 * W), jnp.bfloat16),
            jax.ShapeDtypeStruct((extent, n, W), jnp.float32),
        ),
        in_specs=[VM] * len(ops),
        out_specs=(VM, VM),
        scratch_shapes=scratch,
        compiler_params=PARAMS,
        cost_estimate=pl.CostEstimate(flops=tiles << 28, transcendentals=tiles << 17, bytes_accessed=tiles << 18),
        name=f"evaluate_{i0}",
    )(*ops)


def apply_call(i0, i1, leaf_dev, n, tiles, own, far, prev):
    extent = leaf_dev + REACH
    ops = [tiles, own, *far, *([] if prev is None else [prev])]
    return pl.pallas_call(
        functools.partial(apply_kernel, i0, i1, leaf_dev),
        out_shape=jax.ShapeDtypeStruct((extent, n, W), jnp.float32),
        in_specs=[VM] * len(ops),
        out_specs=VM,
        scratch_shapes=[pltpu.VMEM((extent, 2 * n, W), jnp.bfloat16)],
        compiler_params=PARAMS,
        cost_estimate=pl.CostEstimate(flops=tiles.shape[0] << 27, transcendentals=0, bytes_accessed=tiles.size * 2),
        name=f"apply_{i0}",
    )(*ops)


def shift(value, by):
    length = lax.axis_size("leaf")
    return lax.ppermute(value, "leaf", [(i, i + by) for i in range(length) if 0 <= i + by < length])


def sum_over_leaf(value):
    length = lax.axis_size("leaf")
    value = value + lax.ppermute(value, "leaf", [(i, i ^ 1) for i in range(length)])
    copies = jnp.broadcast_to(value, (length // 2, *value.shape))
    groups = [[i for i in range(length) if i % 2 == c] for c in range(2)]
    got = lax.all_to_all(
        copies, "leaf", split_axis=0, concat_axis=0, tiled=True, axis_index_groups=groups
    )
    return jnp.sum(got, axis=0)


def to_rows(acc):
    return jnp.moveaxis(acc, 1, 0).reshape(acc.shape[1], -1)


def body(coords, site_order, leaf_pairs, pair_count, probes):
    leaf_dev, width = site_order.shape
    n = probes.shape[0]
    edge = REACH * width
    base = (lax.axis_index("leaf") * leaf_dev).astype(jnp.int32).reshape(1)
    *prepared, packed = prepare_call(leaf_pairs, pair_count, base, coords, site_order, probes)
    far = (shift(packed, -1),)
    cut0, cut1 = leaf_dev // 2, leaf_dev - REACH

    def operator(run, far):
        t0, acc = run(0, cut0, (), None)
        t1, acc = run(cut1, leaf_dev, far, acc)
        back = shift(to_rows(acc[leaf_dev:]), 1)
        part_far = acc[leaf_dev:]
        t2, acc = run(cut0, cut1, (), acc)
        part_own = to_rows(acc[:leaf_dev])
        return (t0, t1, t2), part_own, part_far, back

    def run_first(i0, i1, far, prev):
        return evaluate_call(i0, i1, leaf_dev, n, prepared, far, prev)

    tiles, part, _, back = operator(run_first, far)
    image = NUGGET * probes + part
    image = jnp.concatenate([image[:, :edge] + back, image[:, edge:]], axis=1)
    image_far = shift(image[:, :edge], -1)
    by_start = {0: tiles[0], cut1: tiles[1], cut0: tiles[2]}

    def run_second(i0, i1, far, prev):
        return None, apply_call(i0, i1, leaf_dev, n, by_start[i0], image, far, prev)

    _, part2, part2_far, back2 = operator(run_second, (image_far,))
    image2_here = NUGGET * image + part2
    far_dot = jnp.sum(jnp.moveaxis(part2_far, 1, 0) * image_far.reshape(n, REACH, width), axis=(1, 2))
    sums = jnp.stack(
        [
            jnp.sum(probes * probes, axis=1),
            jnp.sum(probes * image, axis=1),
            jnp.sum(image * image, axis=1),
            jnp.sum(image * image2_here, axis=1) + far_dot,
        ]
    )
    rr, bw, ww, wz = sum_over_leaf(sums)
    image2 = jnp.concatenate([image2_here[:, :edge] + back2, image2_here[:, edge:]], axis=1)
    alpha = rr / bw
    rr1 = rr - 2.0 * alpha * bw + alpha * alpha * ww
    beta = rr1 / rr
    g = 1.0 + beta
    curve = g * g * bw - 2.0 * g * alpha * ww + alpha * alpha * wz
    alpha1 = rr1 / curve
    c = lambda x: x[:, None]
    direction1 = c(g) * probes - c(alpha) * image
    image1 = c(g) * image - c(alpha) * image2
    solution = c(alpha) * probes + c(alpha1) * direction1
    residual = probes - c(alpha) * image - c(alpha1) * image1
    return solution, residual


def solution(mesh):
    in_specs = (P(None, "leaf"), P("leaf", None), P(None, "leaf"), P("leaf"), P("probe", "leaf"))
    out_specs = (P("probe", "leaf"), P("probe", "leaf"))
    return jax.shard_map(body, mesh=mesh, in_specs=in_specs, out_specs=out_specs, check_vma=False)
```

```python
import functools
import math

import jax
import jax.numpy as jnp
from jax import lax
from jax.experimental import pallas as pl
from jax.experimental.pallas import tpu as pltpu
from jax.sharding import PartitionSpec as P

REACH = 5
STEPS = REACH + 1
UNIT = 0.025
LENGTH = 0.12
NUGGET = 0.5
W = 256
TAPER = REACH * UNIT
DECAY = math.sqrt(3.0) * TAPER / LENGTH
LOG2E = math.log2(math.e)
CHUNK = 16
HALF = W // 2
FLOOR_INV = 1e18
KAPPA = DECAY * LOG2E
PEAK = KAPPA**6 / (4.0 * DECAY) * 2.0**KAPPA
ROUNDER = 1.5 * 2.0 ** (23 + math.ceil(math.log2(PEAK)) - 8)


def split2(x):
    hi = x.astype(jnp.bfloat16)
    lo = (x - hi.astype(jnp.float32)).astype(jnp.bfloat16)
    return hi, lo


def split3(x):
    hi = x.astype(jnp.bfloat16)
    rest = x - hi.astype(jnp.float32)
    mid = rest.astype(jnp.bfloat16)
    lo = (rest - mid.astype(jnp.float32)).astype(jnp.bfloat16)
    return hi, mid, lo


def load_values(v_ref, src_ref, leaves, first):
    n = v_ref.shape[1] // 2
    for k in range(leaves):
        hi, lo = split2(src_ref[0:n, k * W : (k + 1) * W])
        v_ref[first + k] = jnp.concatenate([hi, lo], axis=0)


def prepare_kernel(
    pairs_ref, count_ref, base_ref, coords_hbm, order_hbm, b_hbm,
    listed_ref, pts_ref, cols_ref, v_ref, center_ref, edge_ref, coords_ref, order_ref, b_ref, sems,
):
    copies = [
        pltpu.make_async_copy(coords_hbm, coords_ref, sems.at[0]),
        pltpu.make_async_copy(order_hbm, order_ref, sems.at[1]),
        pltpu.make_async_copy(b_hbm, b_ref, sems.at[2]),
    ]
    for copy in copies:
        copy.start()
    slots = pairs_ref.shape[1]
    row = pairs_ref[0:1, :]
    place = (row - base_ref[0]) * STEPS + pairs_ref[1:2, :] - row
    live = lax.broadcasted_iota(jnp.int32, (1, slots), 1) < count_ref[0]
    place = jnp.where(live, place, -1)
    hit = lax.broadcasted_iota(jnp.int32, (slots, slots), 0) == place
    found = jnp.sum(hit.astype(jnp.float32), axis=1, keepdims=True)
    listed_ref[...] = jnp.broadcast_to(found.astype(jnp.bfloat16)[:, :, None], listed_ref.shape)
    for copy in copies:
        copy.wait()
    leaves = order_ref.shape[0]
    n = b_ref.shape[0]
    sub = lax.broadcasted_iota(jnp.int32, (W, W), 0)
    dot = functools.partial(jnp.dot, preferred_element_type=jnp.float32)
    center = jnp.broadcast_to(coords_ref[:, 0:1], (3, W))
    center_ref[...] = center
    zero = jnp.zeros((5, W), jnp.float32)
    for k in range(leaves):
        at = slice(k * W, (k + 1) * W)
        sel = (sub == order_ref[k : k + 1, :]).astype(jnp.float32).astype(jnp.bfloat16)
        parts = [dot(p, sel) for p in split3(coords_ref[:, at])]
        got = parts[0] + parts[1] + parts[2]
        here = (got - center) * (KAPPA / TAPER)
        pts_ref[k, 0:3, :] = here
        parts = [p.astype(jnp.float32) for p in split3(here)]
        stack = jnp.concatenate([z for p in parts for z in (p, zero)], axis=0)
        cols_ref[k] = jnp.transpose(stack).astype(jnp.bfloat16)
        if k < REACH:
            edge_ref[0:n, at] = b_ref[:, at]
            edge_ref[n : n + 3, at] = got
    load_values(v_ref, b_ref, leaves, 0)


def spread_rows(bc_ref, cols):
    r = lax.broadcasted_iota(jnp.int32, (24, 3 * HALF), 0)
    c = lax.broadcasted_iota(jnp.int32, (24, 3 * HALF), 1)
    sel = ((r & 7) == (c >> 7)).astype(jnp.float32).astype(jnp.bfloat16)
    bc_ref[...] = jnp.dot(cols, sel, preferred_element_type=jnp.float32)


def make_tile(t_ref, bc_ref, other, same):
    b = [
        [jnp.broadcast_to(other[c : c + 1, h * HALF : (h + 1) * HALF], (CHUNK, HALF)) for c in range(3)]
        for h in range(2)
    ]
    for k in range(W // CHUNK):
        rows = slice(k * CHUNK, (k + 1) * CHUNK)
        lower = k * CHUNK >= HALF
        for h in range(2):
            at = slice(h * HALF, (h + 1) * HALF)
            at_lo = slice(W + h * HALF, W + (h + 1) * HALF)
            if same and lower and h == 0:
                t_ref[rows, at] = jnp.zeros((CHUNK, HALF), jnp.bfloat16)
                t_ref[rows, at_lo] = jnp.zeros((CHUNK, HALF), jnp.bfloat16)
                continue
            u = None
            for c in range(3):
                d = bc_ref[rows, c * HALF : (c + 1) * HALF] - b[h][c]
                u = d * d if u is None else u + d * d
            u = jnp.minimum(u, KAPPA * KAPPA)
            q = u * jnp.minimum(lax.rsqrt(u), FLOOR_INV)
            t = KAPPA - q
            e = jnp.exp2(t)
            t = t * t
            t = t * t
            x = ((q + KAPPA / 4.0) * (q + KAPPA / DECAY)) * (t * e)
            if same and lower == bool(h):
                x = x * 0.5
            hi = (x + ROUNDER) - ROUNDER
            t_ref[rows, at] = hi.astype(jnp.bfloat16)
            t_ref[rows, at_lo] = (x - hi).astype(jnp.bfloat16)


def products(t_ref, vi, vj, listed):
    hi = t_ref[:, 0:W]
    lo = t_ref[:, W : 2 * W]
    dot = functools.partial(lax.dot_general, preferred_element_type=jnp.float32)
    nt = (((1,), (1,)), ((), ()))
    nn = (((1,), (0,)), ((), ()))
    n = vi.shape[0] // 2
    keep = jnp.concatenate([listed, listed], axis=1)
    keep = jnp.concatenate([keep, keep], axis=0)
    vi = vi * keep
    vj = vj * keep
    p = dot(vj, hi, nt)
    to_row = p[:n] + p[n:] + dot(vj[:n], lo, nt)
    p = dot(vi, hi, nn)
    to_col = p[:n] + p[n:] + dot(vi[:n], lo, nn)
    return to_row, to_col


def put_rows(out_ref, acc_ref, first, leaves, own_ref=None):
    for k in range(leaves):
        at = slice(k * W, (k + 1) * W)
        x = acc_ref[first + k] * (1.0 / PEAK)
        out_ref[:, at] = x if own_ref is None else x + NUGGET * own_ref[:, at]


def evaluate_kernel(i0, i1, leaf_dev, last, listed_ref, pts_ref, cols_ref, v_ref, center_ref, *rest):
    rest = list(rest)
    far = i1 + REACH > leaf_dev
    shift_by = 0
    edge_ref = rest.pop(0) if far else None
    own_ref = rest.pop(0) if last else None
    prev_ref = rest.pop(0) if i0 else None
    tiles_ref = rest.pop(0)
    acc_ref = rest.pop(1 if last else 0)
    rows_ref = rest.pop(0) if last or far else None
    bc_ref = rest.pop(0)
    if far:
        pts_all, v_all = rest
        n = v_ref.shape[1] // 2
        own = leaf_dev - i0
        pts_all[0:own] = pts_ref[i0:leaf_dev]
        v_all[0:own] = v_ref[i0:leaf_dev]
        for k in range(REACH):
            got = edge_ref[n : n + 3, k * W : (k + 1) * W]
            pts_all[own + k, 0:3, :] = (got - center_ref[...]) * (KAPPA / TAPER)
        load_values(v_all, edge_ref, REACH, own)
        pts_ref, v_ref = pts_all, v_all
        shift_by = i0
    if i0:
        acc_ref[...] = prev_ref[...]
    else:
        acc_ref[...] = jnp.zeros_like(acc_ref)
    tiles_ref[0] = jnp.zeros_like(tiles_ref[0])

    def finish(i, slot):
        to_row, to_col = products(
            tiles_ref.at[slot], v_ref[i - shift_by], v_ref[i + REACH - shift_by], listed_ref[i * STEPS + REACH]
        )
        acc_ref[i] += to_row
        acc_ref[i + REACH] += to_col

    def one_leaf(i, _):
        slot = (i - i0) * STEPS
        spread_rows(bc_ref, cols_ref[i])
        vi = v_ref[i - shift_by]

        def make(d):
            make_tile(tiles_ref.at[slot + (1 + d)], bc_ref, pts_ref.at[i + d - shift_by], d == 0)

        make(0)
        finish(jnp.maximum(i - 1, i0), slot)
        total = None
        for d in range(REACH):
            make(d + 1)
            to_row, to_col = products(
                tiles_ref.at[slot + (1 + d)], vi, v_ref[i + d - shift_by], listed_ref[i * STEPS + d]
            )
            total = to_row if total is None else total + to_row
            acc_ref[i + d] += to_col
        acc_ref[i] += total
        return 0

    lax.fori_loop(i0, i1, one_leaf, 0)
    finish(i1 - 1, (i1 - i0) * STEPS)
    if far:
        put_rows(rows_ref, acc_ref, leaf_dev, REACH)
    if last:
        put_rows(rows_ref, acc_ref, 0, leaf_dev, own_ref)


def apply_kernel(i0, i1, leaf_dev, last, listed_ref, tiles_ref, w_ref, *rest):
    rest = list(rest)
    far = i1 + REACH > leaf_dev
    far_ref = rest.pop(0) if far else None
    prev_ref = rest.pop(0) if i0 else None
    acc_ref = rest.pop(1 if last else 0)
    rows_ref = rest.pop(0) if last or far else None
    v_ref = rest.pop(0)
    load_values(v_ref, w_ref, leaf_dev, 0)
    if far:
        load_values(v_ref, far_ref, REACH, leaf_dev)
    if i0:
        acc_ref[...] = prev_ref[...]
    else:
        acc_ref[...] = jnp.zeros_like(acc_ref)

    def one_leaf(i, _):
        slot = (i - i0) * STEPS
        vi = v_ref[i]
        total = None
        for d in range(STEPS):
            to_row, to_col = products(
                tiles_ref.at[slot + (1 + d)], vi, v_ref[i + d], listed_ref[i * STEPS + d]
            )
            total = to_row if total is None else total + to_row
            acc_ref[i + d] += to_col
        acc_ref[i] += total
        return 0

    lax.fori_loop(i0, i1, one_leaf, 0)
    if far:
        put_rows(rows_ref, acc_ref, leaf_dev, REACH)
    if last:
        put_rows(rows_ref, acc_ref, 0, leaf_dev, w_ref)


VM = pl.BlockSpec(memory_space=pltpu.VMEM)
SM = pl.BlockSpec(memory_space=pltpu.SMEM)
ANY = pl.BlockSpec(memory_space=pl.ANY)
PARAMS = pltpu.CompilerParams(vmem_limit_bytes=8 << 20)


def prepare_call(pairs, count, base, coords, order, b):
    leaves = order.shape[0]
    n = b.shape[0]
    return pl.pallas_call(
        prepare_kernel,
        out_shape=(
            jax.ShapeDtypeStruct((pairs.shape[1], 16, HALF), jnp.bfloat16),
            jax.ShapeDtypeStruct((leaves, 8, W), jnp.float32),
            jax.ShapeDtypeStruct((leaves, W, 24), jnp.bfloat16),
            jax.ShapeDtypeStruct((leaves, 2 * n, W), jnp.bfloat16),
            jax.ShapeDtypeStruct((3, W), jnp.float32),
            jax.ShapeDtypeStruct((n + 3, REACH * W), jnp.float32),
        ),
        in_specs=[VM, SM, SM, ANY, ANY, ANY],
        out_specs=(VM,) * 6,
        scratch_shapes=[
            pltpu.VMEM(coords.shape, jnp.float32),
            pltpu.VMEM(order.shape, jnp.int32),
            pltpu.VMEM(b.shape, jnp.float32),
            pltpu.SemaphoreType.DMA((3,)),
        ],
        compiler_params=PARAMS,
        name="prepare",
    )(pairs, count, base, coords, order, b)


def shapes_out(leaf_dev, n, far, last):
    acc = (leaf_dev + REACH, n, W)
    rows = (n, (leaf_dev if last else REACH) * W)
    f32 = jnp.float32
    if last:
        return [jax.ShapeDtypeStruct(rows, f32)], [pltpu.VMEM(acc, f32)]
    return [jax.ShapeDtypeStruct(acc, f32)] + ([jax.ShapeDtypeStruct(rows, f32)] if far else []), []


def evaluate_call(i0, i1, leaf_dev, n, prepared, far, own, prev):
    tiles = (i1 - i0) * STEPS
    last = own is not None
    ops = [*prepared, *far, *([own] if last else []), *([] if prev is None else [prev])]
    outs, held_acc = shapes_out(leaf_dev, n, bool(far), last)
    scratch = [*held_acc, pltpu.VMEM((W, 3 * HALF), jnp.float32)]
    if far:
        held = leaf_dev - i0 + REACH
        scratch += [pltpu.VMEM((held, 8, W), jnp.float32), pltpu.VMEM((held, 2 * n, W), jnp.bfloat16)]
    outs = [jax.ShapeDtypeStruct((tiles + 1, W, 2 * W), jnp.bfloat16), *outs]
    return pl.pallas_call(
        functools.partial(evaluate_kernel, i0, i1, leaf_dev, last),
        out_shape=outs,
        in_specs=[VM] * len(ops),
        out_specs=[VM] * len(outs),
        scratch_shapes=scratch,
        compiler_params=PARAMS,
        cost_estimate=pl.CostEstimate(flops=tiles << 28, transcendentals=tiles << 17, bytes_accessed=tiles << 18),
        name=f"evaluate_{i0}",
    )(*ops)


def apply_call(i0, i1, leaf_dev, n, listed, tiles, own, far, last, prev):
    ops = [listed, tiles, own, *far, *([] if prev is None else [prev])]
    outs, held_acc = shapes_out(leaf_dev, n, bool(far), last)
    return pl.pallas_call(
        functools.partial(apply_kernel, i0, i1, leaf_dev, last),
        out_shape=outs,
        in_specs=[VM] * len(ops),
        out_specs=[VM] * len(outs),
        scratch_shapes=[*held_acc, pltpu.VMEM((leaf_dev + REACH, 2 * n, W), jnp.bfloat16)],
        compiler_params=PARAMS,
        cost_estimate=pl.CostEstimate(flops=tiles.shape[0] << 27, transcendentals=0, bytes_accessed=tiles.size * 2),
        name=f"apply_{i0}",
    )(*ops)


def shift(value, by):
    length = lax.axis_size("leaf")
    return lax.ppermute(value, "leaf", [(i, i + by) for i in range(length) if 0 <= i + by < length])


def sum_over_leaf(value):
    length = lax.axis_size("leaf")
    value = value + lax.ppermute(value, "leaf", [(i, i ^ 1) for i in range(length)])
    copies = jnp.broadcast_to(value, (length // 2, *value.shape))
    groups = [[i for i in range(length) if i % 2 == c] for c in range(2)]
    got = lax.all_to_all(
        copies, "leaf", split_axis=0, concat_axis=0, tiled=True, axis_index_groups=groups
    )
    return jnp.sum(got, axis=0)


def body(coords, site_order, leaf_pairs, pair_count, probes):
    leaf_dev, width = site_order.shape
    n = probes.shape[0]
    edge = REACH * width
    base = (lax.axis_index("leaf") * leaf_dev).astype(jnp.int32).reshape(1)
    *prepared, packed = prepare_call(leaf_pairs, pair_count, base, coords, site_order, probes)
    far = shift(packed, -1)
    cut0, cut1 = leaf_dev - REACH - 5, leaf_dev - REACH
    evaluate = functools.partial(evaluate_call, leaf_dev=leaf_dev, n=n, prepared=prepared)
    tiles0, acc = evaluate(0, cut0, far=(), own=None, prev=None)
    tiles1, acc, send = evaluate(cut1, leaf_dev, far=(far,), own=None, prev=acc)
    back = shift(send, 1)
    tiles2, image = evaluate(cut0, cut1, far=(), own=probes, prev=acc)
    image = jnp.concatenate([image[:, :edge] + back, image[:, edge:]], axis=1)

    image_far = shift(image[:, :edge], -1)
    apply = functools.partial(apply_call, leaf_dev=leaf_dev, n=n, listed=prepared[0], own=image)
    (acc,) = apply(0, cut0, tiles=tiles0, far=(), last=False, prev=None)
    acc, send = apply(cut1, leaf_dev, tiles=tiles1, far=(image_far,), last=False, prev=acc)
    back = shift(send, 1)
    (image2,) = apply(cut0, cut1, tiles=tiles2, far=(), last=True, prev=acc)
    image2 = jnp.concatenate([image2[:, :edge] + back, image2[:, edge:]], axis=1)
    sums = jnp.stack(
        [
            jnp.sum(probes * probes, axis=1),
            jnp.sum(probes * image, axis=1),
            jnp.sum(image * image, axis=1),
            jnp.sum(image * image2, axis=1),
        ]
    )
    rr, bw, ww, wz = sum_over_leaf(sums)
    alpha = rr / bw
    rr1 = rr - 2.0 * alpha * bw + alpha * alpha * ww
    beta = rr1 / rr
    g = 1.0 + beta
    curve = g * g * bw - 2.0 * g * alpha * ww + alpha * alpha * wz
    alpha1 = rr1 / curve
    c = lambda x: x[:, None]
    direction1 = c(g) * probes - c(alpha) * image
    image1 = c(g) * image - c(alpha) * image2
    solution = c(alpha) * probes + c(alpha1) * direction1
    residual = probes - c(alpha) * image - c(alpha1) * image1
    return solution, residual


def solution(mesh):
    in_specs = (P(None, "leaf"), P("leaf", None), P(None, "leaf"), P("leaf"), P("probe", "leaf"))
    out_specs = (P("probe", "leaf"), P("probe", "leaf"))
    return jax.shard_map(body, mesh=mesh, in_specs=in_specs, out_specs=out_specs, check_vma=False)
```

```python
import functools
import math

import jax
import jax.numpy as jnp
from jax import lax
from jax.experimental import pallas as pl
from jax.experimental.pallas import tpu as pltpu
from jax.sharding import PartitionSpec as P

REACH = 5
STEPS = REACH + 1
UNIT = 0.025
LENGTH = 0.12
NUGGET = 0.5
W = 256
TAPER = REACH * UNIT
DECAY = math.sqrt(3.0) * TAPER / LENGTH
LOG2E = math.log2(math.e)
CHUNK = 16
HALF = W // 2
FLOOR_INV = 1e18
KAPPA = DECAY * LOG2E
PEAK = KAPPA**6 / (4.0 * DECAY) * 2.0**KAPPA
SCALE = KAPPA / TAPER
COMPACT = 20.0 * KAPPA * KAPPA
RANGE = 1e15
TINY = 1e-12
GROUPS = 6
ROUNDER = 1.5 * 2.0 ** (23 + math.ceil(math.log2(PEAK)) - 8)


def split2(x):
    hi = x.astype(jnp.bfloat16)
    lo = (x - hi.astype(jnp.float32)).astype(jnp.bfloat16)
    return hi, lo


def split3(x):
    hi = x.astype(jnp.bfloat16)
    rest = x - hi.astype(jnp.float32)
    mid = rest.astype(jnp.bfloat16)
    lo = (rest - mid.astype(jnp.float32)).astype(jnp.bfloat16)
    return hi, mid, lo


def load_values(v_ref, src_ref, leaves, first):
    n = v_ref.shape[1] // 2
    for k in range(leaves):
        hi, lo = split2(src_ref[0:n, k * W : (k + 1) * W])
        v_ref[first + k] = jnp.concatenate([hi, lo], axis=0)


def split_rows(point, center, top, weight):
    x = (point - center) * SCALE
    sq = x * x
    sq = sq[0:1] + sq[1:2] + sq[2:3]
    row = lax.broadcasted_iota(jnp.int32, x.shape, 0)
    x = jnp.where(top, x * weight, jnp.where(row == 3, sq, 0.0))
    hi = x.astype(jnp.bfloat16).astype(jnp.float32)
    rest = x - hi
    mid = rest.astype(jnp.bfloat16).astype(jnp.float32)
    return hi, mid, rest - mid


def prepare_kernel(
    pairs_ref, count_ref, base_ref, coords_hbm, order_hbm, b_hbm,
    listed_ref, pts_ref, cols_ref, v_ref, center_ref, wide_ref, edge_ref, coords_ref, order_ref, b_ref, sems,
):
    copies = [
        pltpu.make_async_copy(coords_hbm, coords_ref, sems.at[0]),
        pltpu.make_async_copy(order_hbm, order_ref, sems.at[1]),
        pltpu.make_async_copy(b_hbm, b_ref, sems.at[2]),
    ]
    for copy in copies:
        copy.start()
    slots = pairs_ref.shape[1]
    row = pairs_ref[0:1, :]
    place = (row - base_ref[0]) * STEPS + pairs_ref[1:2, :] - row
    live = lax.broadcasted_iota(jnp.int32, (1, slots), 1) < count_ref[0]
    place = jnp.where(live, place, -1)
    hit = lax.broadcasted_iota(jnp.int32, (slots, slots), 0) == place
    found = jnp.sum(hit.astype(jnp.float32), axis=1, keepdims=True)
    listed_ref[...] = jnp.broadcast_to(found.astype(jnp.bfloat16)[:, :, None], listed_ref.shape)
    for copy in copies:
        copy.wait()
    leaves = order_ref.shape[0]
    n = b_ref.shape[0]
    sub = lax.broadcasted_iota(jnp.int32, (W, W), 0)
    dot = functools.partial(jnp.dot, preferred_element_type=jnp.float32)
    top = lax.broadcasted_iota(jnp.int32, (8, W), 0) < 3
    pad = jnp.zeros((5, W), jnp.float32)
    wide = jnp.zeros((8, W), jnp.float32)
    for k in range(leaves):
        at = slice(k * W, (k + 1) * W)
        sel = (sub == order_ref[k : k + 1, :]).astype(jnp.float32).astype(jnp.bfloat16)
        parts = [dot(p, sel) for p in split3(coords_ref[:, at])]
        got = parts[0] + parts[1] + parts[2]
        point = jnp.concatenate([got, pad], axis=0)
        center = jnp.broadcast_to(jnp.sum(point, axis=1, keepdims=True) * (1.0 / W), (8, W))
        pts_ref[k] = point
        center_ref[k] = center
        hi, mid, lo = split_rows(point, center, top, 1.0)
        square = jnp.where(top, 0.0, hi + mid + lo)
        first = center if k == 0 else first
        far_off = jnp.abs(point - first) * (SCALE * COMPACT / RANGE)
        wide = jnp.maximum(wide, jnp.maximum(square, far_off))
        one = jnp.where(lax.broadcasted_iota(jnp.int32, (8, W), 0) == 3, 1.0, 0.0)
        stack = [hi, jnp.where(top, hi, mid), jnp.where(top, hi, lo)]
        stack += [jnp.where(top, mid, one), jnp.where(top, mid, one), jnp.where(top, lo, one)]
        cols_ref[k] = jnp.transpose(jnp.concatenate(stack, axis=0)).astype(jnp.bfloat16)
        if k < REACH:
            edge_ref[0:n, at] = b_ref[:, at]
            edge_ref[n : n + 3, at] = got
    wide_ref[...] = wide
    load_values(v_ref, b_ref, leaves, 0)


def spread_rows(bc_ref, points):
    cols = jnp.transpose(points)
    for c in range(3):
        bc_ref[:, c * HALF : (c + 1) * HALF] = jnp.broadcast_to(cols[:, c : c + 1], (W, HALF))


def far_squares(bc_ref, other):
    def block(rows, h):
        u = None
        for c in range(3):
            b = jnp.broadcast_to(other[c : c + 1, h * HALF : (h + 1) * HALF], (CHUNK, HALF))
            d = bc_ref[rows, c * HALF : (c + 1) * HALF] - b
            u = d * d if u is None else u + d * d
        return u * (SCALE * SCALE)

    return block


def near_squares(cols, other, center):
    top = lax.broadcasted_iota(jnp.int32, (8, W), 0) < 3
    one = jnp.where(lax.broadcasted_iota(jnp.int32, (8, W), 0) == 3, 1.0, 0.0)
    hi, mid, lo = split_rows(other, center, top, -2.0)
    stack = [jnp.where(top, hi, one), jnp.where(top, mid, one), jnp.where(top, lo, one)]
    stack += [hi, mid, jnp.where(top, hi, lo)]
    rows = jnp.concatenate(stack, axis=0).astype(jnp.bfloat16)
    all_u = jnp.dot(cols, rows, preferred_element_type=jnp.float32)
    return lambda rows, h: all_u[rows, h * HALF : (h + 1) * HALF]


def make_tile(t_ref, block, same):
    for k in range(W // CHUNK):
        rows = slice(k * CHUNK, (k + 1) * CHUNK)
        lower = k * CHUNK >= HALF
        for h in range(2):
            if same and lower and h == 0:
                t_ref[0, rows, :] = jnp.zeros((CHUNK, HALF), jnp.bfloat16)
                t_ref[2, rows, :] = jnp.zeros((CHUNK, HALF), jnp.bfloat16)
                continue
            u = jnp.minimum(jnp.maximum(block(rows, h), TINY), KAPPA * KAPPA)
            q = u * lax.rsqrt(u)
            t = KAPPA - q
            e = jnp.exp2(t)
            t = t * t
            t = t * t
            x = ((q + KAPPA / 4.0) * (q + KAPPA / DECAY)) * (t * e)
            if same and lower == bool(h):
                x = x * 0.5
            hi = (x + ROUNDER) - ROUNDER
            t_ref[h, rows, :] = hi.astype(jnp.bfloat16)
            t_ref[2 + h, rows, :] = (x - hi).astype(jnp.bfloat16)


def products(t_ref, vi, vj, listed):
    hi = jnp.concatenate([t_ref[0], t_ref[1]], axis=1)
    lo = jnp.concatenate([t_ref[2], t_ref[3]], axis=1)
    dot = functools.partial(lax.dot_general, preferred_element_type=jnp.float32)
    nt = (((1,), (1,)), ((), ()))
    nn = (((1,), (0,)), ((), ()))
    n = vi.shape[0] // 2
    keep = jnp.concatenate([listed, listed], axis=1)
    keep = jnp.concatenate([keep, keep], axis=0)
    vi = vi * keep
    vj = vj * keep
    p = dot(vj, hi, nt)
    to_row = p[:n] + p[n:] + dot(vj[:n], lo, nt)
    p = dot(vi, hi, nn)
    to_col = p[:n] + p[n:] + dot(vi[:n], lo, nn)
    return to_row, to_col


def put_rows(out_ref, acc_ref, first, leaves, own_ref=None):
    for k in range(leaves):
        at = slice(k * W, (k + 1) * W)
        x = acc_ref[first + k] * (1.0 / PEAK)
        out_ref[:, at] = x if own_ref is None else x + NUGGET * own_ref[:, at]


def evaluate_kernel(i0, i1, leaf_dev, last, listed_ref, pts_ref, cols_ref, v_ref, center_ref, wide_ref, *rest):
    rest = list(rest)
    far = i1 + REACH > leaf_dev
    shift_by = 0
    edge_ref = rest.pop(0) if far else None
    own_ref = rest.pop(0) if last else None
    prev_ref = rest.pop(0) if i0 else None
    tiles_ref = rest.pop(0)
    acc_ref = rest.pop(1 if last else 0)
    rows_ref = rest.pop(0) if last or far else None
    bc_ref = rest.pop(0)
    compact = jnp.max(wide_ref[...]) <= COMPACT
    if far:
        pts_all, v_all = rest
        n = v_ref.shape[1] // 2
        own = leaf_dev - i0
        pts_all[0:own] = pts_ref[i0:leaf_dev]
        v_all[0:own] = v_ref[i0:leaf_dev]
        first = center_ref[leaf_dev - 1, 0:3, :]
        pts_all[own:] = jnp.zeros_like(pts_all[own:])
        for k in range(REACH):
            got = edge_ref[n : n + 3, k * W : (k + 1) * W]
            pts_all[own + k, 0:3, :] = got
            far_off = jnp.abs(got - first) * (SCALE * COMPACT / RANGE)
            wide = far_off if k == 0 else jnp.maximum(wide, far_off)
        load_values(v_all, edge_ref, REACH, own)
        compact = compact & (jnp.max(wide) <= COMPACT)
        pts_ref, v_ref = pts_all, v_all
        shift_by = i0
    if i0:
        acc_ref[...] = prev_ref[...]
    else:
        acc_ref[...] = jnp.zeros_like(acc_ref)
    tiles_ref[0] = jnp.zeros_like(tiles_ref[0])

    def finish(i, slot):
        to_row, to_col = products(
            tiles_ref.at[slot], v_ref[i - shift_by], v_ref[i + REACH - shift_by], listed_ref[i * STEPS + REACH]
        )
        acc_ref[i] += to_row
        acc_ref[i + REACH] += to_col

    def near_leaf(i, _):
        slot = (i - i0) * STEPS
        cols = cols_ref[i]
        center = center_ref[i]
        vi = v_ref[i - shift_by]

        def make(d):
            block = near_squares(cols, pts_ref[i + d - shift_by], center)
            make_tile(tiles_ref.at[slot + (1 + d)], block, d == 0)

        make(0)
        finish(jnp.maximum(i - 1, i0), slot)
        total = None
        for d in range(REACH):
            make(d + 1)
            to_row, to_col = products(
                tiles_ref.at[slot + (1 + d)], vi, v_ref[i + d - shift_by], listed_ref[i * STEPS + d]
            )
            total = to_row if total is None else total + to_row
            acc_ref[i + d] += to_col
        acc_ref[i] += total
        return 0

    def far_leaf(i, _):
        slot = (i - i0) * STEPS
        spread_rows(bc_ref, pts_ref[i - shift_by])

        def step(d, _):
            t_ref = tiles_ref.at[slot + (1 + d)]
            block = far_squares(bc_ref, pts_ref.at[i + d - shift_by])
            lax.cond(d == 0, lambda: make_tile(t_ref, block, True), lambda: make_tile(t_ref, block, False))

            @pl.when(d < REACH)
            def _():
                to_row, to_col = products(
                    t_ref, v_ref[i - shift_by], v_ref[i + d - shift_by], listed_ref[i * STEPS + d]
                )
                acc_ref[i] += to_row
                acc_ref[i + d] += to_col

            return 0

        @pl.when(i > i0)
        def _():
            finish(i - 1, slot)

        return lax.fori_loop(0, STEPS, step, 0)

    @pl.when(compact)
    def _():
        lax.fori_loop(i0, i1, near_leaf, 0)

    @pl.when(jnp.logical_not(compact))
    def _():
        lax.fori_loop(i0, i1, far_leaf, 0)

    finish(i1 - 1, (i1 - i0) * STEPS)
    if far:
        put_rows(rows_ref, acc_ref, leaf_dev, REACH)
    if last:
        put_rows(rows_ref, acc_ref, 0, leaf_dev, own_ref)


def apply_kernel(i0, i1, leaf_dev, last, listed_ref, tiles_ref, w_ref, *rest):
    rest = list(rest)
    far = i1 + REACH > leaf_dev
    far_ref = rest.pop(0) if far else None
    prev_ref = rest.pop(0) if i0 else None
    acc_ref = rest.pop(1 if last else 0)
    rows_ref = rest.pop(0) if last or far else None
    v_ref = rest.pop(0)
    load_values(v_ref, w_ref, leaf_dev, 0)
    if far:
        load_values(v_ref, far_ref, REACH, leaf_dev)
    if i0:
        acc_ref[...] = prev_ref[...]
    else:
        acc_ref[...] = jnp.zeros_like(acc_ref)

    def one_leaf(i, _):
        slot = (i - i0) * STEPS
        vi = v_ref[i]
        total = None
        for d in range(STEPS):
            to_row, to_col = products(
                tiles_ref.at[slot + (1 + d)], vi, v_ref[i + d], listed_ref[i * STEPS + d]
            )
            total = to_row if total is None else total + to_row
            acc_ref[i + d] += to_col
        acc_ref[i] += total
        return 0

    lax.fori_loop(i0, i1, one_leaf, 0)
    if far:
        put_rows(rows_ref, acc_ref, leaf_dev, REACH)
    if last:
        put_rows(rows_ref, acc_ref, 0, leaf_dev, w_ref)


VM = pl.BlockSpec(memory_space=pltpu.VMEM)
SM = pl.BlockSpec(memory_space=pltpu.SMEM)
ANY = pl.BlockSpec(memory_space=pl.ANY)
PARAMS = pltpu.CompilerParams(vmem_limit_bytes=8 << 20)


def prepare_call(pairs, count, base, coords, order, b):
    leaves = order.shape[0]
    n = b.shape[0]
    return pl.pallas_call(
        prepare_kernel,
        out_shape=(
            jax.ShapeDtypeStruct((pairs.shape[1], 16, HALF), jnp.bfloat16),
            jax.ShapeDtypeStruct((leaves, 8, W), jnp.float32),
            jax.ShapeDtypeStruct((leaves, W, 8 * GROUPS), jnp.bfloat16),
            jax.ShapeDtypeStruct((leaves, 2 * n, W), jnp.bfloat16),
            jax.ShapeDtypeStruct((leaves, 8, W), jnp.float32),
            jax.ShapeDtypeStruct((8, W), jnp.float32),
            jax.ShapeDtypeStruct((n + 3, REACH * W), jnp.float32),
        ),
        in_specs=[VM, SM, SM, ANY, ANY, ANY],
        out_specs=(VM,) * 7,
        scratch_shapes=[
            pltpu.VMEM(coords.shape, jnp.float32),
            pltpu.VMEM(order.shape, jnp.int32),
            pltpu.VMEM(b.shape, jnp.float32),
            pltpu.SemaphoreType.DMA((3,)),
        ],
        compiler_params=PARAMS,
        name="prepare",
    )(pairs, count, base, coords, order, b)


def shapes_out(leaf_dev, n, far, last):
    acc = (leaf_dev + REACH, n, W)
    rows = (n, (leaf_dev if last else REACH) * W)
    f32 = jnp.float32
    if last:
        return [jax.ShapeDtypeStruct(rows, f32)], [pltpu.VMEM(acc, f32)]
    return [jax.ShapeDtypeStruct(acc, f32)] + ([jax.ShapeDtypeStruct(rows, f32)] if far else []), []


def evaluate_call(i0, i1, leaf_dev, n, prepared, far, own, prev):
    tiles = (i1 - i0) * STEPS
    last = own is not None
    ops = [*prepared, *far, *([own] if last else []), *([] if prev is None else [prev])]
    outs, held_acc = shapes_out(leaf_dev, n, bool(far), last)
    scratch = [*held_acc, pltpu.VMEM((W, 3 * HALF), jnp.float32)]
    if far:
        held = leaf_dev - i0 + REACH
        scratch += [pltpu.VMEM((held, 8, W), jnp.float32), pltpu.VMEM((held, 2 * n, W), jnp.bfloat16)]
    outs = [jax.ShapeDtypeStruct((tiles + 1, 4, W, HALF), jnp.bfloat16), *outs]
    return pl.pallas_call(
        functools.partial(evaluate_kernel, i0, i1, leaf_dev, last),
        out_shape=outs,
        in_specs=[VM] * len(ops),
        out_specs=[VM] * len(outs),
        scratch_shapes=scratch,
        compiler_params=PARAMS,
        cost_estimate=pl.CostEstimate(flops=tiles << 28, transcendentals=tiles << 17, bytes_accessed=tiles << 18),
        name=f"evaluate_{i0}",
    )(*ops)


def apply_call(i0, i1, leaf_dev, n, listed, tiles, own, far, last, prev):
    ops = [listed, tiles, own, *far, *([] if prev is None else [prev])]
    outs, held_acc = shapes_out(leaf_dev, n, bool(far), last)
    return pl.pallas_call(
        functools.partial(apply_kernel, i0, i1, leaf_dev, last),
        out_shape=outs,
        in_specs=[VM] * len(ops),
        out_specs=[VM] * len(outs),
        scratch_shapes=[*held_acc, pltpu.VMEM((leaf_dev + REACH, 2 * n, W), jnp.bfloat16)],
        compiler_params=PARAMS,
        cost_estimate=pl.CostEstimate(flops=tiles.shape[0] << 27, transcendentals=0, bytes_accessed=tiles.size * 2),
        name=f"apply_{i0}",
    )(*ops)


def shift(value, by):
    length = lax.axis_size("leaf")
    return lax.ppermute(value, "leaf", [(i, i + by) for i in range(length) if 0 <= i + by < length])


def sum_over_leaf(value):
    length = lax.axis_size("leaf")
    value = value + lax.ppermute(value, "leaf", [(i, i ^ 1) for i in range(length)])
    copies = jnp.broadcast_to(value, (length // 2, *value.shape))
    groups = [[i for i in range(length) if i % 2 == c] for c in range(2)]
    got = lax.all_to_all(
        copies, "leaf", split_axis=0, concat_axis=0, tiled=True, axis_index_groups=groups
    )
    return jnp.sum(got, axis=0)


def body(coords, site_order, leaf_pairs, pair_count, probes):
    leaf_dev, width = site_order.shape
    n = probes.shape[0]
    edge = REACH * width
    base = (lax.axis_index("leaf") * leaf_dev).astype(jnp.int32).reshape(1)
    *prepared, packed = prepare_call(leaf_pairs, pair_count, base, coords, site_order, probes)
    far = shift(packed, -1)
    cut0, cut1 = leaf_dev - REACH - 5, leaf_dev - REACH
    evaluate = functools.partial(evaluate_call, leaf_dev=leaf_dev, n=n, prepared=prepared)
    tiles0, acc = evaluate(0, cut0, far=(), own=None, prev=None)
    tiles1, acc, send = evaluate(cut1, leaf_dev, far=(far,), own=None, prev=acc)
    back = shift(send, 1)
    tiles2, image = evaluate(cut0, cut1, far=(), own=probes, prev=acc)
    image = jnp.concatenate([image[:, :edge] + back, image[:, edge:]], axis=1)

    image_far = shift(image[:, :edge], -1)
    apply = functools.partial(apply_call, leaf_dev=leaf_dev, n=n, listed=prepared[0], own=image)
    (acc,) = apply(0, cut0, tiles=tiles0, far=(), last=False, prev=None)
    acc, send = apply(cut1, leaf_dev, tiles=tiles1, far=(image_far,), last=False, prev=acc)
    back = shift(send, 1)
    (image2,) = apply(cut0, cut1, tiles=tiles2, far=(), last=True, prev=acc)
    image2 = jnp.concatenate([image2[:, :edge] + back, image2[:, edge:]], axis=1)
    sums = jnp.stack(
        [
            jnp.sum(probes * probes, axis=1),
            jnp.sum(probes * image, axis=1),
            jnp.sum(image * image, axis=1),
            jnp.sum(image * image2, axis=1),
        ]
    )
    rr, bw, ww, wz = sum_over_leaf(sums)
    alpha = rr / bw
    rr1 = rr - 2.0 * alpha * bw + alpha * alpha * ww
    beta = rr1 / rr
    g = 1.0 + beta
    curve = g * g * bw - 2.0 * g * alpha * ww + alpha * alpha * wz
    alpha1 = rr1 / curve
    c = lambda x: x[:, None]
    direction1 = c(g) * probes - c(alpha) * image
    image1 = c(g) * image - c(alpha) * image2
    solution = c(alpha) * probes + c(alpha1) * direction1
    residual = probes - c(alpha) * image - c(alpha1) * image1
    return solution, residual


def solution(mesh):
    in_specs = (P(None, "leaf"), P("leaf", None), P(None, "leaf"), P("leaf"), P("probe", "leaf"))
    out_specs = (P("probe", "leaf"), P("probe", "leaf"))
    return jax.shard_map(body, mesh=mesh, in_specs=in_specs, out_specs=out_specs, check_vma=False)
```

```python
import functools
import math

import jax
import jax.numpy as jnp
from jax import lax
from jax.experimental import pallas as pl
from jax.experimental.pallas import tpu as pltpu
from jax.sharding import PartitionSpec as P

REACH = 5
STEPS = REACH + 1
UNIT = 0.025
LENGTH = 0.12
NUGGET = 0.5
W = 256
TAPER = REACH * UNIT
DECAY = math.sqrt(3.0) * TAPER / LENGTH
LOG2E = math.log2(math.e)
CHUNK = 16
HALF = W // 2
FLOOR_INV = 1e18
KAPPA = DECAY * LOG2E
PEAK = KAPPA**6 / (4.0 * DECAY) * 2.0**KAPPA
SCALE = KAPPA / TAPER
COMPACT = 20.0 * KAPPA * KAPPA
RANGE = 1e15
TINY = 1e-12
GROUPS = 6
ROUNDER = 1.5 * 2.0 ** (23 + math.ceil(math.log2(PEAK)) - 8)


def split2(x):
    hi = x.astype(jnp.bfloat16)
    lo = (x - hi.astype(jnp.float32)).astype(jnp.bfloat16)
    return hi, lo


def split3(x):
    hi = x.astype(jnp.bfloat16)
    rest = x - hi.astype(jnp.float32)
    mid = rest.astype(jnp.bfloat16)
    lo = (rest - mid.astype(jnp.float32)).astype(jnp.bfloat16)
    return hi, mid, lo


def load_values(v_ref, src_ref, leaves, first):
    n = v_ref.shape[1] // 2
    for k in range(leaves):
        hi, lo = split2(src_ref[0:n, k * W : (k + 1) * W])
        v_ref[first + k] = jnp.concatenate([hi, lo], axis=0)


def split_rows(point, center, top, weight):
    x = (point - center) * SCALE
    sq = x * x
    sq = sq[0:1] + sq[1:2] + sq[2:3]
    row = lax.broadcasted_iota(jnp.int32, x.shape, 0)
    x = jnp.where(top, x * weight, jnp.where(row == 3, sq, 0.0))
    hi = x.astype(jnp.bfloat16).astype(jnp.float32)
    rest = x - hi
    mid = rest.astype(jnp.bfloat16).astype(jnp.float32)
    return hi, mid, rest - mid


def prepare_kernel(
    count_ref, base_ref, pairs_hbm, coords_hbm, order_hbm, b_hbm,
    listed_ref, pts_ref, cols_ref, v_ref, center_ref, wide_ref, edge_ref,
    pairs_ref, coords_ref, order_ref, b_ref, sems,
):
    copies = [
        pltpu.make_async_copy(pairs_hbm, pairs_ref, sems.at[0]),
        pltpu.make_async_copy(coords_hbm, coords_ref, sems.at[1]),
        pltpu.make_async_copy(order_hbm, order_ref, sems.at[2]),
        pltpu.make_async_copy(b_hbm, b_ref, sems.at[3]),
    ]
    for copy in copies:
        copy.start()
    copies[0].wait()
    slots = pairs_ref.shape[1]
    row = pairs_ref[0:1, :]
    place = (row - base_ref[0]) * STEPS + pairs_ref[1:2, :] - row
    live = lax.broadcasted_iota(jnp.int32, (1, slots), 1) < count_ref[0]
    place = jnp.where(live, place, -1)
    hit = lax.broadcasted_iota(jnp.int32, (slots, slots), 0) == place
    found = jnp.sum(hit.astype(jnp.float32), axis=1, keepdims=True)
    listed_ref[...] = jnp.broadcast_to(found.astype(jnp.bfloat16)[:, :, None], listed_ref.shape)
    for copy in copies[1:]:
        copy.wait()
    leaves = order_ref.shape[0]
    n = b_ref.shape[0]
    sub = lax.broadcasted_iota(jnp.int32, (W, W), 0)
    dot = functools.partial(jnp.dot, preferred_element_type=jnp.float32)
    top = lax.broadcasted_iota(jnp.int32, (8, W), 0) < 3
    pad = jnp.zeros((5, W), jnp.float32)
    wide = jnp.zeros((8, W), jnp.float32)
    for k in range(leaves):
        at = slice(k * W, (k + 1) * W)
        sel = (sub == order_ref[k : k + 1, :]).astype(jnp.float32).astype(jnp.bfloat16)
        parts = [dot(p, sel) for p in split3(coords_ref[:, at])]
        got = parts[0] + parts[1] + parts[2]
        point = jnp.concatenate([got, pad], axis=0)
        center = jnp.broadcast_to(jnp.sum(point, axis=1, keepdims=True) * (1.0 / W), (8, W))
        pts_ref[k] = point
        center_ref[k] = center
        hi, mid, lo = split_rows(point, center, top, 1.0)
        square = jnp.where(top, 0.0, hi + mid + lo)
        first = center if k == 0 else first
        far_off = jnp.abs(point - first) * (SCALE * COMPACT / RANGE)
        wide = jnp.maximum(wide, jnp.maximum(square, far_off))
        one = jnp.where(lax.broadcasted_iota(jnp.int32, (8, W), 0) == 3, 1.0, 0.0)
        stack = [hi, jnp.where(top, hi, mid), jnp.where(top, hi, lo)]
        stack += [jnp.where(top, mid, one), jnp.where(top, mid, one), jnp.where(top, lo, one)]
        cols_ref[k] = jnp.transpose(jnp.concatenate(stack, axis=0)).astype(jnp.bfloat16)
        if k < REACH:
            edge_ref[0:n, at] = b_ref[:, at]
            edge_ref[n : n + 3, at] = got
    wide_ref[...] = wide
    load_values(v_ref, b_ref, leaves, 0)


def spread_rows(bc_ref, points):
    cols = jnp.transpose(points)
    for c in range(3):
        bc_ref[:, c * HALF : (c + 1) * HALF] = jnp.broadcast_to(cols[:, c : c + 1], (W, HALF))


def far_squares(bc_ref, other):
    def block(rows, h):
        u = None
        for c in range(3):
            b = jnp.broadcast_to(other[c : c + 1, h * HALF : (h + 1) * HALF], (CHUNK, HALF))
            d = bc_ref[rows, c * HALF : (c + 1) * HALF] - b
            u = d * d if u is None else u + d * d
        return u * (SCALE * SCALE)

    return block


def near_squares(cols, other, center):
    top = lax.broadcasted_iota(jnp.int32, (8, W), 0) < 3
    one = jnp.where(lax.broadcasted_iota(jnp.int32, (8, W), 0) == 3, 1.0, 0.0)
    hi, mid, lo = split_rows(other, center, top, -2.0)
    stack = [jnp.where(top, hi, one), jnp.where(top, mid, one), jnp.where(top, lo, one)]
    stack += [hi, mid, jnp.where(top, hi, lo)]
    rows = jnp.concatenate(stack, axis=0).astype(jnp.bfloat16)
    all_u = jnp.dot(cols, rows, preferred_element_type=jnp.float32)
    return lambda rows, h: all_u[rows, h * HALF : (h + 1) * HALF]


def make_tile(t_ref, block, same):
    for k in range(W // CHUNK):
        rows = slice(k * CHUNK, (k + 1) * CHUNK)
        lower = k * CHUNK >= HALF
        for h in range(2):
            if same and lower and h == 0:
                t_ref[0, rows, :] = jnp.zeros((CHUNK, HALF), jnp.bfloat16)
                t_ref[2, rows, :] = jnp.zeros((CHUNK, HALF), jnp.bfloat16)
                continue
            u = jnp.minimum(jnp.maximum(block(rows, h), TINY), KAPPA * KAPPA)
            q = u * lax.rsqrt(u)
            t = KAPPA - q
            e = jnp.exp2(t)
            t = t * t
            t = t * t
            x = ((q + KAPPA / 4.0) * (q + KAPPA / DECAY)) * (t * e)
            if same and lower == bool(h):
                x = x * 0.5
            hi = (x + ROUNDER) - ROUNDER
            t_ref[h, rows, :] = hi.astype(jnp.bfloat16)
            t_ref[2 + h, rows, :] = (x - hi).astype(jnp.bfloat16)


def products(t_ref, vi, vj, listed):
    hi = jnp.concatenate([t_ref[0], t_ref[1]], axis=1)
    lo = jnp.concatenate([t_ref[2], t_ref[3]], axis=1)
    dot = functools.partial(lax.dot_general, preferred_element_type=jnp.float32)
    nt = (((1,), (1,)), ((), ()))
    nn = (((1,), (0,)), ((), ()))
    n = vi.shape[0] // 2
    keep = jnp.concatenate([listed, listed], axis=1)
    keep = jnp.concatenate([keep, keep], axis=0)
    vi = vi * keep
    vj = vj * keep
    p = dot(vj, hi, nt)
    to_row = p[:n] + p[n:] + dot(vj[:n], lo, nt)
    p = dot(vi, hi, nn)
    to_col = p[:n] + p[n:] + dot(vi[:n], lo, nn)
    return to_row, to_col


def put_rows(out_ref, acc_ref, first, leaves, own_ref=None):
    for k in range(leaves):
        at = slice(k * W, (k + 1) * W)
        x = acc_ref[first + k] * (1.0 / PEAK)
        out_ref[:, at] = x if own_ref is None else x + NUGGET * own_ref[:, at]


def evaluate_kernel(i0, i1, leaf_dev, last, listed_ref, pts_ref, cols_ref, v_ref, center_ref, wide_ref, *rest):
    rest = list(rest)
    far = i1 + REACH > leaf_dev
    shift_by = 0
    edge_ref = rest.pop(0) if far else None
    own_ref = rest.pop(0) if last else None
    prev_ref = rest.pop(0) if i0 else None
    tiles_ref = rest.pop(0)
    acc_ref = rest.pop(1 if last else 0)
    rows_ref = rest.pop(0) if last or far else None
    bc_ref = rest.pop(0)
    compact = jnp.max(wide_ref[...]) <= COMPACT
    if far:
        pts_all, v_all = rest
        n = v_ref.shape[1] // 2
        own = leaf_dev - i0
        pts_all[0:own] = pts_ref[i0:leaf_dev]
        v_all[0:own] = v_ref[i0:leaf_dev]
        first = center_ref[leaf_dev - 1, 0:3, :]
        pts_all[own:] = jnp.zeros_like(pts_all[own:])
        for k in range(REACH):
            got = edge_ref[n : n + 3, k * W : (k + 1) * W]
            pts_all[own + k, 0:3, :] = got
            far_off = jnp.abs(got - first) * (SCALE * COMPACT / RANGE)
            wide = far_off if k == 0 else jnp.maximum(wide, far_off)
        load_values(v_all, edge_ref, REACH, own)
        compact = compact & (jnp.max(wide) <= COMPACT)
        pts_ref, v_ref = pts_all, v_all
        shift_by = i0
    if i0:
        acc_ref[...] = prev_ref[...]
    else:
        acc_ref[...] = jnp.zeros_like(acc_ref)
    tiles_ref[0] = jnp.zeros_like(tiles_ref[0])

    def finish(i, slot):
        to_row, to_col = products(
            tiles_ref.at[slot], v_ref[i - shift_by], v_ref[i + REACH - shift_by], listed_ref[i * STEPS + REACH]
        )
        acc_ref[i] += to_row
        acc_ref[i + REACH] += to_col

    def near_leaf(i, _):
        slot = (i - i0) * STEPS
        cols = cols_ref[i]
        center = center_ref[i]
        vi = v_ref[i - shift_by]

        def make(d):
            block = near_squares(cols, pts_ref[i + d - shift_by], center)
            make_tile(tiles_ref.at[slot + (1 + d)], block, d == 0)

        make(0)
        finish(jnp.maximum(i - 1, i0), slot)
        total = None
        for d in range(REACH):
            make(d + 1)
            to_row, to_col = products(
                tiles_ref.at[slot + (1 + d)], vi, v_ref[i + d - shift_by], listed_ref[i * STEPS + d]
            )
            total = to_row if total is None else total + to_row
            acc_ref[i + d] += to_col
        acc_ref[i] += total
        return 0

    def far_leaf(i, _):
        slot = (i - i0) * STEPS
        spread_rows(bc_ref, pts_ref[i - shift_by])

        def step(d, _):
            t_ref = tiles_ref.at[slot + (1 + d)]
            block = far_squares(bc_ref, pts_ref.at[i + d - shift_by])
            lax.cond(d == 0, lambda: make_tile(t_ref, block, True), lambda: make_tile(t_ref, block, False))

            @pl.when(d < REACH)
            def _():
                to_row, to_col = products(
                    t_ref, v_ref[i - shift_by], v_ref[i + d - shift_by], listed_ref[i * STEPS + d]
                )
                acc_ref[i] += to_row
                acc_ref[i + d] += to_col

            return 0

        @pl.when(i > i0)
        def _():
            finish(i - 1, slot)

        return lax.fori_loop(0, STEPS, step, 0)

    @pl.when(compact)
    def _():
        lax.fori_loop(i0, i1, near_leaf, 0)

    @pl.when(jnp.logical_not(compact))
    def _():
        lax.fori_loop(i0, i1, far_leaf, 0)

    finish(i1 - 1, (i1 - i0) * STEPS)
    if far:
        put_rows(rows_ref, acc_ref, leaf_dev, REACH)
    if last:
        put_rows(rows_ref, acc_ref, 0, leaf_dev, own_ref)


def apply_kernel(i0, i1, leaf_dev, last, listed_ref, tiles_ref, w_ref, *rest):
    rest = list(rest)
    far = i1 + REACH > leaf_dev
    far_ref = rest.pop(0) if far or last else None
    prev_ref = rest.pop(0) if i0 else None
    acc_ref = rest.pop(0)
    rows_ref = rest.pop(0) if last or far else None
    v_ref = rest.pop(0)
    load_values(v_ref, w_ref, leaf_dev, 0)
    if far:
        load_values(v_ref, far_ref, REACH, leaf_dev)
    if i0:
        acc_ref[...] = prev_ref[...]
    else:
        acc_ref[...] = jnp.zeros_like(acc_ref)

    def one_leaf(i, _):
        slot = (i - i0) * STEPS
        vi = v_ref[i]
        total = None
        for d in range(STEPS):
            to_row, to_col = products(
                tiles_ref.at[slot + (1 + d)], vi, v_ref[i + d], listed_ref[i * STEPS + d]
            )
            total = to_row if total is None else total + to_row
            acc_ref[i + d] += to_col
        acc_ref[i] += total
        return 0

    lax.fori_loop(i0, i1, one_leaf, 0)
    if far:
        put_rows(rows_ref, acc_ref, leaf_dev, REACH)
    if last:
        total = jnp.zeros(rows_ref.shape, jnp.float32)
        for k in range(leaf_dev):
            total += acc_ref[k] * w_ref[:, k * W : (k + 1) * W]
        for k in range(REACH):
            total += acc_ref[leaf_dev + k] * far_ref[:, k * W : (k + 1) * W]
        rows_ref[...] = total * (1.0 / PEAK)


def finish_kernel(leaf_dev, acc_ref, own_ref, back_ref, rows_ref):
    put_rows(rows_ref, acc_ref, 0, leaf_dev, own_ref)
    rows_ref[:, 0 : REACH * W] += back_ref[...]


VM = pl.BlockSpec(memory_space=pltpu.VMEM)
SM = pl.BlockSpec(memory_space=pltpu.SMEM)
HBM = pl.BlockSpec(memory_space=pltpu.HBM)
PARAMS = pltpu.CompilerParams(vmem_limit_bytes=8 << 20)


def prepare_call(pairs, count, base, coords, order, b):
    leaves = order.shape[0]
    n = b.shape[0]
    return pl.pallas_call(
        prepare_kernel,
        out_shape=(
            jax.ShapeDtypeStruct((pairs.shape[1], 16, HALF), jnp.bfloat16),
            jax.ShapeDtypeStruct((leaves, 8, W), jnp.float32),
            jax.ShapeDtypeStruct((leaves, W, 8 * GROUPS), jnp.bfloat16),
            jax.ShapeDtypeStruct((leaves, 2 * n, W), jnp.bfloat16),
            jax.ShapeDtypeStruct((leaves, 8, W), jnp.float32),
            jax.ShapeDtypeStruct((8, W), jnp.float32),
            jax.ShapeDtypeStruct((n + 3, REACH * W), jnp.float32),
        ),
        in_specs=[SM, SM, HBM, HBM, HBM, HBM],
        out_specs=(VM,) * 7,
        scratch_shapes=[
            pltpu.VMEM(pairs.shape, jnp.int32),
            pltpu.VMEM(coords.shape, jnp.float32),
            pltpu.VMEM(order.shape, jnp.int32),
            pltpu.VMEM(b.shape, jnp.float32),
            pltpu.SemaphoreType.DMA((4,)),
        ],
        compiler_params=PARAMS,
        name="prepare",
    )(count, base, *(pltpu.with_memory_space_constraint(x, pltpu.HBM) for x in (pairs, coords, order, b)))


def shapes_out(leaf_dev, n, far, last):
    acc = (leaf_dev + REACH, n, W)
    rows = (n, (leaf_dev if last else REACH) * W)
    f32 = jnp.float32
    if last:
        return [jax.ShapeDtypeStruct(rows, f32)], [pltpu.VMEM(acc, f32)]
    return [jax.ShapeDtypeStruct(acc, f32)] + ([jax.ShapeDtypeStruct(rows, f32)] if far else []), []


def evaluate_call(i0, i1, leaf_dev, n, prepared, far, own, prev):
    tiles = (i1 - i0) * STEPS
    last = own is not None
    ops = [*prepared, *far, *([own] if last else []), *([] if prev is None else [prev])]
    outs, held_acc = shapes_out(leaf_dev, n, bool(far), last)
    scratch = [*held_acc, pltpu.VMEM((W, 3 * HALF), jnp.float32)]
    if far:
        held = leaf_dev - i0 + REACH
        scratch += [pltpu.VMEM((held, 8, W), jnp.float32), pltpu.VMEM((held, 2 * n, W), jnp.bfloat16)]
    outs = [jax.ShapeDtypeStruct((tiles + 1, 4, W, HALF), jnp.bfloat16), *outs]
    return pl.pallas_call(
        functools.partial(evaluate_kernel, i0, i1, leaf_dev, last),
        out_shape=outs,
        in_specs=[VM] * len(ops),
        out_specs=[VM] * len(outs),
        scratch_shapes=scratch,
        compiler_params=PARAMS,
        cost_estimate=pl.CostEstimate(flops=tiles << 28, transcendentals=tiles << 17, bytes_accessed=tiles << 18),
        name=f"evaluate_{i0}",
    )(*ops)


def apply_call(i0, i1, leaf_dev, n, listed, tiles, own, far, last, prev):
    ops = [listed, tiles, own, *far, *([] if prev is None else [prev])]
    extent = leaf_dev + REACH
    f32 = jnp.float32
    outs = [jax.ShapeDtypeStruct((extent, n, W), f32)]
    if far:
        outs += [jax.ShapeDtypeStruct((n, W if last else REACH * W), f32)]
    return pl.pallas_call(
        functools.partial(apply_kernel, i0, i1, leaf_dev, last),
        out_shape=outs,
        in_specs=[VM] * len(ops),
        out_specs=[VM] * len(outs),
        scratch_shapes=[pltpu.VMEM((extent, 2 * n, W), jnp.bfloat16)],
        compiler_params=PARAMS,
        cost_estimate=pl.CostEstimate(flops=tiles.shape[0] << 27, transcendentals=0, bytes_accessed=tiles.size * 2),
        name=f"apply_{i0}",
    )(*ops)


def finish_call(leaf_dev, acc, own, back):
    return pl.pallas_call(
        functools.partial(finish_kernel, leaf_dev),
        out_shape=jax.ShapeDtypeStruct(own.shape, jnp.float32),
        in_specs=[VM] * 3,
        out_specs=VM,
        compiler_params=PARAMS,
        name="finish",
    )(acc, own, back)


def shift(value, by):
    length = lax.axis_size("leaf")
    return lax.ppermute(value, "leaf", [(i, i + by) for i in range(length) if 0 <= i + by < length])


def sum_over_leaf(value):
    length = lax.axis_size("leaf")
    value = value + lax.ppermute(value, "leaf", [(i, i ^ 1) for i in range(length)])
    copies = jnp.broadcast_to(value, (length // 2, *value.shape))
    groups = [[i for i in range(length) if i % 2 == c] for c in range(2)]
    got = lax.all_to_all(
        copies, "leaf", split_axis=0, concat_axis=0, tiled=True, axis_index_groups=groups
    )
    return jnp.sum(got, axis=0)


def body(coords, site_order, leaf_pairs, pair_count, probes):
    leaf_dev, width = site_order.shape
    n = probes.shape[0]
    edge = REACH * width
    base = (lax.axis_index("leaf") * leaf_dev).astype(jnp.int32).reshape(1)
    *prepared, packed = prepare_call(leaf_pairs, pair_count, base, coords, site_order, probes)
    far = shift(packed, -1)
    cut0, cut1 = leaf_dev - REACH - 5, leaf_dev - REACH
    evaluate = functools.partial(evaluate_call, leaf_dev=leaf_dev, n=n, prepared=prepared)
    tiles0, acc = evaluate(0, cut0, far=(), own=None, prev=None)
    tiles1, acc, send = evaluate(cut1, leaf_dev, far=(far,), own=None, prev=acc)
    back = shift(send, 1)
    tiles2, image = evaluate(cut0, cut1, far=(), own=probes, prev=acc)
    image = jnp.concatenate([image[:, :edge] + back, image[:, edge:]], axis=1)

    image_far = shift(image[:, :edge], -1)
    apply = functools.partial(apply_call, leaf_dev=leaf_dev, n=n, listed=prepared[0], own=image)
    (acc,) = apply(0, cut0, tiles=tiles0, far=(), last=False, prev=None)
    acc, send = apply(cut1, leaf_dev, tiles=tiles1, far=(image_far,), last=False, prev=acc)
    back = shift(send, 1)
    acc, dots = apply(cut0, cut1, tiles=tiles2, far=(image_far,), last=True, prev=acc)
    dots, back = lax.optimization_barrier((dots, back))
    square = jnp.sum(image * image, axis=1)
    sums = jnp.stack(
        [
            jnp.sum(probes * probes, axis=1),
            jnp.sum(probes * image, axis=1),
            square,
            jnp.sum(dots, axis=1) + NUGGET * square,
        ]
    )
    image2 = finish_call(leaf_dev, acc, image, back)
    rr, bw, ww, wz = sum_over_leaf(sums)
    alpha = rr / bw
    rr1 = rr - 2.0 * alpha * bw + alpha * alpha * ww
    beta = rr1 / rr
    g = 1.0 + beta
    curve = g * g * bw - 2.0 * g * alpha * ww + alpha * alpha * wz
    alpha1 = rr1 / curve
    c = lambda x: x[:, None]
    direction1 = c(g) * probes - c(alpha) * image
    image1 = c(g) * image - c(alpha) * image2
    solution = c(alpha) * probes + c(alpha1) * direction1
    residual = probes - c(alpha) * image - c(alpha1) * image1
    return solution, residual


def solution(mesh):
    in_specs = (P(None, "leaf"), P("leaf", None), P(None, "leaf"), P("leaf"), P("probe", "leaf"))
    out_specs = (P("probe", "leaf"), P("probe", "leaf"))
    return jax.shard_map(body, mesh=mesh, in_specs=in_specs, out_specs=out_specs, check_vma=False)
```

```python
import functools
import math

import jax
import jax.numpy as jnp
from jax import lax
from jax.experimental import pallas as pl
from jax.experimental.pallas import tpu as pltpu
from jax.sharding import PartitionSpec as P

REACH = 5
STEPS = REACH + 1
UNIT = 0.025
LENGTH = 0.12
NUGGET = 0.5
W = 256
TAPER = REACH * UNIT
DECAY = math.sqrt(3.0) * TAPER / LENGTH
LOG2E = math.log2(math.e)
CHUNK = 16
HALF = W // 2
FLOOR_INV = 1e18
KAPPA = DECAY * LOG2E
PEAK = KAPPA**6 / (4.0 * DECAY) * 2.0**KAPPA
SCALE = KAPPA / TAPER
COMPACT = 20.0 * KAPPA * KAPPA
RANGE = 1e15
TINY = 1e-12
GROUPS = 6


def split2(x):
    hi = x.astype(jnp.bfloat16)
    lo = (x - hi.astype(jnp.float32)).astype(jnp.bfloat16)
    return hi, lo


def split3(x):
    hi = x.astype(jnp.bfloat16)
    rest = x - hi.astype(jnp.float32)
    mid = rest.astype(jnp.bfloat16)
    lo = (rest - mid.astype(jnp.float32)).astype(jnp.bfloat16)
    return hi, mid, lo


def load_values(v_ref, src_ref, leaves, first):
    n = v_ref.shape[1] // 2
    for k in range(leaves):
        hi, lo = split2(src_ref[0:n, k * W : (k + 1) * W])
        v_ref[first + k] = jnp.concatenate([hi, lo], axis=0)


def split_rows(point, center, top, weight):
    x = (point - center) * SCALE
    sq = x * x
    sq = sq[0:1] + sq[1:2] + sq[2:3]
    row = lax.broadcasted_iota(jnp.int32, x.shape, 0)
    x = jnp.where(top, x * weight, jnp.where(row == 3, sq, 0.0))
    hi = x.astype(jnp.bfloat16).astype(jnp.float32)
    rest = x - hi
    mid = rest.astype(jnp.bfloat16).astype(jnp.float32)
    return hi, mid, rest - mid


def prepare_kernel(
    count_ref, base_ref, pairs_hbm, coords_hbm, order_hbm, b_hbm,
    listed_ref, pts_ref, cols_ref, v_ref, center_ref, wide_ref, edge_ref,
    pairs_ref, coords_ref, order_ref, b_ref, sems,
):
    copies = [
        pltpu.make_async_copy(pairs_hbm, pairs_ref, sems.at[0]),
        pltpu.make_async_copy(coords_hbm, coords_ref, sems.at[1]),
        pltpu.make_async_copy(order_hbm, order_ref, sems.at[2]),
        pltpu.make_async_copy(b_hbm, b_ref, sems.at[3]),
    ]
    for copy in copies:
        copy.start()
    copies[0].wait()
    slots = pairs_ref.shape[1]
    row = pairs_ref[0:1, :]
    place = (row - base_ref[0]) * STEPS + pairs_ref[1:2, :] - row
    live = lax.broadcasted_iota(jnp.int32, (1, slots), 1) < count_ref[0]
    place = jnp.where(live, place, -1)
    hit = lax.broadcasted_iota(jnp.int32, (slots, slots), 0) == place
    found = jnp.sum(hit.astype(jnp.float32), axis=1, keepdims=True)
    listed_ref[...] = jnp.broadcast_to(found.astype(jnp.bfloat16)[:, :, None], listed_ref.shape)
    for copy in copies[1:]:
        copy.wait()
    leaves = order_ref.shape[0]
    n = b_ref.shape[0]
    sub = lax.broadcasted_iota(jnp.int32, (W, W), 0)
    dot = functools.partial(jnp.dot, preferred_element_type=jnp.float32)
    top = lax.broadcasted_iota(jnp.int32, (8, W), 0) < 3
    pad = jnp.zeros((5, W), jnp.float32)
    wide = jnp.zeros((8, W), jnp.float32)
    for k in range(leaves):
        at = slice(k * W, (k + 1) * W)
        sel = (sub == order_ref[k : k + 1, :]).astype(jnp.float32).astype(jnp.bfloat16)
        parts = [dot(p, sel) for p in split3(coords_ref[:, at])]
        got = parts[0] + parts[1] + parts[2]
        point = jnp.concatenate([got, pad], axis=0)
        center = jnp.broadcast_to(jnp.sum(point, axis=1, keepdims=True) * (1.0 / W), (8, W))
        pts_ref[k] = point
        center_ref[k] = center
        hi, mid, lo = split_rows(point, center, top, 1.0)
        square = jnp.where(top, 0.0, hi + mid + lo)
        first = center if k == 0 else first
        far_off = jnp.abs(point - first) * (SCALE * COMPACT / RANGE)
        wide = jnp.maximum(wide, jnp.maximum(square, far_off))
        one = jnp.where(lax.broadcasted_iota(jnp.int32, (8, W), 0) == 3, 1.0, 0.0)
        stack = [hi, jnp.where(top, hi, mid), jnp.where(top, hi, lo)]
        stack += [jnp.where(top, mid, one), jnp.where(top, mid, one), jnp.where(top, lo, one)]
        cols_ref[k] = jnp.transpose(jnp.concatenate(stack, axis=0)).astype(jnp.bfloat16)
        if k < REACH:
            edge_ref[0:n, at] = b_ref[:, at]
            edge_ref[n : n + 3, at] = got
    wide_ref[...] = wide
    load_values(v_ref, b_ref, leaves, 0)


def spread_rows(bc_ref, points):
    cols = jnp.transpose(points)
    for c in range(3):
        bc_ref[:, c * HALF : (c + 1) * HALF] = jnp.broadcast_to(cols[:, c : c + 1], (W, HALF))


def far_squares(bc_ref, other):
    def block(rows, h):
        u = None
        for c in range(3):
            b = jnp.broadcast_to(other[c : c + 1, h * HALF : (h + 1) * HALF], (CHUNK, HALF))
            d = bc_ref[rows, c * HALF : (c + 1) * HALF] - b
            u = d * d if u is None else u + d * d
        return u * (SCALE * SCALE)

    return block


def near_squares(cols, other, center):
    top = lax.broadcasted_iota(jnp.int32, (8, W), 0) < 3
    one = jnp.where(lax.broadcasted_iota(jnp.int32, (8, W), 0) == 3, 1.0, 0.0)
    hi, mid, lo = split_rows(other, center, top, -2.0)
    stack = [jnp.where(top, hi, one), jnp.where(top, mid, one), jnp.where(top, lo, one)]
    stack += [hi, mid, jnp.where(top, hi, lo)]
    rows = jnp.concatenate(stack, axis=0).astype(jnp.bfloat16)
    all_u = jnp.dot(cols, rows, preferred_element_type=jnp.float32)
    return lambda rows, h: all_u[rows, h * HALF : (h + 1) * HALF]


def make_tile(t_ref, block, same):
    for k in range(W // CHUNK):
        rows = slice(k * CHUNK, (k + 1) * CHUNK)
        lower = k * CHUNK >= HALF
        for h in range(2):
            if same and lower and h == 0:
                t_ref[0, rows, :] = jnp.zeros((CHUNK, HALF), jnp.bfloat16)
                t_ref[2, rows, :] = jnp.zeros((CHUNK, HALF), jnp.bfloat16)
                continue
            u = jnp.minimum(jnp.maximum(block(rows, h), TINY), KAPPA * KAPPA)
            q = u * lax.rsqrt(u)
            t = KAPPA - q
            e = jnp.exp2(t)
            t = t * t
            t = t * t
            x = ((q + KAPPA / 4.0) * (q + KAPPA / DECAY)) * (t * e)
            if same and lower == bool(h):
                x = x * 0.5
            hi, lo = split2(x)
            t_ref[h, rows, :] = hi
            t_ref[2 + h, rows, :] = lo


def product(t_ref, v, listed, transposed):
    hi = jnp.concatenate([t_ref[0], t_ref[1]], axis=1)
    lo = jnp.concatenate([t_ref[2], t_ref[3]], axis=1)
    dims = (((1,), (1 if transposed else 0,)), ((), ()))
    dot = functools.partial(lax.dot_general, dimension_numbers=dims, preferred_element_type=jnp.float32)
    n = v.shape[0] // 2
    keep = jnp.concatenate([listed, listed], axis=1)
    v = v * jnp.concatenate([keep, keep], axis=0)
    p = dot(v, hi)
    return p[:n] + p[n:] + dot(v[:n], lo)


def products(t_ref, vi, vj, listed):
    return product(t_ref, vj, listed, True), product(t_ref, vi, listed, False)


def put_rows(out_ref, acc_ref, first, leaves, own_ref=None):
    for k in range(leaves):
        at = slice(k * W, (k + 1) * W)
        x = acc_ref[first + k] * (1.0 / PEAK)
        out_ref[:, at] = x if own_ref is None else x + NUGGET * own_ref[:, at]


def evaluate_kernel(i0, i1, leaf_dev, last, listed_ref, pts_ref, cols_ref, v_ref, center_ref, wide_ref, *rest):
    rest = list(rest)
    far = i1 + REACH > leaf_dev
    shift_by = 0
    edge_ref = rest.pop(0) if far else None
    own_ref = rest.pop(0) if last else None
    prev_ref = rest.pop(0) if i0 else None
    tiles_ref = rest.pop(0)
    acc_ref = rest.pop(1 if last else 0)
    rows_ref = rest.pop(0) if last or far else None
    bc_ref = rest.pop(0)
    compact = jnp.max(wide_ref[...]) <= COMPACT
    if far:
        pts_all, v_all = rest
        n = v_ref.shape[1] // 2
        own = leaf_dev - i0
        pts_all[0:own] = pts_ref[i0:leaf_dev]
        v_all[0:own] = v_ref[i0:leaf_dev]
        first = center_ref[leaf_dev - 1, 0:3, :]
        pts_all[own:] = jnp.zeros_like(pts_all[own:])
        for k in range(REACH):
            got = edge_ref[n : n + 3, k * W : (k + 1) * W]
            pts_all[own + k, 0:3, :] = got
            far_off = jnp.abs(got - first) * (SCALE * COMPACT / RANGE)
            wide = far_off if k == 0 else jnp.maximum(wide, far_off)
        load_values(v_all, edge_ref, REACH, own)
        compact = compact & (jnp.max(wide) <= COMPACT)
        pts_ref, v_ref = pts_all, v_all
        shift_by = i0
    if i0:
        acc_ref[...] = prev_ref[...]
    else:
        acc_ref[...] = jnp.zeros_like(acc_ref)
    tiles_ref[0] = jnp.zeros_like(tiles_ref[0])

    def finish(i, slot):
        to_row, to_col = products(
            tiles_ref.at[slot], v_ref[i - shift_by], v_ref[i + REACH - shift_by], listed_ref[i * STEPS + REACH]
        )
        acc_ref[i] += to_row
        acc_ref[i + REACH] += to_col

    def near_leaf(i, _):
        slot = (i - i0) * STEPS
        cols = cols_ref[i]
        center = center_ref[i]
        vi = v_ref[i - shift_by]

        def make(d):
            block = near_squares(cols, pts_ref[i + d - shift_by], center)
            make_tile(tiles_ref.at[slot + (1 + d)], block, d == 0)

        make(0)
        finish(jnp.maximum(i - 1, i0), slot)
        total = None
        for d in range(REACH):
            make(d + 1)
            to_row, to_col = products(
                tiles_ref.at[slot + (1 + d)], vi, v_ref[i + d - shift_by], listed_ref[i * STEPS + d]
            )
            total = to_row if total is None else total + to_row
            acc_ref[i + d] += to_col
        acc_ref[i] += total
        return 0

    def far_leaf(i, _):
        slot = (i - i0) * STEPS
        spread_rows(bc_ref, pts_ref[i - shift_by])

        def step(d, _):
            t_ref = tiles_ref.at[slot + (1 + d)]
            block = far_squares(bc_ref, pts_ref.at[i + d - shift_by])
            lax.cond(d == 0, lambda: make_tile(t_ref, block, True), lambda: make_tile(t_ref, block, False))

            @pl.when(d < REACH)
            def _():
                to_row, to_col = products(
                    t_ref, v_ref[i - shift_by], v_ref[i + d - shift_by], listed_ref[i * STEPS + d]
                )
                acc_ref[i] += to_row
                acc_ref[i + d] += to_col

            return 0

        @pl.when(i > i0)
        def _():
            finish(i - 1, slot)

        return lax.fori_loop(0, STEPS, step, 0)

    @pl.when(compact)
    def _():
        lax.fori_loop(i0, i1, near_leaf, 0)

    @pl.when(jnp.logical_not(compact))
    def _():
        lax.fori_loop(i0, i1, far_leaf, 0)

    finish(i1 - 1, (i1 - i0) * STEPS)
    if far:
        put_rows(rows_ref, acc_ref, leaf_dev, REACH)
    if last:
        put_rows(rows_ref, acc_ref, 0, leaf_dev, own_ref)


def clear_or_copy(acc_ref, prev_ref):
    acc_ref[...] = jnp.zeros_like(acc_ref) if prev_ref is None else prev_ref[...]


def weighted(acc_ref, field_ref, first, leaves):
    total = acc_ref[first] * field_ref[:, 0:W]
    for k in range(1, leaves):
        total += acc_ref[first + k] * field_ref[:, k * W : (k + 1) * W]
    return total


def apply_kernel(i0, i1, leaf_dev, last, listed_ref, tiles_ref, w_ref, *rest):
    rest = list(rest)
    if last:
        far_ref, extra_ref = rest.pop(0), rest.pop(0)
    prev_ref = rest.pop(0) if i0 else None
    acc_ref = rest.pop(0)
    dots_ref = rest.pop(0) if last else None
    v_ref = rest.pop(0)
    load_values(v_ref, w_ref, leaf_dev, 0)
    clear_or_copy(acc_ref, prev_ref)

    def one_leaf(i, _):
        slot = (i - i0) * STEPS
        vi = v_ref[i]
        total = None
        for d in range(STEPS):
            to_row, to_col = products(
                tiles_ref.at[slot + (1 + d)], vi, v_ref[i + d], listed_ref[i * STEPS + d]
            )
            total = to_row if total is None else total + to_row
            acc_ref[i + d] += to_col
        acc_ref[i] += total
        return 0

    lax.fori_loop(i0, i1, one_leaf, 0)
    if last:
        total = weighted(acc_ref, w_ref, 0, leaf_dev) + weighted(acc_ref, far_ref, leaf_dev, REACH)
        dots_ref[...] = (total + extra_ref[...]) * (1.0 / PEAK)


def edge_kernel(i0, leaf_dev, listed_ref, tiles_ref, w_ref, far_ref, prev_ref, acc_ref, send_ref, dots_ref, v_ref, part_ref):
    held = leaf_dev - i0
    load_values(v_ref, w_ref, leaf_dev, 0)
    clear_or_copy(part_ref, None)

    def one_leaf(i, _):
        slot = (i - i0) * STEPS
        vi = v_ref[i]
        for d in range(STEPS):
            part_ref[i - i0 + d] += product(
                tiles_ref.at[slot + (1 + d)], vi, listed_ref[i * STEPS + d], False
            )
        return 0

    lax.fori_loop(i0, leaf_dev, one_leaf, 0)
    dots_ref[...] = weighted(part_ref, w_ref.at[:, i0 * W :], 0, held) + weighted(part_ref, far_ref, held, REACH)
    acc_ref[...] = prev_ref[...]
    for k in range(held + REACH):
        acc_ref[i0 + k] += part_ref[k]
    put_rows(send_ref, acc_ref, leaf_dev, REACH)


def finish_kernel(
    i0, leaf_dev, listed_ref, tiles_hbm, w_ref, far_ref, prev_ref, back_ref, rows_ref, v_ref, acc_ref, tiles_ref, sems
):
    copies = []
    for k in range(leaf_dev - i0):
        at = pl.ds(k * STEPS, STEPS)
        copies.append(pltpu.make_async_copy(tiles_hbm.at[pl.ds(k * STEPS + 1, STEPS)], tiles_ref.at[at], sems.at[k]))
        copies[k].start()
    load_values(v_ref, w_ref.at[:, i0 * W :], leaf_dev - i0, 0)
    load_values(v_ref, far_ref, REACH, leaf_dev - i0)
    acc_ref[...] = prev_ref[...]
    for k, copy in enumerate(copies):
        copy.wait()
        total = None
        for d in range(STEPS):
            to_row = product(tiles_ref.at[k * STEPS + d], v_ref[k + d], listed_ref[(i0 + k) * STEPS + d], True)
            total = to_row if total is None else total + to_row
        acc_ref[i0 + k] += total
    put_rows(rows_ref, acc_ref, 0, leaf_dev, w_ref)
    rows_ref[:, 0 : REACH * W] += back_ref[...]


VM = pl.BlockSpec(memory_space=pltpu.VMEM)
SM = pl.BlockSpec(memory_space=pltpu.SMEM)
HBM = pl.BlockSpec(memory_space=pltpu.HBM)
PARAMS = pltpu.CompilerParams(vmem_limit_bytes=8 << 20)


def prepare_call(pairs, count, base, coords, order, b):
    leaves = order.shape[0]
    n = b.shape[0]
    return pl.pallas_call(
        prepare_kernel,
        out_shape=(
            jax.ShapeDtypeStruct((pairs.shape[1], 16, HALF), jnp.bfloat16),
            jax.ShapeDtypeStruct((leaves, 8, W), jnp.float32),
            jax.ShapeDtypeStruct((leaves, W, 8 * GROUPS), jnp.bfloat16),
            jax.ShapeDtypeStruct((leaves, 2 * n, W), jnp.bfloat16),
            jax.ShapeDtypeStruct((leaves, 8, W), jnp.float32),
            jax.ShapeDtypeStruct((8, W), jnp.float32),
            jax.ShapeDtypeStruct((n + 3, REACH * W), jnp.float32),
        ),
        in_specs=[SM, SM, HBM, HBM, HBM, HBM],
        out_specs=(VM,) * 7,
        scratch_shapes=[
            pltpu.VMEM(pairs.shape, jnp.int32),
            pltpu.VMEM(coords.shape, jnp.float32),
            pltpu.VMEM(order.shape, jnp.int32),
            pltpu.VMEM(b.shape, jnp.float32),
            pltpu.SemaphoreType.DMA((4,)),
        ],
        compiler_params=PARAMS,
        name="prepare",
    )(count, base, *(pltpu.with_memory_space_constraint(x, pltpu.HBM) for x in (pairs, coords, order, b)))


def shapes_out(leaf_dev, n, far, last):
    acc = (leaf_dev + REACH, n, W)
    rows = (n, (leaf_dev if last else REACH) * W)
    f32 = jnp.float32
    if last:
        return [jax.ShapeDtypeStruct(rows, f32)], [pltpu.VMEM(acc, f32)]
    return [jax.ShapeDtypeStruct(acc, f32)] + ([jax.ShapeDtypeStruct(rows, f32)] if far else []), []


def evaluate_call(i0, i1, leaf_dev, n, prepared, far, own, prev):
    tiles = (i1 - i0) * STEPS
    last = own is not None
    ops = [*prepared, *far, *([own] if last else []), *([] if prev is None else [prev])]
    outs, held_acc = shapes_out(leaf_dev, n, bool(far), last)
    scratch = [*held_acc, pltpu.VMEM((W, 3 * HALF), jnp.float32)]
    if far:
        held = leaf_dev - i0 + REACH
        scratch += [pltpu.VMEM((held, 8, W), jnp.float32), pltpu.VMEM((held, 2 * n, W), jnp.bfloat16)]
    outs = [jax.ShapeDtypeStruct((tiles + 1, 4, W, HALF), jnp.bfloat16), *outs]
    return pl.pallas_call(
        functools.partial(evaluate_kernel, i0, i1, leaf_dev, last),
        out_shape=outs,
        in_specs=[VM] * len(ops),
        out_specs=[VM] * len(outs),
        scratch_shapes=scratch,
        compiler_params=PARAMS,
        cost_estimate=pl.CostEstimate(flops=tiles << 28, transcendentals=tiles << 17, bytes_accessed=tiles << 18),
        name=f"evaluate_{i0}",
    )(*ops)


def small_call(kernel, name, outs, scratch, tiles, ops, in_hbm=()):
    return pl.pallas_call(
        kernel,
        out_shape=[jax.ShapeDtypeStruct(shape, jnp.float32) for shape in outs],
        in_specs=[HBM if k in in_hbm else VM for k in range(len(ops))],
        out_specs=[VM] * len(outs),
        scratch_shapes=scratch,
        compiler_params=pltpu.CompilerParams(vmem_limit_bytes=14 << 20) if in_hbm else PARAMS,
        cost_estimate=pl.CostEstimate(flops=tiles.shape[0] << 27, transcendentals=0, bytes_accessed=tiles.size * 2),
        name=name,
    )(*[pltpu.with_memory_space_constraint(x, pltpu.HBM) if k in in_hbm else x for k, x in enumerate(ops)])


def apply_call(i0, i1, leaf_dev, n, listed, tiles, own, last, prev):
    acc = (leaf_dev + REACH, n, W)
    ops = [listed, tiles, own, *last, *([] if prev is None else [prev])]
    return small_call(
        functools.partial(apply_kernel, i0, i1, leaf_dev, bool(last)),
        f"apply_{i0}",
        [acc, (n, W)] if last else [acc],
        [pltpu.VMEM((leaf_dev, 2 * n, W), jnp.bfloat16)],
        tiles,
        ops,
    )


def edge_call(i0, leaf_dev, n, listed, tiles, own, far, prev):
    acc = (leaf_dev + REACH, n, W)
    return small_call(
        functools.partial(edge_kernel, i0, leaf_dev),
        "apply_edge",
        [acc, (n, REACH * W), (n, W)],
        [
            pltpu.VMEM((leaf_dev, 2 * n, W), jnp.bfloat16),
            pltpu.VMEM((leaf_dev - i0 + REACH, n, W), jnp.float32),
        ],
        tiles,
        [listed, tiles, own, far, prev],
    )


def finish_call(i0, leaf_dev, n, listed, tiles, own, far, prev, back):
    acc = (leaf_dev + REACH, n, W)
    return small_call(
        functools.partial(finish_kernel, i0, leaf_dev),
        "finish",
        [own.shape],
        [
            pltpu.VMEM((leaf_dev - i0 + REACH, 2 * n, W), jnp.bfloat16),
            pltpu.VMEM(acc, jnp.float32),
            pltpu.VMEM((tiles.shape[0] - 1, *tiles.shape[1:]), jnp.bfloat16),
            pltpu.SemaphoreType.DMA((leaf_dev - i0,)),
        ],
        tiles,
        [listed, tiles, own, far, prev, back],
        in_hbm=(1,),
    )[0]


def shift(value, by):
    length = lax.axis_size("leaf")
    return lax.ppermute(value, "leaf", [(i, i + by) for i in range(length) if 0 <= i + by < length])


def sum_over_leaf(value):
    length = lax.axis_size("leaf")
    value = value + lax.ppermute(value, "leaf", [(i, i ^ 1) for i in range(length)])
    copies = jnp.broadcast_to(value.reshape(-1), (length // 2, value.size))
    groups = [[i for i in range(length) if i % 2 == c] for c in range(2)]
    got = lax.all_to_all(
        copies, "leaf", split_axis=0, concat_axis=0, tiled=True, axis_index_groups=groups
    )
    return jnp.sum(got, axis=0).reshape(value.shape)


def body(coords, site_order, leaf_pairs, pair_count, probes):
    leaf_dev, width = site_order.shape
    n = probes.shape[0]
    edge = REACH * width
    base = (lax.axis_index("leaf") * leaf_dev).astype(jnp.int32).reshape(1)
    *prepared, packed = prepare_call(leaf_pairs, pair_count, base, coords, site_order, probes)
    far = shift(packed, -1)
    cut0, cut1 = leaf_dev - REACH - 5, leaf_dev - REACH
    evaluate = functools.partial(evaluate_call, leaf_dev=leaf_dev, n=n, prepared=prepared)
    tiles0, acc = evaluate(0, cut0, far=(), own=None, prev=None)
    tiles1, acc, send = evaluate(cut1, leaf_dev, far=(far,), own=None, prev=acc)
    back = shift(send, 1)
    tiles2, image = evaluate(cut0, cut1, far=(), own=probes, prev=acc)
    image = jnp.concatenate([image[:, :edge] + back, image[:, edge:]], axis=1)

    image_far = shift(image[:, :edge], -1)
    common = dict(leaf_dev=leaf_dev, n=n, listed=prepared[0], own=image)
    (acc,) = apply_call(0, cut0, tiles=tiles0, last=(), prev=None, **common)
    acc, send, edge_dots = edge_call(cut1, tiles=tiles1, far=image_far, prev=acc, **common)
    back = shift(send, 1)
    acc, dots = apply_call(cut0, cut1, tiles=tiles2, last=(image_far, edge_dots), prev=acc, **common)
    dots, back = lax.optimization_barrier((dots, back))
    square = jnp.sum(image * image, axis=1)
    sums = jnp.stack(
        [
            jnp.sum(probes * probes, axis=1),
            jnp.sum(probes * image, axis=1),
            square,
            jnp.sum(dots, axis=1) + NUGGET * square,
        ]
    )
    image2 = finish_call(cut1, tiles=tiles1, far=image_far, prev=acc, back=back, **common)
    rr, bw, ww, wz = sum_over_leaf(sums)
    alpha = rr / bw
    rr1 = rr - 2.0 * alpha * bw + alpha * alpha * ww
    beta = rr1 / rr
    g = 1.0 + beta
    curve = g * g * bw - 2.0 * g * alpha * ww + alpha * alpha * wz
    alpha1 = rr1 / curve
    c = lambda x: x[:, None]
    direction1 = c(g) * probes - c(alpha) * image
    image1 = c(g) * image - c(alpha) * image2
    solution = c(alpha) * probes + c(alpha1) * direction1
    residual = probes - c(alpha) * image - c(alpha1) * image1
    return solution, residual


def solution(mesh):
    in_specs = (P(None, "leaf"), P("leaf", None), P(None, "leaf"), P("leaf"), P("probe", "leaf"))
    out_specs = (P("probe", "leaf"), P("probe", "leaf"))
    return jax.shard_map(body, mesh=mesh, in_specs=in_specs, out_specs=out_specs, check_vma=False)
```

```python
import functools
import math

import jax
import jax.numpy as jnp
from jax import lax
from jax.experimental import pallas as pl
from jax.experimental.pallas import tpu as pltpu
from jax.sharding import PartitionSpec as P

REACH = 5
STEPS = REACH + 1
UNIT = 0.025
LENGTH = 0.12
NUGGET = 0.5
W = 256
TAPER = REACH * UNIT
DECAY = math.sqrt(3.0) * TAPER / LENGTH
LOG2E = math.log2(math.e)
CHUNK = 16
HALF = W // 2
FLOOR_INV = 1e18
KAPPA = DECAY * LOG2E
PEAK = KAPPA**6 / (4.0 * DECAY) * 2.0**KAPPA
SCALE = KAPPA / TAPER
COMPACT = 20.0 * KAPPA * KAPPA
RANGE = 1e15
TINY = 1e-12
GROUPS = 6


def split2(x):
    hi = x.astype(jnp.bfloat16)
    lo = (x - hi.astype(jnp.float32)).astype(jnp.bfloat16)
    return hi, lo


def split3(x):
    hi = x.astype(jnp.bfloat16)
    rest = x - hi.astype(jnp.float32)
    mid = rest.astype(jnp.bfloat16)
    lo = (rest - mid.astype(jnp.float32)).astype(jnp.bfloat16)
    return hi, mid, lo


def load_values(v_ref, src_ref, leaves, first):
    n = v_ref.shape[1] // 2
    for k in range(leaves):
        hi, lo = split2(src_ref[0:n, k * W : (k + 1) * W])
        v_ref[first + k] = jnp.concatenate([hi, lo], axis=0)


def split_rows(point, center, top, weight):
    x = (point - center) * SCALE
    sq = x * x
    sq = sq[0:1] + sq[1:2] + sq[2:3]
    row = lax.broadcasted_iota(jnp.int32, x.shape, 0)
    x = jnp.where(top, x * weight, jnp.where(row == 3, sq, 0.0))
    hi = x.astype(jnp.bfloat16).astype(jnp.float32)
    rest = x - hi
    mid = rest.astype(jnp.bfloat16).astype(jnp.float32)
    return hi, mid, rest - mid


def prepare_kernel(
    count_ref, base_ref, pairs_hbm, coords_hbm, order_hbm, b_hbm,
    listed_ref, pts_ref, cols_ref, v_ref, center_ref, wide_ref, edge_ref,
    pairs_ref, coords_ref, order_ref, b_ref, sems,
):
    copies = [
        pltpu.make_async_copy(pairs_hbm, pairs_ref, sems.at[0]),
        pltpu.make_async_copy(coords_hbm, coords_ref, sems.at[1]),
        pltpu.make_async_copy(order_hbm, order_ref, sems.at[2]),
        pltpu.make_async_copy(b_hbm, b_ref, sems.at[3]),
    ]
    for copy in copies:
        copy.start()
    copies[0].wait()
    slots = pairs_ref.shape[1]
    row = pairs_ref[0:1, :]
    place = (row - base_ref[0]) * STEPS + pairs_ref[1:2, :] - row
    live = lax.broadcasted_iota(jnp.int32, (1, slots), 1) < count_ref[0]
    place = jnp.where(live, place, -1)
    hit = lax.broadcasted_iota(jnp.int32, (slots, slots), 0) == place
    found = jnp.sum(hit.astype(jnp.float32), axis=1, keepdims=True)
    listed_ref[...] = jnp.broadcast_to(found.astype(jnp.bfloat16)[:, :, None], listed_ref.shape)
    for copy in copies[1:]:
        copy.wait()
    leaves = order_ref.shape[0]
    n = b_ref.shape[0]
    sub = lax.broadcasted_iota(jnp.int32, (W, W), 0).astype(jnp.float32).astype(jnp.bfloat16)
    one, zero = jnp.ones((W, W), jnp.bfloat16), jnp.zeros((W, W), jnp.bfloat16)
    dot = functools.partial(jnp.dot, preferred_element_type=jnp.float32)
    top = lax.broadcasted_iota(jnp.int32, (8, W), 0) < 3
    pad = jnp.zeros((5, W), jnp.float32)
    wide = jnp.zeros((8, W), jnp.float32)
    for k in range(leaves):
        at = slice(k * W, (k + 1) * W)
        order = order_ref[k : k + 1, :].astype(jnp.float32).astype(jnp.bfloat16)
        sel = jnp.where(sub == jnp.broadcast_to(order, (W, W)), one, zero)
        raw = jnp.concatenate([coords_ref[:, at], pad], axis=0)
        parts = dot(jnp.concatenate(split3(raw), axis=0), sel)
        point = parts[0:8] + parts[8:16] + parts[16:24]
        got = point[0:3]
        center = jnp.broadcast_to(jnp.sum(point, axis=1, keepdims=True) * (1.0 / W), (8, W))
        pts_ref[k] = point
        center_ref[k] = center
        hi, mid, lo = split_rows(point, center, top, 1.0)
        square = jnp.where(top, 0.0, hi + mid + lo)
        first = center if k == 0 else first
        far_off = jnp.abs(point - first) * (SCALE * COMPACT / RANGE)
        wide = jnp.maximum(wide, jnp.maximum(square, far_off))
        unit = jnp.where(lax.broadcasted_iota(jnp.int32, (8, W), 0) == 3, 1.0, 0.0)
        stack = [hi, jnp.where(top, hi, mid), jnp.where(top, hi, lo)]
        stack += [jnp.where(top, mid, unit), jnp.where(top, mid, unit), jnp.where(top, lo, unit)]
        cols_ref[k] = jnp.transpose(jnp.concatenate(stack, axis=0)).astype(jnp.bfloat16)
        if k < REACH:
            edge_ref[0:n, at] = b_ref[:, at]
            edge_ref[n : n + 3, at] = got
    wide_ref[...] = wide
    load_values(v_ref, b_ref, leaves, 0)


def spread_rows(bc_ref, points):
    cols = jnp.transpose(points)
    for c in range(3):
        bc_ref[:, c * HALF : (c + 1) * HALF] = jnp.broadcast_to(cols[:, c : c + 1], (W, HALF))


def far_squares(bc_ref, other):
    def block(rows, h):
        u = None
        for c in range(3):
            b = jnp.broadcast_to(other[c : c + 1, h * HALF : (h + 1) * HALF], (CHUNK, HALF))
            d = bc_ref[rows, c * HALF : (c + 1) * HALF] - b
            u = d * d if u is None else u + d * d
        return u * (SCALE * SCALE)

    return block


def near_squares(cols, other, center):
    top = lax.broadcasted_iota(jnp.int32, (8, W), 0) < 3
    one = jnp.where(lax.broadcasted_iota(jnp.int32, (8, W), 0) == 3, 1.0, 0.0)
    hi, mid, lo = split_rows(other, center, top, -2.0)
    stack = [jnp.where(top, hi, one), jnp.where(top, mid, one), jnp.where(top, lo, one)]
    stack += [hi, mid, jnp.where(top, hi, lo)]
    rows = jnp.concatenate(stack, axis=0).astype(jnp.bfloat16)
    all_u = jnp.dot(cols, rows, preferred_element_type=jnp.float32)
    return lambda rows, h: all_u[rows, h * HALF : (h + 1) * HALF]


def make_tile(t_ref, block, same):
    for k in range(W // CHUNK):
        rows = slice(k * CHUNK, (k + 1) * CHUNK)
        lower = k * CHUNK >= HALF
        for h in range(2):
            if same and lower and h == 0:
                t_ref[0, rows, :] = jnp.zeros((CHUNK, HALF), jnp.bfloat16)
                t_ref[2, rows, :] = jnp.zeros((CHUNK, HALF), jnp.bfloat16)
                continue
            u = jnp.minimum(jnp.maximum(block(rows, h), TINY), KAPPA * KAPPA)
            q = u * lax.rsqrt(u)
            t = KAPPA - q
            e = jnp.exp2(t)
            t = t * t
            t = t * t
            x = ((q + KAPPA / 4.0) * (q + KAPPA / DECAY)) * (t * e)
            if same and lower == bool(h):
                x = x * 0.5
            hi, lo = split2(x)
            t_ref[h, rows, :] = hi
            t_ref[2 + h, rows, :] = lo


def product(t_ref, v, listed, transposed):
    hi = jnp.concatenate([t_ref[0], t_ref[1]], axis=1)
    lo = jnp.concatenate([t_ref[2], t_ref[3]], axis=1)
    dims = (((1,), (1 if transposed else 0,)), ((), ()))
    dot = functools.partial(lax.dot_general, dimension_numbers=dims, preferred_element_type=jnp.float32)
    n = v.shape[0] // 2
    keep = jnp.concatenate([listed, listed], axis=1)
    v = v * jnp.concatenate([keep, keep], axis=0)
    p = dot(v, hi)
    return p[:n] + p[n:] + dot(v[:n], lo)


def products(t_ref, vi, vj, listed):
    return product(t_ref, vj, listed, True), product(t_ref, vi, listed, False)


def put_rows(out_ref, acc_ref, first, leaves, own_ref=None):
    for k in range(leaves):
        at = slice(k * W, (k + 1) * W)
        x = acc_ref[first + k] * (1.0 / PEAK)
        out_ref[:, at] = x if own_ref is None else x + NUGGET * own_ref[:, at]


def evaluate_kernel(i0, i1, leaf_dev, last, listed_ref, pts_ref, cols_ref, v_ref, center_ref, wide_ref, *rest):
    rest = list(rest)
    far = i1 + REACH > leaf_dev
    shift_by = 0
    edge_ref = rest.pop(0) if far else None
    own_ref = rest.pop(0) if last else None
    prev_ref = rest.pop(0) if i0 else None
    tiles_ref = rest.pop(0)
    acc_ref = rest.pop(1 if last else 0)
    rows_ref = rest.pop(0) if last or far else None
    bc_ref = rest.pop(0)
    compact = jnp.max(wide_ref[...]) <= COMPACT
    if far:
        pts_all, v_all = rest
        n = v_ref.shape[1] // 2
        own = leaf_dev - i0
        pts_all[0:own] = pts_ref[i0:leaf_dev]
        v_all[0:own] = v_ref[i0:leaf_dev]
        first = center_ref[leaf_dev - 1, 0:3, :]
        pts_all[own:] = jnp.zeros_like(pts_all[own:])
        for k in range(REACH):
            got = edge_ref[n : n + 3, k * W : (k + 1) * W]
            pts_all[own + k, 0:3, :] = got
            far_off = jnp.abs(got - first) * (SCALE * COMPACT / RANGE)
            wide = far_off if k == 0 else jnp.maximum(wide, far_off)
        load_values(v_all, edge_ref, REACH, own)
        compact = compact & (jnp.max(wide) <= COMPACT)
        pts_ref, v_ref = pts_all, v_all
        shift_by = i0
    if i0:
        acc_ref[...] = prev_ref[...]
    else:
        acc_ref[...] = jnp.zeros_like(acc_ref)
    tiles_ref[0] = jnp.zeros_like(tiles_ref[0])

    def finish(i, slot):
        to_row, to_col = products(
            tiles_ref.at[slot], v_ref[i - shift_by], v_ref[i + REACH - shift_by], listed_ref[i * STEPS + REACH]
        )
        acc_ref[i] += to_row
        acc_ref[i + REACH] += to_col

    def near_leaf(i, _):
        slot = (i - i0) * STEPS
        cols = cols_ref[i]
        center = center_ref[i]
        vi = v_ref[i - shift_by]

        def make(d):
            block = near_squares(cols, pts_ref[i + d - shift_by], center)
            make_tile(tiles_ref.at[slot + (1 + d)], block, d == 0)

        make(0)
        finish(jnp.maximum(i - 1, i0), slot)
        total = None
        for d in range(REACH):
            make(d + 1)
            to_row, to_col = products(
                tiles_ref.at[slot + (1 + d)], vi, v_ref[i + d - shift_by], listed_ref[i * STEPS + d]
            )
            total = to_row if total is None else total + to_row
            acc_ref[i + d] += to_col
        acc_ref[i] += total
        return 0

    def far_leaf(i, _):
        slot = (i - i0) * STEPS
        spread_rows(bc_ref, pts_ref[i - shift_by])

        def step(d, _):
            t_ref = tiles_ref.at[slot + (1 + d)]
            block = far_squares(bc_ref, pts_ref.at[i + d - shift_by])
            lax.cond(d == 0, lambda: make_tile(t_ref, block, True), lambda: make_tile(t_ref, block, False))

            @pl.when(d < REACH)
            def _():
                to_row, to_col = products(
                    t_ref, v_ref[i - shift_by], v_ref[i + d - shift_by], listed_ref[i * STEPS + d]
                )
                acc_ref[i] += to_row
                acc_ref[i + d] += to_col

            return 0

        @pl.when(i > i0)
        def _():
            finish(i - 1, slot)

        return lax.fori_loop(0, STEPS, step, 0)

    @pl.when(compact)
    def _():
        lax.fori_loop(i0, i1, near_leaf, 0)

    @pl.when(jnp.logical_not(compact))
    def _():
        lax.fori_loop(i0, i1, far_leaf, 0)

    finish(i1 - 1, (i1 - i0) * STEPS)
    if far:
        put_rows(rows_ref, acc_ref, leaf_dev, REACH)
    if last:
        put_rows(rows_ref, acc_ref, 0, leaf_dev, own_ref)


def clear_or_copy(acc_ref, prev_ref):
    acc_ref[...] = jnp.zeros_like(acc_ref) if prev_ref is None else prev_ref[...]


def weighted(acc_ref, field_ref, first, leaves):
    total = acc_ref[first] * field_ref[:, 0:W]
    for k in range(1, leaves):
        total += acc_ref[first + k] * field_ref[:, k * W : (k + 1) * W]
    return total


def apply_kernel(i0, i1, leaf_dev, last, listed_ref, tiles_ref, w_ref, *rest):
    rest = list(rest)
    if last:
        far_ref, extra_ref = rest.pop(0), rest.pop(0)
    prev_ref = rest.pop(0) if i0 else None
    acc_ref = rest.pop(0)
    dots_ref = rest.pop(0) if last else None
    v_ref = rest.pop(0)
    load_values(v_ref, w_ref, leaf_dev, 0)
    clear_or_copy(acc_ref, prev_ref)

    def one_leaf(i, _):
        slot = (i - i0) * STEPS
        vi = v_ref[i]
        total = None
        for d in range(STEPS):
            to_row, to_col = products(
                tiles_ref.at[slot + (1 + d)], vi, v_ref[i + d], listed_ref[i * STEPS + d]
            )
            total = to_row if total is None else total + to_row
            acc_ref[i + d] += to_col
        acc_ref[i] += total
        return 0

    lax.fori_loop(i0, i1, one_leaf, 0)
    if last:
        total = weighted(acc_ref, w_ref, 0, leaf_dev) + weighted(acc_ref, far_ref, leaf_dev, REACH)
        dots_ref[...] = (total + extra_ref[...]) * (1.0 / PEAK)


def edge_kernel(i0, leaf_dev, listed_ref, tiles_ref, w_ref, far_ref, prev_ref, acc_ref, send_ref, dots_ref, v_ref, part_ref):
    held = leaf_dev - i0
    load_values(v_ref, w_ref, leaf_dev, 0)
    clear_or_copy(part_ref, None)

    def one_leaf(i, _):
        slot = (i - i0) * STEPS
        vi = v_ref[i]
        for d in range(STEPS):
            part_ref[i - i0 + d] += product(
                tiles_ref.at[slot + (1 + d)], vi, listed_ref[i * STEPS + d], False
            )
        return 0

    lax.fori_loop(i0, leaf_dev, one_leaf, 0)
    dots_ref[...] = weighted(part_ref, w_ref.at[:, i0 * W :], 0, held) + weighted(part_ref, far_ref, held, REACH)
    acc_ref[...] = prev_ref[...]
    for k in range(held + REACH):
        acc_ref[i0 + k] += part_ref[k]
    put_rows(send_ref, acc_ref, leaf_dev, REACH)


def finish_kernel(
    i0, leaf_dev, listed_ref, tiles_hbm, w_ref, far_ref, prev_ref, back_ref, rows_ref, v_ref, acc_ref, tiles_ref, sems
):
    copies = []
    for k in range(leaf_dev - i0):
        at = pl.ds(k * STEPS, STEPS)
        copies.append(pltpu.make_async_copy(tiles_hbm.at[pl.ds(k * STEPS + 1, STEPS)], tiles_ref.at[at], sems.at[k]))
    copies[0].start()
    load_values(v_ref, w_ref.at[:, i0 * W :], leaf_dev - i0, 0)
    load_values(v_ref, far_ref, REACH, leaf_dev - i0)
    acc_ref[...] = prev_ref[...]
    copies[1].start()
    for k, copy in enumerate(copies):
        copy.wait()
        if k + 2 < len(copies):
            copies[k + 2].start()
        total = None
        for d in range(STEPS):
            to_row = product(tiles_ref.at[k * STEPS + d], v_ref[k + d], listed_ref[(i0 + k) * STEPS + d], True)
            total = to_row if total is None else total + to_row
        acc_ref[i0 + k] += total
    put_rows(rows_ref, acc_ref, 0, leaf_dev, w_ref)
    rows_ref[:, 0 : REACH * W] += back_ref[...]


VM = pl.BlockSpec(memory_space=pltpu.VMEM)
SM = pl.BlockSpec(memory_space=pltpu.SMEM)
HBM = pl.BlockSpec(memory_space=pltpu.HBM)
PARAMS = pltpu.CompilerParams(vmem_limit_bytes=8 << 20)


def prepare_call(pairs, count, base, coords, order, b):
    leaves = order.shape[0]
    n = b.shape[0]
    return pl.pallas_call(
        prepare_kernel,
        out_shape=(
            jax.ShapeDtypeStruct((pairs.shape[1], 16, HALF), jnp.bfloat16),
            jax.ShapeDtypeStruct((leaves, 8, W), jnp.float32),
            jax.ShapeDtypeStruct((leaves, W, 8 * GROUPS), jnp.bfloat16),
            jax.ShapeDtypeStruct((leaves, 2 * n, W), jnp.bfloat16),
            jax.ShapeDtypeStruct((leaves, 8, W), jnp.float32),
            jax.ShapeDtypeStruct((8, W), jnp.float32),
            jax.ShapeDtypeStruct((n + 3, REACH * W), jnp.float32),
        ),
        in_specs=[SM, SM, HBM, HBM, HBM, HBM],
        out_specs=(VM,) * 7,
        scratch_shapes=[
            pltpu.VMEM(pairs.shape, jnp.int32),
            pltpu.VMEM(coords.shape, jnp.float32),
            pltpu.VMEM(order.shape, jnp.int32),
            pltpu.VMEM(b.shape, jnp.float32),
            pltpu.SemaphoreType.DMA((4,)),
        ],
        compiler_params=PARAMS,
        name="prepare",
    )(count, base, *(pltpu.with_memory_space_constraint(x, pltpu.HBM) for x in (pairs, coords, order, b)))


def shapes_out(leaf_dev, n, far, last):
    acc = (leaf_dev + REACH, n, W)
    rows = (n, (leaf_dev if last else REACH) * W)
    f32 = jnp.float32
    if last:
        return [jax.ShapeDtypeStruct(rows, f32)], [pltpu.VMEM(acc, f32)]
    return [jax.ShapeDtypeStruct(acc, f32)] + ([jax.ShapeDtypeStruct(rows, f32)] if far else []), []


def evaluate_call(i0, i1, leaf_dev, n, prepared, far, own, prev):
    tiles = (i1 - i0) * STEPS
    last = own is not None
    ops = [*prepared, *far, *([own] if last else []), *([] if prev is None else [prev])]
    outs, held_acc = shapes_out(leaf_dev, n, bool(far), last)
    scratch = [*held_acc, pltpu.VMEM((W, 3 * HALF), jnp.float32)]
    if far:
        held = leaf_dev - i0 + REACH
        scratch += [pltpu.VMEM((held, 8, W), jnp.float32), pltpu.VMEM((held, 2 * n, W), jnp.bfloat16)]
    outs = [jax.ShapeDtypeStruct((tiles + 1, 4, W, HALF), jnp.bfloat16), *outs]
    return pl.pallas_call(
        functools.partial(evaluate_kernel, i0, i1, leaf_dev, last),
        out_shape=outs,
        in_specs=[VM] * len(ops),
        out_specs=[VM] * len(outs),
        scratch_shapes=scratch,
        compiler_params=PARAMS,
        cost_estimate=pl.CostEstimate(flops=tiles << 28, transcendentals=tiles << 17, bytes_accessed=tiles << 18),
        name=f"evaluate_{i0}",
    )(*ops)


def small_call(kernel, name, outs, scratch, tiles, ops, in_hbm=()):
    return pl.pallas_call(
        kernel,
        out_shape=[jax.ShapeDtypeStruct(shape, jnp.float32) for shape in outs],
        in_specs=[HBM if k in in_hbm else VM for k in range(len(ops))],
        out_specs=[VM] * len(outs),
        scratch_shapes=scratch,
        compiler_params=pltpu.CompilerParams(vmem_limit_bytes=14 << 20) if in_hbm else PARAMS,
        cost_estimate=pl.CostEstimate(flops=tiles.shape[0] << 27, transcendentals=0, bytes_accessed=tiles.size * 2),
        name=name,
    )(*[pltpu.with_memory_space_constraint(x, pltpu.HBM) if k in in_hbm else x for k, x in enumerate(ops)])


def apply_call(i0, i1, leaf_dev, n, listed, tiles, own, last, prev):
    acc = (leaf_dev + REACH, n, W)
    ops = [listed, tiles, own, *last, *([] if prev is None else [prev])]
    return small_call(
        functools.partial(apply_kernel, i0, i1, leaf_dev, bool(last)),
        f"apply_{i0}",
        [acc, (n, W)] if last else [acc],
        [pltpu.VMEM((leaf_dev, 2 * n, W), jnp.bfloat16)],
        tiles,
        ops,
    )


def edge_call(i0, leaf_dev, n, listed, tiles, own, far, prev):
    acc = (leaf_dev + REACH, n, W)
    return small_call(
        functools.partial(edge_kernel, i0, leaf_dev),
        "apply_edge",
        [acc, (n, REACH * W), (n, W)],
        [
            pltpu.VMEM((leaf_dev, 2 * n, W), jnp.bfloat16),
            pltpu.VMEM((leaf_dev - i0 + REACH, n, W), jnp.float32),
        ],
        tiles,
        [listed, tiles, own, far, prev],
    )


def finish_call(i0, leaf_dev, n, listed, tiles, own, far, prev, back):
    acc = (leaf_dev + REACH, n, W)
    return small_call(
        functools.partial(finish_kernel, i0, leaf_dev),
        "finish",
        [own.shape],
        [
            pltpu.VMEM((leaf_dev - i0 + REACH, 2 * n, W), jnp.bfloat16),
            pltpu.VMEM(acc, jnp.float32),
            pltpu.VMEM((tiles.shape[0] - 1, *tiles.shape[1:]), jnp.bfloat16),
            pltpu.SemaphoreType.DMA((leaf_dev - i0,)),
        ],
        tiles,
        [listed, tiles, own, far, prev, back],
        in_hbm=(1,),
    )[0]


def shift(value, by):
    length = lax.axis_size("leaf")
    return lax.ppermute(value, "leaf", [(i, i + by) for i in range(length) if 0 <= i + by < length])


def sum_over_leaf(value):
    length = lax.axis_size("leaf")
    value = value + lax.ppermute(value, "leaf", [(i, i ^ 1) for i in range(length)])
    copies = jnp.broadcast_to(value.reshape(-1), (length // 2, value.size))
    groups = [[i for i in range(length) if i % 2 == c] for c in range(2)]
    got = lax.all_to_all(
        copies, "leaf", split_axis=0, concat_axis=0, tiled=True, axis_index_groups=groups
    )
    return jnp.sum(got, axis=0).reshape(value.shape)


def body(coords, site_order, leaf_pairs, pair_count, probes):
    leaf_dev, width = site_order.shape
    n = probes.shape[0]
    edge = REACH * width
    base = (lax.axis_index("leaf") * leaf_dev).astype(jnp.int32).reshape(1)
    *prepared, packed = prepare_call(leaf_pairs, pair_count, base, coords, site_order, probes)
    far = shift(packed, -1)
    cut0, cut1 = leaf_dev - REACH - 5, leaf_dev - REACH
    evaluate = functools.partial(evaluate_call, leaf_dev=leaf_dev, n=n, prepared=prepared)
    tiles0, acc = evaluate(0, cut0, far=(), own=None, prev=None)
    tiles1, acc, send = evaluate(cut1, leaf_dev, far=(far,), own=None, prev=acc)
    back = shift(send, 1)
    tiles2, image = evaluate(cut0, cut1, far=(), own=probes, prev=acc)
    image = jnp.concatenate([image[:, :edge] + back, image[:, edge:]], axis=1)

    image_far = shift(image[:, :edge], -1)
    common = dict(leaf_dev=leaf_dev, n=n, listed=prepared[0], own=image)
    (acc,) = apply_call(0, cut0, tiles=tiles0, last=(), prev=None, **common)
    acc, send, edge_dots = edge_call(cut1, tiles=tiles1, far=image_far, prev=acc, **common)
    back = shift(send, 1)
    acc, dots = apply_call(cut0, cut1, tiles=tiles2, last=(image_far, edge_dots), prev=acc, **common)
    dots, back = lax.optimization_barrier((dots, back))
    square = jnp.sum(image * image, axis=1)
    sums = jnp.stack(
        [
            jnp.sum(probes * probes, axis=1),
            jnp.sum(probes * image, axis=1),
            square,
            jnp.sum(dots, axis=1) + NUGGET * square,
        ]
    )
    image2 = finish_call(cut1, tiles=tiles1, far=image_far, prev=acc, back=back, **common)
    rr, bw, ww, wz = sum_over_leaf(sums)
    alpha = rr / bw
    rr1 = rr - 2.0 * alpha * bw + alpha * alpha * ww
    beta = rr1 / rr
    g = 1.0 + beta
    curve = g * g * bw - 2.0 * g * alpha * ww + alpha * alpha * wz
    alpha1 = rr1 / curve
    c = lambda x: x[:, None]
    direction1 = c(g) * probes - c(alpha) * image
    image1 = c(g) * image - c(alpha) * image2
    solution = c(alpha) * probes + c(alpha1) * direction1
    residual = probes - c(alpha) * image - c(alpha1) * image1
    return solution, residual


def solution(mesh):
    in_specs = (P(None, "leaf"), P("leaf", None), P(None, "leaf"), P("leaf"), P("probe", "leaf"))
    out_specs = (P("probe", "leaf"), P("probe", "leaf"))
    return jax.shard_map(body, mesh=mesh, in_specs=in_specs, out_specs=out_specs, check_vma=False)
```

```python
import functools
import math

import jax
import jax.numpy as jnp
from jax import lax
from jax.experimental import pallas as pl
from jax.experimental.pallas import tpu as pltpu
from jax.sharding import PartitionSpec as P

REACH = 5
STEPS = REACH + 1
UNIT = 0.025
LENGTH = 0.12
NUGGET = 0.5
W = 256
TAPER = REACH * UNIT
DECAY = math.sqrt(3.0) * TAPER / LENGTH
LOG2E = math.log2(math.e)
CHUNK = 16
HALF = W // 2
FLOOR_INV = 1e18
KAPPA = DECAY * LOG2E
PEAK = KAPPA**6 / (4.0 * DECAY) * 2.0**KAPPA
SCALE = KAPPA / TAPER
COMPACT = 20.0 * KAPPA * KAPPA
RANGE = 1e15
TINY = 1e-12
GROUPS = 6


def split2(x):
    hi = x.astype(jnp.bfloat16)
    lo = (x - hi.astype(jnp.float32)).astype(jnp.bfloat16)
    return hi, lo


def split3(x):
    hi = x.astype(jnp.bfloat16)
    rest = x - hi.astype(jnp.float32)
    mid = rest.astype(jnp.bfloat16)
    lo = (rest - mid.astype(jnp.float32)).astype(jnp.bfloat16)
    return hi, mid, lo


def load_values(v_ref, src_ref, leaves, first):
    n = v_ref.shape[1] // 2
    for k in range(leaves):
        hi, lo = split2(src_ref[0:n, k * W : (k + 1) * W])
        v_ref[first + k] = jnp.concatenate([hi, lo], axis=0)


def split_rows(point, center, top, weight):
    x = (point - center) * SCALE
    sq = x * x
    sq = sq[0:1] + sq[1:2] + sq[2:3]
    row = lax.broadcasted_iota(jnp.int32, x.shape, 0)
    x = jnp.where(top, x * weight, jnp.where(row == 3, sq, 0.0))
    hi = x.astype(jnp.bfloat16).astype(jnp.float32)
    rest = x - hi
    mid = rest.astype(jnp.bfloat16).astype(jnp.float32)
    return hi, mid, rest - mid


def prepare_kernel(
    count_ref, base_ref, pairs_hbm, coords_hbm, order_hbm, b_hbm,
    listed_ref, pts_ref, cols_ref, v_ref, center_ref, wide_ref, edge_ref,
    pairs_ref, coords_ref, order_ref, b_ref, sems,
):
    copies = [
        pltpu.make_async_copy(pairs_hbm, pairs_ref, sems.at[0]),
        pltpu.make_async_copy(coords_hbm, coords_ref, sems.at[1]),
        pltpu.make_async_copy(order_hbm, order_ref, sems.at[2]),
        pltpu.make_async_copy(b_hbm, b_ref, sems.at[3]),
    ]
    for copy in copies:
        copy.start()
    copies[0].wait()
    slots = pairs_ref.shape[1]
    row = pairs_ref[0:1, :]
    place = (row - base_ref[0]) * STEPS + pairs_ref[1:2, :] - row
    live = lax.broadcasted_iota(jnp.int32, (1, slots), 1) < count_ref[0]
    place = jnp.where(live, place, -1)
    hit = lax.broadcasted_iota(jnp.int32, (slots, slots), 0) == place
    found = jnp.sum(hit.astype(jnp.float32), axis=1, keepdims=True)
    listed_ref[...] = jnp.broadcast_to(found.astype(jnp.bfloat16)[:, :, None], listed_ref.shape)
    for copy in copies[1:]:
        copy.wait()
    leaves = order_ref.shape[0]
    n = b_ref.shape[0]
    sub = lax.broadcasted_iota(jnp.int32, (W, W), 0).astype(jnp.float32).astype(jnp.bfloat16)
    one, zero = jnp.ones((W, W), jnp.bfloat16), jnp.zeros((W, W), jnp.bfloat16)
    dot = functools.partial(jnp.dot, preferred_element_type=jnp.float32)
    top = lax.broadcasted_iota(jnp.int32, (8, W), 0) < 3
    pad = jnp.zeros((5, W), jnp.float32)
    wide = jnp.zeros((8, W), jnp.float32)
    for k in range(leaves):
        at = slice(k * W, (k + 1) * W)
        order = order_ref[k : k + 1, :].astype(jnp.float32).astype(jnp.bfloat16)
        sel = jnp.where(sub == jnp.broadcast_to(order, (W, W)), one, zero)
        raw = jnp.concatenate([coords_ref[:, at], pad], axis=0)
        parts = dot(jnp.concatenate(split3(raw), axis=0), sel)
        point = parts[0:8] + parts[8:16] + parts[16:24]
        got = point[0:3]
        center = jnp.broadcast_to(jnp.sum(point, axis=1, keepdims=True) * (1.0 / W), (8, W))
        pts_ref[k] = point
        center_ref[k] = center
        hi, mid, lo = split_rows(point, center, top, 1.0)
        square = jnp.where(top, 0.0, hi + mid + lo)
        first = center if k == 0 else first
        far_off = jnp.abs(point - first) * (SCALE * COMPACT / RANGE)
        wide = jnp.maximum(wide, jnp.maximum(square, far_off))
        unit = jnp.where(lax.broadcasted_iota(jnp.int32, (8, W), 0) == 3, 1.0, 0.0)
        stack = [hi, jnp.where(top, hi, mid), jnp.where(top, hi, lo)]
        stack += [jnp.where(top, mid, unit), jnp.where(top, mid, unit), jnp.where(top, lo, unit)]
        cols_ref[k] = jnp.transpose(jnp.concatenate(stack, axis=0)).astype(jnp.bfloat16)
        if k < REACH:
            edge_ref[0:n, at] = b_ref[:, at]
            edge_ref[n : n + 3, at] = got
    wide_ref[...] = wide
    load_values(v_ref, b_ref, leaves, 0)


def spread_rows(bc_ref, points):
    cols = jnp.transpose(points)
    for c in range(3):
        bc_ref[:, c * HALF : (c + 1) * HALF] = jnp.broadcast_to(cols[:, c : c + 1], (W, HALF))


def far_squares(bc_ref, other):
    def block(rows, h):
        u = None
        for c in range(3):
            b = jnp.broadcast_to(other[c : c + 1, h * HALF : (h + 1) * HALF], (CHUNK, HALF))
            d = bc_ref[rows, c * HALF : (c + 1) * HALF] - b
            u = d * d if u is None else u + d * d
        return u * (SCALE * SCALE)

    return block


def near_squares(cols, other, center):
    top = lax.broadcasted_iota(jnp.int32, (8, W), 0) < 3
    one = jnp.where(lax.broadcasted_iota(jnp.int32, (8, W), 0) == 3, 1.0, 0.0)
    hi, mid, lo = split_rows(other, center, top, -2.0)
    stack = [jnp.where(top, hi, one), jnp.where(top, mid, one), jnp.where(top, lo, one)]
    stack += [hi, mid, jnp.where(top, hi, lo)]
    rows = jnp.concatenate(stack, axis=0).astype(jnp.bfloat16)
    all_u = jnp.dot(cols, rows, preferred_element_type=jnp.float32)
    return lambda rows, h: all_u[rows, h * HALF : (h + 1) * HALF]


def make_tile(t_ref, block, same):
    for k in range(W // CHUNK):
        rows = slice(k * CHUNK, (k + 1) * CHUNK)
        lower = k * CHUNK >= HALF
        for h in range(2):
            if same and lower and h == 0:
                t_ref[0, rows, :] = jnp.zeros((CHUNK, HALF), jnp.bfloat16)
                t_ref[2, rows, :] = jnp.zeros((CHUNK, HALF), jnp.bfloat16)
                continue
            u = jnp.minimum(jnp.maximum(block(rows, h), TINY), KAPPA * KAPPA)
            q = u * lax.rsqrt(u)
            t = KAPPA - q
            e = jnp.exp2(t)
            t = t * t
            t = t * t
            x = ((q + KAPPA / 4.0) * (q + KAPPA / DECAY)) * (t * e)
            if same and lower == bool(h):
                x = x * 0.5
            hi, lo = split2(x)
            t_ref[h, rows, :] = hi
            t_ref[2 + h, rows, :] = lo


def product(t_ref, v, listed, transposed):
    hi = jnp.concatenate([t_ref[0], t_ref[1]], axis=1)
    lo = jnp.concatenate([t_ref[2], t_ref[3]], axis=1)
    dims = (((1,), (1 if transposed else 0,)), ((), ()))
    dot = functools.partial(lax.dot_general, dimension_numbers=dims, preferred_element_type=jnp.float32)
    n = v.shape[0] // 2
    keep = jnp.concatenate([listed, listed], axis=1)
    v = v * jnp.concatenate([keep, keep], axis=0)
    p = dot(v, hi)
    return p[:n] + p[n:] + dot(v[:n], lo)


def products(t_ref, vi, vj, listed):
    return product(t_ref, vj, listed, True), product(t_ref, vi, listed, False)


def put_rows(out_ref, acc_ref, first, leaves, own_ref=None):
    for k in range(leaves):
        at = slice(k * W, (k + 1) * W)
        x = acc_ref[first + k] * (1.0 / PEAK)
        out_ref[:, at] = x if own_ref is None else x + NUGGET * own_ref[:, at]


def evaluate_kernel(i0, i1, leaf_dev, last, listed_ref, pts_ref, cols_ref, v_ref, center_ref, wide_ref, *rest):
    rest = list(rest)
    far = i1 + REACH > leaf_dev
    shift_by = 0
    edge_ref = rest.pop(0) if far else None
    own_ref = rest.pop(0) if last else None
    prev_ref = rest.pop(0) if i0 else None
    tiles_ref = rest.pop(0)
    acc_ref = rest.pop(1 if last else 0)
    rows_ref = rest.pop(0) if last or far else None
    bc_ref = rest.pop(0)
    compact = jnp.max(wide_ref[...]) <= COMPACT
    if far:
        pts_all, v_all = rest
        n = v_ref.shape[1] // 2
        own = leaf_dev - i0
        pts_all[0:own] = pts_ref[i0:leaf_dev]
        v_all[0:own] = v_ref[i0:leaf_dev]
        first = center_ref[leaf_dev - 1, 0:3, :]
        pts_all[own:] = jnp.zeros_like(pts_all[own:])
        for k in range(REACH):
            got = edge_ref[n : n + 3, k * W : (k + 1) * W]
            pts_all[own + k, 0:3, :] = got
            far_off = jnp.abs(got - first) * (SCALE * COMPACT / RANGE)
            wide = far_off if k == 0 else jnp.maximum(wide, far_off)
        load_values(v_all, edge_ref, REACH, own)
        compact = compact & (jnp.max(wide) <= COMPACT)
        pts_ref, v_ref = pts_all, v_all
        shift_by = i0
    if i0:
        acc_ref[...] = prev_ref[...]
    else:
        acc_ref[...] = jnp.zeros_like(acc_ref)
    tiles_ref[0] = jnp.zeros_like(tiles_ref[0])

    def finish(i, slot):
        to_row, to_col = products(
            tiles_ref.at[slot], v_ref[i - shift_by], v_ref[i + REACH - shift_by], listed_ref[i * STEPS + REACH]
        )
        acc_ref[i] += to_row
        acc_ref[i + REACH] += to_col

    def near_leaf(i, _):
        slot = (i - i0) * STEPS
        cols = cols_ref[i]
        center = center_ref[i]
        vi = v_ref[i - shift_by]

        def make(d):
            block = near_squares(cols, pts_ref[i + d - shift_by], center)
            make_tile(tiles_ref.at[slot + (1 + d)], block, d == 0)

        make(0)
        finish(jnp.maximum(i - 1, i0), slot)
        total = None
        for d in range(REACH):
            make(d + 1)
            to_row, to_col = products(
                tiles_ref.at[slot + (1 + d)], vi, v_ref[i + d - shift_by], listed_ref[i * STEPS + d]
            )
            total = to_row if total is None else total + to_row
            acc_ref[i + d] += to_col
        acc_ref[i] += total
        return 0

    def far_leaf(i, _):
        slot = (i - i0) * STEPS
        spread_rows(bc_ref, pts_ref[i - shift_by])

        def step(d, _):
            t_ref = tiles_ref.at[slot + (1 + d)]
            block = far_squares(bc_ref, pts_ref.at[i + d - shift_by])
            lax.cond(d == 0, lambda: make_tile(t_ref, block, True), lambda: make_tile(t_ref, block, False))

            @pl.when(d < REACH)
            def _():
                to_row, to_col = products(
                    t_ref, v_ref[i - shift_by], v_ref[i + d - shift_by], listed_ref[i * STEPS + d]
                )
                acc_ref[i] += to_row
                acc_ref[i + d] += to_col

            return 0

        @pl.when(i > i0)
        def _():
            finish(i - 1, slot)

        return lax.fori_loop(0, STEPS, step, 0)

    @pl.when(compact)
    def _():
        lax.fori_loop(i0, i1, near_leaf, 0)

    @pl.when(jnp.logical_not(compact))
    def _():
        lax.fori_loop(i0, i1, far_leaf, 0)

    finish(i1 - 1, (i1 - i0) * STEPS)
    if far:
        put_rows(rows_ref, acc_ref, leaf_dev, REACH)
    if last:
        put_rows(rows_ref, acc_ref, 0, leaf_dev, own_ref)


def clear_or_copy(acc_ref, prev_ref):
    acc_ref[...] = jnp.zeros_like(acc_ref) if prev_ref is None else prev_ref[...]


def weighted(acc_ref, field_ref, first, leaves):
    total = acc_ref[first] * field_ref[:, 0:W]
    for k in range(1, leaves):
        total += acc_ref[first + k] * field_ref[:, k * W : (k + 1) * W]
    return total


def apply_kernel(i0, i1, leaf_dev, last, listed_ref, tiles_ref, w_ref, *rest):
    rest = list(rest)
    if last:
        far_ref, extra_ref = rest.pop(0), rest.pop(0)
    prev_ref = rest.pop(0) if i0 else None
    acc_ref = rest.pop(0)
    dots_ref = rest.pop(0) if last else None
    v_ref = rest.pop(0)
    load_values(v_ref, w_ref, leaf_dev, 0)
    clear_or_copy(acc_ref, prev_ref)

    def one_leaf(i, _):
        slot = (i - i0) * STEPS
        vi = v_ref[i]
        total = None
        for d in range(STEPS):
            to_row, to_col = products(
                tiles_ref.at[slot + (1 + d)], vi, v_ref[i + d], listed_ref[i * STEPS + d]
            )
            total = to_row if total is None else total + to_row
            acc_ref[i + d] += to_col
        acc_ref[i] += total
        return 0

    lax.fori_loop(i0, i1, one_leaf, 0)
    if last:
        total = weighted(acc_ref, w_ref, 0, leaf_dev) + weighted(acc_ref, far_ref, leaf_dev, REACH)
        dots_ref[...] = (total + extra_ref[...]) * (1.0 / PEAK)


def edge_kernel(i0, leaf_dev, listed_ref, tiles_ref, w_ref, far_ref, prev_ref, acc_ref, send_ref, dots_ref, v_ref, part_ref):
    held = leaf_dev - i0
    load_values(v_ref, w_ref, leaf_dev, 0)
    clear_or_copy(part_ref, None)

    def one_leaf(i, _):
        slot = (i - i0) * STEPS
        vi = v_ref[i]
        for d in range(STEPS):
            part_ref[i - i0 + d] += product(
                tiles_ref.at[slot + (1 + d)], vi, listed_ref[i * STEPS + d], False
            )
        return 0

    lax.fori_loop(i0, leaf_dev, one_leaf, 0)
    dots_ref[...] = weighted(part_ref, w_ref.at[:, i0 * W :], 0, held) + weighted(part_ref, far_ref, held, REACH)
    acc_ref[...] = prev_ref[...]
    for k in range(held + REACH):
        acc_ref[i0 + k] += part_ref[k]
    put_rows(send_ref, acc_ref, leaf_dev, REACH)


def finish_kernel(
    i0, leaf_dev, listed_ref, tiles_hbm, w_ref, far_ref, prev_ref, rows_ref, v_ref, acc_ref, tiles_ref, sems
):
    copies = []
    for k in range(leaf_dev - i0):
        at = pl.ds(k * STEPS, STEPS)
        copies.append(pltpu.make_async_copy(tiles_hbm.at[pl.ds(k * STEPS + 1, STEPS)], tiles_ref.at[at], sems.at[k]))
    copies[0].start()
    load_values(v_ref, w_ref.at[:, i0 * W :], leaf_dev - i0, 0)
    load_values(v_ref, far_ref, REACH, leaf_dev - i0)
    acc_ref[...] = prev_ref[...]
    copies[1].start()
    for k, copy in enumerate(copies):
        copy.wait()
        if k + 2 < len(copies):
            copies[k + 2].start()
        total = None
        for d in range(STEPS):
            to_row = product(tiles_ref.at[k * STEPS + d], v_ref[k + d], listed_ref[(i0 + k) * STEPS + d], True)
            total = to_row if total is None else total + to_row
        acc_ref[i0 + k] += total
    put_rows(rows_ref, acc_ref, 0, leaf_dev, w_ref)


VM = pl.BlockSpec(memory_space=pltpu.VMEM)
SM = pl.BlockSpec(memory_space=pltpu.SMEM)
HBM = pl.BlockSpec(memory_space=pltpu.HBM)
PARAMS = pltpu.CompilerParams(vmem_limit_bytes=8 << 20)


def prepare_call(pairs, count, base, coords, order, b):
    leaves = order.shape[0]
    n = b.shape[0]
    return pl.pallas_call(
        prepare_kernel,
        out_shape=(
            jax.ShapeDtypeStruct((pairs.shape[1], 16, HALF), jnp.bfloat16),
            jax.ShapeDtypeStruct((leaves, 8, W), jnp.float32),
            jax.ShapeDtypeStruct((leaves, W, 8 * GROUPS), jnp.bfloat16),
            jax.ShapeDtypeStruct((leaves, 2 * n, W), jnp.bfloat16),
            jax.ShapeDtypeStruct((leaves, 8, W), jnp.float32),
            jax.ShapeDtypeStruct((8, W), jnp.float32),
            jax.ShapeDtypeStruct((n + 3, REACH * W), jnp.float32),
        ),
        in_specs=[SM, SM, HBM, HBM, HBM, HBM],
        out_specs=(VM,) * 7,
        scratch_shapes=[
            pltpu.VMEM(pairs.shape, jnp.int32),
            pltpu.VMEM(coords.shape, jnp.float32),
            pltpu.VMEM(order.shape, jnp.int32),
            pltpu.VMEM(b.shape, jnp.float32),
            pltpu.SemaphoreType.DMA((4,)),
        ],
        compiler_params=PARAMS,
        name="prepare",
    )(count, base, *(pltpu.with_memory_space_constraint(x, pltpu.HBM) for x in (pairs, coords, order, b)))


def shapes_out(leaf_dev, n, far, last):
    acc = (leaf_dev + REACH, n, W)
    rows = (n, (leaf_dev if last else REACH) * W)
    f32 = jnp.float32
    if last:
        return [jax.ShapeDtypeStruct(rows, f32)], [pltpu.VMEM(acc, f32)]
    return [jax.ShapeDtypeStruct(acc, f32)] + ([jax.ShapeDtypeStruct(rows, f32)] if far else []), []


def evaluate_call(i0, i1, leaf_dev, n, prepared, far, own, prev):
    tiles = (i1 - i0) * STEPS
    last = own is not None
    ops = [*prepared, *far, *([own] if last else []), *([] if prev is None else [prev])]
    outs, held_acc = shapes_out(leaf_dev, n, bool(far), last)
    scratch = [*held_acc, pltpu.VMEM((W, 3 * HALF), jnp.float32)]
    if far:
        held = leaf_dev - i0 + REACH
        scratch += [pltpu.VMEM((held, 8, W), jnp.float32), pltpu.VMEM((held, 2 * n, W), jnp.bfloat16)]
    outs = [jax.ShapeDtypeStruct((tiles + 1, 4, W, HALF), jnp.bfloat16), *outs]
    return pl.pallas_call(
        functools.partial(evaluate_kernel, i0, i1, leaf_dev, last),
        out_shape=outs,
        in_specs=[VM] * len(ops),
        out_specs=[VM] * len(outs),
        scratch_shapes=scratch,
        compiler_params=PARAMS,
        cost_estimate=pl.CostEstimate(flops=tiles << 28, transcendentals=tiles << 17, bytes_accessed=tiles << 18),
        name=f"evaluate_{i0}",
    )(*ops)


def small_call(kernel, name, outs, scratch, tiles, ops, in_hbm=()):
    return pl.pallas_call(
        kernel,
        out_shape=[jax.ShapeDtypeStruct(shape, jnp.float32) for shape in outs],
        in_specs=[HBM if k in in_hbm else VM for k in range(len(ops))],
        out_specs=[VM] * len(outs),
        scratch_shapes=scratch,
        compiler_params=pltpu.CompilerParams(vmem_limit_bytes=14 << 20) if in_hbm else PARAMS,
        cost_estimate=pl.CostEstimate(flops=tiles.shape[0] << 27, transcendentals=0, bytes_accessed=tiles.size * 2),
        name=name,
    )(*[pltpu.with_memory_space_constraint(x, pltpu.HBM) if k in in_hbm else x for k, x in enumerate(ops)])


def apply_call(i0, i1, leaf_dev, n, listed, tiles, own, last, prev):
    acc = (leaf_dev + REACH, n, W)
    ops = [listed, tiles, own, *last, *([] if prev is None else [prev])]
    return small_call(
        functools.partial(apply_kernel, i0, i1, leaf_dev, bool(last)),
        f"apply_{i0}",
        [acc, (n, W)] if last else [acc],
        [pltpu.VMEM((leaf_dev, 2 * n, W), jnp.bfloat16)],
        tiles,
        ops,
    )


def edge_call(i0, leaf_dev, n, listed, tiles, own, far, prev):
    acc = (leaf_dev + REACH, n, W)
    return small_call(
        functools.partial(edge_kernel, i0, leaf_dev),
        "apply_edge",
        [acc, (n, REACH * W), (n, W)],
        [
            pltpu.VMEM((leaf_dev, 2 * n, W), jnp.bfloat16),
            pltpu.VMEM((leaf_dev - i0 + REACH, n, W), jnp.float32),
        ],
        tiles,
        [listed, tiles, own, far, prev],
    )


def finish_call(i0, leaf_dev, n, listed, tiles, own, far, prev):
    acc = (leaf_dev + REACH, n, W)
    return small_call(
        functools.partial(finish_kernel, i0, leaf_dev),
        "finish",
        [own.shape],
        [
            pltpu.VMEM((leaf_dev - i0 + REACH, 2 * n, W), jnp.bfloat16),
            pltpu.VMEM(acc, jnp.float32),
            pltpu.VMEM((tiles.shape[0] - 1, *tiles.shape[1:]), jnp.bfloat16),
            pltpu.SemaphoreType.DMA((leaf_dev - i0,)),
        ],
        tiles,
        [listed, tiles, own, far, prev],
        in_hbm=(1,),
    )[0]


def shift(value, by):
    length = lax.axis_size("leaf")
    return lax.ppermute(value, "leaf", [(i, i + by) for i in range(length) if 0 <= i + by < length])


def sum_over_leaf(value):
    length = lax.axis_size("leaf")
    value = value + lax.ppermute(value, "leaf", [(i, i ^ 1) for i in range(length)])
    copies = jnp.broadcast_to(value.reshape(-1), (length // 2, value.size))
    groups = [[i for i in range(length) if i % 2 == c] for c in range(2)]
    got = lax.all_to_all(
        copies, "leaf", split_axis=0, concat_axis=0, tiled=True, axis_index_groups=groups
    )
    return jnp.sum(got, axis=0).reshape(value.shape)


def body(coords, site_order, leaf_pairs, pair_count, probes):
    leaf_dev, width = site_order.shape
    n = probes.shape[0]
    edge = REACH * width
    base = (lax.axis_index("leaf") * leaf_dev).astype(jnp.int32).reshape(1)
    *prepared, packed = prepare_call(leaf_pairs, pair_count, base, coords, site_order, probes)
    far = shift(packed, -1)
    cut0, cut1 = leaf_dev - REACH - 5, leaf_dev - REACH
    evaluate = functools.partial(evaluate_call, leaf_dev=leaf_dev, n=n, prepared=prepared)
    tiles0, acc = evaluate(0, cut0, far=(), own=None, prev=None)
    tiles1, acc, send = evaluate(cut1, leaf_dev, far=(far,), own=None, prev=acc)
    back = shift(send, 1)
    tiles2, image = evaluate(cut0, cut1, far=(), own=probes, prev=acc)
    image = jnp.concatenate([image[:, :edge] + back, image[:, edge:]], axis=1)

    image_far = shift(image[:, :edge], -1)
    common = dict(leaf_dev=leaf_dev, n=n, listed=prepared[0], own=image)
    (acc,) = apply_call(0, cut0, tiles=tiles0, last=(), prev=None, **common)
    acc, send, edge_dots = edge_call(cut1, tiles=tiles1, far=image_far, prev=acc, **common)
    back = shift(send, 1)
    acc, dots = apply_call(cut0, cut1, tiles=tiles2, last=(image_far, edge_dots), prev=acc, **common)
    square = jnp.sum(image * image, axis=1)
    sums = jnp.stack(
        [
            jnp.sum(probes * probes, axis=1),
            jnp.sum(probes * image, axis=1),
            square,
            jnp.sum(dots, axis=1) + NUGGET * square,
        ]
    )
    image2 = finish_call(cut1, tiles=tiles1, far=image_far, prev=acc, **common)
    image2 = jnp.concatenate([image2[:, :edge] + back, image2[:, edge:]], axis=1)
    rr, bw, ww, wz = sum_over_leaf(sums)
    alpha = rr / bw
    rr1 = rr - 2.0 * alpha * bw + alpha * alpha * ww
    beta = rr1 / rr
    g = 1.0 + beta
    curve = g * g * bw - 2.0 * g * alpha * ww + alpha * alpha * wz
    alpha1 = rr1 / curve
    c = lambda x: x[:, None]
    direction1 = c(g) * probes - c(alpha) * image
    image1 = c(g) * image - c(alpha) * image2
    solution = c(alpha) * probes + c(alpha1) * direction1
    residual = probes - c(alpha) * image - c(alpha1) * image1
    return solution, residual


def solution(mesh):
    in_specs = (P(None, "leaf"), P("leaf", None), P(None, "leaf"), P("leaf"), P("probe", "leaf"))
    out_specs = (P("probe", "leaf"), P("probe", "leaf"))
    return jax.shard_map(body, mesh=mesh, in_specs=in_specs, out_specs=out_specs, check_vma=False)
```

```python
import functools
import math

import jax
import jax.numpy as jnp
from jax import lax
from jax.experimental import pallas as pl
from jax.experimental.pallas import tpu as pltpu
from jax.sharding import PartitionSpec as P

REACH = 5
STEPS = REACH + 1
UNIT = 0.025
LENGTH = 0.12
NUGGET = 0.5
W = 256
TAPER = REACH * UNIT
DECAY = math.sqrt(3.0) * TAPER / LENGTH
LOG2E = math.log2(math.e)
CHUNK = 16
HALF = W // 2
FLOOR_INV = 1e18
KAPPA = DECAY * LOG2E
PEAK = KAPPA**6 / (4.0 * DECAY) * 2.0**KAPPA
SCALE = KAPPA / TAPER
COMPACT = 20.0 * KAPPA * KAPPA
RANGE = 1e15
TINY = 1e-12
GROUPS = 6


def split2(x):
    hi = x.astype(jnp.bfloat16)
    lo = (x - hi.astype(jnp.float32)).astype(jnp.bfloat16)
    return hi, lo


def split3(x):
    hi = x.astype(jnp.bfloat16)
    rest = x - hi.astype(jnp.float32)
    mid = rest.astype(jnp.bfloat16)
    lo = (rest - mid.astype(jnp.float32)).astype(jnp.bfloat16)
    return hi, mid, lo


def load_values(v_ref, src_ref, leaves, first):
    n = v_ref.shape[1] // 2
    for k in range(leaves):
        hi, lo = split2(src_ref[0:n, k * W : (k + 1) * W])
        v_ref[first + k] = jnp.concatenate([hi, lo], axis=0)


def split_rows(point, center, top, weight):
    x = (point - center) * SCALE
    sq = x * x
    sq = sq[0:1] + sq[1:2] + sq[2:3]
    row = lax.broadcasted_iota(jnp.int32, x.shape, 0)
    x = jnp.where(top, x * weight, jnp.where(row == 3, sq, 0.0))
    hi = x.astype(jnp.bfloat16).astype(jnp.float32)
    rest = x - hi
    mid = rest.astype(jnp.bfloat16).astype(jnp.float32)
    return hi, mid, rest - mid


def prepare_kernel(
    count_ref, base_ref, pairs_hbm, coords_hbm, order_hbm, b_hbm,
    listed_ref, pts_ref, cols_ref, v_ref, center_ref, wide_ref, edge_ref,
    pairs_ref, coords_ref, order_ref, b_ref, sems,
):
    copies = [
        pltpu.make_async_copy(pairs_hbm, pairs_ref, sems.at[0]),
        pltpu.make_async_copy(coords_hbm, coords_ref, sems.at[1]),
        pltpu.make_async_copy(order_hbm, order_ref, sems.at[2]),
        pltpu.make_async_copy(b_hbm, b_ref, sems.at[3]),
    ]
    for copy in copies:
        copy.start()
    copies[0].wait()
    slots = pairs_ref.shape[1]
    row = pairs_ref[0:1, :]
    place = (row - base_ref[0]) * STEPS + pairs_ref[1:2, :] - row
    live = lax.broadcasted_iota(jnp.int32, (1, slots), 1) < count_ref[0]
    place = jnp.where(live, place, -1)
    hit = lax.broadcasted_iota(jnp.int32, (slots, slots), 0) == place
    found = jnp.sum(hit.astype(jnp.float32), axis=1, keepdims=True)
    listed_ref[...] = jnp.broadcast_to(found.astype(jnp.bfloat16)[:, :, None], listed_ref.shape)
    for copy in copies[1:]:
        copy.wait()
    leaves = order_ref.shape[0]
    n = b_ref.shape[0]
    sub = lax.broadcasted_iota(jnp.int32, (W, W), 0).astype(jnp.float32).astype(jnp.bfloat16)
    one, zero = jnp.ones((W, W), jnp.bfloat16), jnp.zeros((W, W), jnp.bfloat16)
    dot = functools.partial(jnp.dot, preferred_element_type=jnp.float32)
    top = lax.broadcasted_iota(jnp.int32, (8, W), 0) < 3
    pad = jnp.zeros((5, W), jnp.float32)
    wide = jnp.zeros((8, W), jnp.float32)
    for k in range(leaves):
        at = slice(k * W, (k + 1) * W)
        order = order_ref[k : k + 1, :].astype(jnp.float32).astype(jnp.bfloat16)
        sel = jnp.where(sub == jnp.broadcast_to(order, (W, W)), one, zero)
        raw = jnp.concatenate([coords_ref[:, at], pad], axis=0)
        parts = dot(jnp.concatenate(split3(raw), axis=0), sel)
        point = parts[0:8] + parts[8:16] + parts[16:24]
        got = point[0:3]
        center = jnp.broadcast_to(jnp.sum(point, axis=1, keepdims=True) * (1.0 / W), (8, W))
        pts_ref[k] = point
        center_ref[k] = center
        hi, mid, lo = split_rows(point, center, top, 1.0)
        square = jnp.where(top, 0.0, hi + mid + lo)
        first = center if k == 0 else first
        far_off = jnp.abs(point - first) * (SCALE * COMPACT / RANGE)
        wide = jnp.maximum(wide, jnp.maximum(square, far_off))
        unit = jnp.where(lax.broadcasted_iota(jnp.int32, (8, W), 0) == 3, 1.0, 0.0)
        stack = [hi, jnp.where(top, hi, mid), jnp.where(top, hi, lo)]
        stack += [jnp.where(top, mid, unit), jnp.where(top, mid, unit), jnp.where(top, lo, unit)]
        cols_ref[k] = jnp.transpose(jnp.concatenate(stack, axis=0)).astype(jnp.bfloat16)
        if k < REACH:
            edge_ref[0:n, at] = b_ref[:, at]
            edge_ref[n : n + 3, at] = got
    wide_ref[...] = wide
    load_values(v_ref, b_ref, leaves, 0)


def spread_rows(bc_ref, points):
    cols = jnp.transpose(points)
    for c in range(3):
        bc_ref[:, c * HALF : (c + 1) * HALF] = jnp.broadcast_to(cols[:, c : c + 1], (W, HALF))


def far_squares(bc_ref, other):
    def block(rows, h):
        u = None
        for c in range(3):
            b = jnp.broadcast_to(other[c : c + 1, h * HALF : (h + 1) * HALF], (CHUNK, HALF))
            d = bc_ref[rows, c * HALF : (c + 1) * HALF] - b
            u = d * d if u is None else u + d * d
        return u * (SCALE * SCALE)

    return block


def near_squares(cols, other, center):
    top = lax.broadcasted_iota(jnp.int32, (8, W), 0) < 3
    one = jnp.where(lax.broadcasted_iota(jnp.int32, (8, W), 0) == 3, 1.0, 0.0)
    hi, mid, lo = split_rows(other, center, top, -2.0)
    stack = [jnp.where(top, hi, one), jnp.where(top, mid, one), jnp.where(top, lo, one)]
    stack += [hi, mid, jnp.where(top, hi, lo)]
    rows = jnp.concatenate(stack, axis=0).astype(jnp.bfloat16)
    all_u = jnp.dot(cols, rows, preferred_element_type=jnp.float32)
    return lambda rows, h: all_u[rows, h * HALF : (h + 1) * HALF]


def make_tile(t_ref, block, same):
    for k in range(W // CHUNK):
        rows = slice(k * CHUNK, (k + 1) * CHUNK)
        lower = k * CHUNK >= HALF
        for h in range(2):
            if same and lower and h == 0:
                t_ref[0, rows, :] = jnp.zeros((CHUNK, HALF), jnp.bfloat16)
                t_ref[2, rows, :] = jnp.zeros((CHUNK, HALF), jnp.bfloat16)
                continue
            u = jnp.minimum(jnp.maximum(block(rows, h), TINY), KAPPA * KAPPA)
            q = u * lax.rsqrt(u)
            t = KAPPA - q
            e = jnp.exp2(t)
            t = t * t
            t = t * t
            x = ((q + KAPPA / 4.0) * (q + KAPPA / DECAY)) * (t * e)
            if same and lower == bool(h):
                x = x * 0.5
            hi, lo = split2(x)
            t_ref[h, rows, :] = hi
            t_ref[2 + h, rows, :] = lo


def product(t_ref, v, listed, transposed):
    hi = jnp.concatenate([t_ref[0], t_ref[1]], axis=1)
    lo = jnp.concatenate([t_ref[2], t_ref[3]], axis=1)
    dims = (((1,), (1 if transposed else 0,)), ((), ()))
    dot = functools.partial(lax.dot_general, dimension_numbers=dims, preferred_element_type=jnp.float32)
    n = v.shape[0] // 2
    keep = jnp.concatenate([listed, listed], axis=1)
    v = v * jnp.concatenate([keep, keep], axis=0)
    p = dot(v, hi)
    return p[:n] + p[n:] + dot(v[:n], lo)


def products(t_ref, vi, vj, listed):
    return product(t_ref, vj, listed, True), product(t_ref, vi, listed, False)


def put_rows(out_ref, acc_ref, first, leaves, own_ref=None):
    for k in range(leaves):
        at = slice(k * W, (k + 1) * W)
        x = acc_ref[first + k] * (1.0 / PEAK)
        out_ref[:, at] = x if own_ref is None else x + NUGGET * own_ref[:, at]


def evaluate_kernel(i0, i1, leaf_dev, last, listed_ref, pts_ref, cols_ref, v_ref, center_ref, wide_ref, *rest):
    rest = list(rest)
    far = i1 + REACH > leaf_dev
    shift_by = 0
    edge_ref = rest.pop(0) if far else None
    own_ref = rest.pop(0) if last else None
    prev_ref = rest.pop(0) if i0 else None
    tiles_ref = rest.pop(0)
    acc_ref = rest.pop(1 if last else 0)
    rows_ref = rest.pop(0) if last or far else None
    bc_ref = rest.pop(0)
    compact = jnp.max(wide_ref[...]) <= COMPACT
    if far:
        pts_all, v_all = rest
        n = v_ref.shape[1] // 2
        own = leaf_dev - i0
        pts_all[0:own] = pts_ref[i0:leaf_dev]
        v_all[0:own] = v_ref[i0:leaf_dev]
        first = center_ref[leaf_dev - 1, 0:3, :]
        pts_all[own:] = jnp.zeros_like(pts_all[own:])
        for k in range(REACH):
            got = edge_ref[n : n + 3, k * W : (k + 1) * W]
            pts_all[own + k, 0:3, :] = got
            far_off = jnp.abs(got - first) * (SCALE * COMPACT / RANGE)
            wide = far_off if k == 0 else jnp.maximum(wide, far_off)
        load_values(v_all, edge_ref, REACH, own)
        compact = compact & (jnp.max(wide) <= COMPACT)
        pts_ref, v_ref = pts_all, v_all
        shift_by = i0
    if i0:
        acc_ref[...] = prev_ref[...]
    else:
        acc_ref[...] = jnp.zeros_like(acc_ref)
    tiles_ref[0] = jnp.zeros_like(tiles_ref[0])

    def finish(i, slot):
        to_row, to_col = products(
            tiles_ref.at[slot], v_ref[i - shift_by], v_ref[i + REACH - shift_by], listed_ref[i * STEPS + REACH]
        )
        acc_ref[i] += to_row
        acc_ref[i + REACH] += to_col

    def near_leaf(i, _):
        slot = (i - i0) * STEPS
        cols = cols_ref[i]
        center = center_ref[i]
        vi = v_ref[i - shift_by]

        def make(d):
            block = near_squares(cols, pts_ref[i + d - shift_by], center)
            make_tile(tiles_ref.at[slot + (1 + d)], block, d == 0)

        make(0)
        finish(jnp.maximum(i - 1, i0), slot)
        total = None
        for d in range(REACH):
            make(d + 1)
            to_row, to_col = products(
                tiles_ref.at[slot + (1 + d)], vi, v_ref[i + d - shift_by], listed_ref[i * STEPS + d]
            )
            total = to_row if total is None else total + to_row
            acc_ref[i + d] += to_col
        acc_ref[i] += total
        return 0

    def far_leaf(i, _):
        slot = (i - i0) * STEPS
        spread_rows(bc_ref, pts_ref[i - shift_by])

        def step(d, _):
            t_ref = tiles_ref.at[slot + (1 + d)]
            block = far_squares(bc_ref, pts_ref.at[i + d - shift_by])
            lax.cond(d == 0, lambda: make_tile(t_ref, block, True), lambda: make_tile(t_ref, block, False))

            @pl.when(d < REACH)
            def _():
                to_row, to_col = products(
                    t_ref, v_ref[i - shift_by], v_ref[i + d - shift_by], listed_ref[i * STEPS + d]
                )
                acc_ref[i] += to_row
                acc_ref[i + d] += to_col

            return 0

        @pl.when(i > i0)
        def _():
            finish(i - 1, slot)

        return lax.fori_loop(0, STEPS, step, 0)

    @pl.when(compact)
    def _():
        lax.fori_loop(i0, i1, near_leaf, 0)

    @pl.when(jnp.logical_not(compact))
    def _():
        lax.fori_loop(i0, i1, far_leaf, 0)

    finish(i1 - 1, (i1 - i0) * STEPS)
    if far:
        put_rows(rows_ref, acc_ref, leaf_dev, REACH)
    if last:
        put_rows(rows_ref, acc_ref, 0, leaf_dev, own_ref)


def clear_or_copy(acc_ref, prev_ref):
    acc_ref[...] = jnp.zeros_like(acc_ref) if prev_ref is None else prev_ref[...]


def weighted(acc_ref, field_ref, first, leaves):
    total = acc_ref[first] * field_ref[:, 0:W]
    for k in range(1, leaves):
        total += acc_ref[first + k] * field_ref[:, k * W : (k + 1) * W]
    return total


def apply_kernel(i0, i1, leaf_dev, last, listed_ref, tiles_ref, w_ref, *rest):
    rest = list(rest)
    if last:
        far_ref, extra_ref = rest.pop(0), rest.pop(0)
    prev_ref = rest.pop(0) if i0 else None
    acc_ref = rest.pop(0)
    dots_ref = rest.pop(0) if last else None
    v_ref = rest.pop(0)
    load_values(v_ref, w_ref, leaf_dev, 0)
    clear_or_copy(acc_ref, prev_ref)

    def one_leaf(i, _):
        slot = (i - i0) * STEPS
        vi = v_ref[i]
        total = None
        for d in range(STEPS):
            to_row, to_col = products(
                tiles_ref.at[slot + (1 + d)], vi, v_ref[i + d], listed_ref[i * STEPS + d]
            )
            total = to_row if total is None else total + to_row
            acc_ref[i + d] += to_col
        acc_ref[i] += total
        return 0

    lax.fori_loop(i0, i1, one_leaf, 0)
    if last:
        total = weighted(acc_ref, w_ref, 0, leaf_dev) + weighted(acc_ref, far_ref, leaf_dev, REACH)
        dots_ref[...] = (total + extra_ref[...]) * (1.0 / PEAK)


def edge_kernel(i0, leaf_dev, listed_ref, tiles_ref, w_ref, far_ref, prev_ref, acc_ref, send_ref, dots_ref, v_ref, part_ref):
    held = leaf_dev - i0
    load_values(v_ref, w_ref, leaf_dev, 0)
    clear_or_copy(part_ref, None)

    def one_leaf(i, _):
        slot = (i - i0) * STEPS
        vi = v_ref[i]
        for d in range(STEPS):
            part_ref[i - i0 + d] += product(
                tiles_ref.at[slot + (1 + d)], vi, listed_ref[i * STEPS + d], False
            )
        return 0

    lax.fori_loop(i0, leaf_dev, one_leaf, 0)
    dots_ref[...] = weighted(part_ref, w_ref.at[:, i0 * W :], 0, held) + weighted(part_ref, far_ref, held, REACH)
    acc_ref[...] = prev_ref[...]
    for k in range(held + REACH):
        acc_ref[i0 + k] += part_ref[k]
    put_rows(send_ref, acc_ref, leaf_dev, REACH)


def finish_kernel(
    i0, leaf_dev, listed_ref, tiles_hbm, w_ref, far_ref, prev_ref, rows_ref, v_ref, acc_ref, tiles_ref, sems
):
    copies = []
    for k in range(leaf_dev - i0):
        at = pl.ds(k * STEPS, STEPS)
        copies.append(pltpu.make_async_copy(tiles_hbm.at[pl.ds(k * STEPS + 1, STEPS)], tiles_ref.at[at], sems.at[k]))
    copies[0].start()
    load_values(v_ref, w_ref.at[:, i0 * W :], leaf_dev - i0, 0)
    load_values(v_ref, far_ref, REACH, leaf_dev - i0)
    acc_ref[...] = prev_ref[...]
    copies[1].start()
    for k, copy in enumerate(copies):
        copy.wait()
        if k + 2 < len(copies):
            copies[k + 2].start()
        total = None
        for d in range(STEPS):
            to_row = product(tiles_ref.at[k * STEPS + d], v_ref[k + d], listed_ref[(i0 + k) * STEPS + d], True)
            total = to_row if total is None else total + to_row
        acc_ref[i0 + k] += total
    put_rows(rows_ref, acc_ref, 0, leaf_dev, w_ref)


VM = pl.BlockSpec(memory_space=pltpu.VMEM)
SM = pl.BlockSpec(memory_space=pltpu.SMEM)
HBM = pl.BlockSpec(memory_space=pltpu.HBM)
PARAMS = pltpu.CompilerParams(vmem_limit_bytes=8 << 20)


def prepare_call(pairs, count, base, coords, order, b):
    leaves = order.shape[0]
    n = b.shape[0]
    return pl.pallas_call(
        prepare_kernel,
        out_shape=(
            jax.ShapeDtypeStruct((pairs.shape[1], 16, HALF), jnp.bfloat16),
            jax.ShapeDtypeStruct((leaves, 8, W), jnp.float32),
            jax.ShapeDtypeStruct((leaves, W, 8 * GROUPS), jnp.bfloat16),
            jax.ShapeDtypeStruct((leaves, 2 * n, W), jnp.bfloat16),
            jax.ShapeDtypeStruct((leaves, 8, W), jnp.float32),
            jax.ShapeDtypeStruct((8, W), jnp.float32),
            jax.ShapeDtypeStruct((n + 3, REACH * W), jnp.float32),
        ),
        in_specs=[SM, SM, HBM, HBM, HBM, HBM],
        out_specs=(VM,) * 7,
        scratch_shapes=[
            pltpu.VMEM(pairs.shape, jnp.int32),
            pltpu.VMEM(coords.shape, jnp.float32),
            pltpu.VMEM(order.shape, jnp.int32),
            pltpu.VMEM(b.shape, jnp.float32),
            pltpu.SemaphoreType.DMA((4,)),
        ],
        compiler_params=PARAMS,
        name="prepare",
    )(count, base, *(pltpu.with_memory_space_constraint(x, pltpu.HBM) for x in (pairs, coords, order, b)))


def shapes_out(leaf_dev, n, far, last):
    acc = (leaf_dev + REACH, n, W)
    rows = (n, (leaf_dev if last else REACH) * W)
    f32 = jnp.float32
    if last:
        return [jax.ShapeDtypeStruct(rows, f32)], [pltpu.VMEM(acc, f32)]
    return [jax.ShapeDtypeStruct(acc, f32)] + ([jax.ShapeDtypeStruct(rows, f32)] if far else []), []


def evaluate_call(i0, i1, leaf_dev, n, prepared, far, own, prev):
    tiles = (i1 - i0) * STEPS
    last = own is not None
    ops = [*prepared, *far, *([own] if last else []), *([] if prev is None else [prev])]
    outs, held_acc = shapes_out(leaf_dev, n, bool(far), last)
    scratch = [*held_acc, pltpu.VMEM((W, 3 * HALF), jnp.float32)]
    if far:
        held = leaf_dev - i0 + REACH
        scratch += [pltpu.VMEM((held, 8, W), jnp.float32), pltpu.VMEM((held, 2 * n, W), jnp.bfloat16)]
    outs = [jax.ShapeDtypeStruct((tiles + 1, 4, W, HALF), jnp.bfloat16), *outs]
    return pl.pallas_call(
        functools.partial(evaluate_kernel, i0, i1, leaf_dev, last),
        out_shape=outs,
        in_specs=[VM] * len(ops),
        out_specs=[VM] * len(outs),
        scratch_shapes=scratch,
        compiler_params=PARAMS,
        cost_estimate=pl.CostEstimate(flops=tiles << 28, transcendentals=tiles << 17, bytes_accessed=tiles << 18),
        name=f"evaluate_{i0}",
    )(*ops)


def small_call(kernel, name, outs, scratch, tiles, ops, in_hbm=()):
    return pl.pallas_call(
        kernel,
        out_shape=[jax.ShapeDtypeStruct(shape, jnp.float32) for shape in outs],
        in_specs=[HBM if k in in_hbm else VM for k in range(len(ops))],
        out_specs=[VM] * len(outs),
        scratch_shapes=scratch,
        compiler_params=pltpu.CompilerParams(vmem_limit_bytes=18 << 20) if in_hbm else PARAMS,
        cost_estimate=pl.CostEstimate(flops=tiles.shape[0] << 27, transcendentals=0, bytes_accessed=tiles.size * 2),
        name=name,
    )(*[pltpu.with_memory_space_constraint(x, pltpu.HBM) if k in in_hbm else x for k, x in enumerate(ops)])


def apply_call(i0, i1, leaf_dev, n, listed, tiles, own, last, prev):
    acc = (leaf_dev + REACH, n, W)
    ops = [listed, tiles, own, *last, *([] if prev is None else [prev])]
    return small_call(
        functools.partial(apply_kernel, i0, i1, leaf_dev, bool(last)),
        f"apply_{i0}",
        [acc, (n, W)] if last else [acc],
        [pltpu.VMEM((leaf_dev, 2 * n, W), jnp.bfloat16)],
        tiles,
        ops,
    )


def edge_call(i0, leaf_dev, n, listed, tiles, own, far, prev):
    acc = (leaf_dev + REACH, n, W)
    return small_call(
        functools.partial(edge_kernel, i0, leaf_dev),
        "apply_edge",
        [acc, (n, REACH * W), (n, W)],
        [
            pltpu.VMEM((leaf_dev, 2 * n, W), jnp.bfloat16),
            pltpu.VMEM((leaf_dev - i0 + REACH, n, W), jnp.float32),
        ],
        tiles,
        [listed, tiles, own, far, prev],
    )


def finish_call(i0, leaf_dev, n, listed, tiles, own, far, prev):
    acc = (leaf_dev + REACH, n, W)
    return small_call(
        functools.partial(finish_kernel, i0, leaf_dev),
        "finish",
        [own.shape],
        [
            pltpu.VMEM((leaf_dev - i0 + REACH, 2 * n, W), jnp.bfloat16),
            pltpu.VMEM(acc, jnp.float32),
            pltpu.VMEM((tiles.shape[0] - 1, *tiles.shape[1:]), jnp.bfloat16),
            pltpu.SemaphoreType.DMA((leaf_dev - i0,)),
        ],
        tiles,
        [listed, tiles, own, far, prev],
        in_hbm=(1,),
    )[0]


def shift(value, by):
    length = lax.axis_size("leaf")
    return lax.ppermute(value, "leaf", [(i, i + by) for i in range(length) if 0 <= i + by < length])


def sum_over_leaf(value):
    length = lax.axis_size("leaf")
    value = value + lax.ppermute(value, "leaf", [(i, i ^ 1) for i in range(length)])
    copies = jnp.broadcast_to(value.reshape(-1), (length // 2, value.size))
    groups = [[i for i in range(length) if i % 2 == c] for c in range(2)]
    got = lax.all_to_all(
        copies, "leaf", split_axis=0, concat_axis=0, tiled=True, axis_index_groups=groups
    )
    return jnp.sum(got, axis=0).reshape(value.shape)


def body(coords, site_order, leaf_pairs, pair_count, probes):
    leaf_dev, width = site_order.shape
    n = probes.shape[0]
    edge = REACH * width
    base = (lax.axis_index("leaf") * leaf_dev).astype(jnp.int32).reshape(1)
    *prepared, packed = prepare_call(leaf_pairs, pair_count, base, coords, site_order, probes)
    far = shift(packed, -1)
    cut0, cut1 = leaf_dev - REACH - 5, leaf_dev - REACH - 2
    evaluate = functools.partial(evaluate_call, leaf_dev=leaf_dev, n=n, prepared=prepared)
    tiles0, acc = evaluate(0, cut0, far=(), own=None, prev=None)
    tiles1, acc, send = evaluate(cut1, leaf_dev, far=(far,), own=None, prev=acc)
    back = shift(send, 1)
    tiles2, image = evaluate(cut0, cut1, far=(), own=probes, prev=acc)
    image = jnp.concatenate([image[:, :edge] + back, image[:, edge:]], axis=1)

    image_far = shift(image[:, :edge], -1)
    common = dict(leaf_dev=leaf_dev, n=n, listed=prepared[0], own=image)
    (acc,) = apply_call(0, cut0, tiles=tiles0, last=(), prev=None, **common)
    acc, send, edge_dots = edge_call(cut1, tiles=tiles1, far=image_far, prev=acc, **common)
    back = shift(send, 1)
    acc, dots = apply_call(cut0, cut1, tiles=tiles2, last=(image_far, edge_dots), prev=acc, **common)
    square = jnp.sum(image * image, axis=1)
    sums = jnp.stack(
        [
            jnp.sum(probes * probes, axis=1),
            jnp.sum(probes * image, axis=1),
            square,
            jnp.sum(dots, axis=1) + NUGGET * square,
        ]
    )
    image2 = finish_call(cut1, tiles=tiles1, far=image_far, prev=acc, **common)
    image2 = jnp.concatenate([image2[:, :edge] + back, image2[:, edge:]], axis=1)
    rr, bw, ww, wz = sum_over_leaf(sums)
    alpha = rr / bw
    rr1 = rr - 2.0 * alpha * bw + alpha * alpha * ww
    beta = rr1 / rr
    g = 1.0 + beta
    curve = g * g * bw - 2.0 * g * alpha * ww + alpha * alpha * wz
    alpha1 = rr1 / curve
    c = lambda x: x[:, None]
    direction1 = c(g) * probes - c(alpha) * image
    image1 = c(g) * image - c(alpha) * image2
    solution = c(alpha) * probes + c(alpha1) * direction1
    residual = probes - c(alpha) * image - c(alpha1) * image1
    return solution, residual


def solution(mesh):
    in_specs = (P(None, "leaf"), P("leaf", None), P(None, "leaf"), P("leaf"), P("probe", "leaf"))
    out_specs = (P("probe", "leaf"), P("probe", "leaf"))
    return jax.shard_map(body, mesh=mesh, in_specs=in_specs, out_specs=out_specs, check_vma=False)
```

```python
import functools
import math

import jax
import jax.numpy as jnp
from jax import lax
from jax.experimental import pallas as pl
from jax.experimental.pallas import tpu as pltpu
from jax.sharding import PartitionSpec as P

REACH = 5
STEPS = REACH + 1
UNIT = 0.025
LENGTH = 0.12
NUGGET = 0.5
W = 256
TAPER = REACH * UNIT
DECAY = math.sqrt(3.0) * TAPER / LENGTH
LOG2E = math.log2(math.e)
CHUNK = 16
HALF = W // 2
FLOOR_INV = 1e18
KAPPA = DECAY * LOG2E
PEAK = KAPPA**6 / (4.0 * DECAY) * 2.0**KAPPA
SCALE = KAPPA / TAPER
COMPACT = 20.0 * KAPPA * KAPPA
RANGE = 1e15
TINY = 1e-12
GROUPS = 6


def split2(x):
    hi = x.astype(jnp.bfloat16)
    lo = (x - hi.astype(jnp.float32)).astype(jnp.bfloat16)
    return hi, lo


def split3(x):
    hi = x.astype(jnp.bfloat16)
    rest = x - hi.astype(jnp.float32)
    mid = rest.astype(jnp.bfloat16)
    lo = (rest - mid.astype(jnp.float32)).astype(jnp.bfloat16)
    return hi, mid, lo


def load_values(v_ref, src_ref, leaves, first):
    n = v_ref.shape[1] // 2
    for k in range(leaves):
        hi, lo = split2(src_ref[0:n, k * W : (k + 1) * W])
        v_ref[first + k] = jnp.concatenate([hi, lo], axis=0)


def split_rows(point, center, top, weight):
    x = (point - center) * SCALE
    sq = x * x
    sq = sq[0:1] + sq[1:2] + sq[2:3]
    row = lax.broadcasted_iota(jnp.int32, x.shape, 0)
    x = jnp.where(top, x * weight, jnp.where(row == 3, sq, 0.0))
    hi = x.astype(jnp.bfloat16).astype(jnp.float32)
    rest = x - hi
    mid = rest.astype(jnp.bfloat16).astype(jnp.float32)
    return hi, mid, rest - mid


def prepare_kernel(
    count_ref, base_ref, pairs_hbm, coords_hbm, order_hbm, b_hbm,
    listed_ref, pts_ref, cols_ref, v_ref, center_ref, wide_ref, edge_ref,
    pairs_ref, coords_ref, order_ref, b_ref, sems,
):
    copies = [
        pltpu.make_async_copy(pairs_hbm, pairs_ref, sems.at[0]),
        pltpu.make_async_copy(coords_hbm, coords_ref, sems.at[1]),
        pltpu.make_async_copy(order_hbm, order_ref, sems.at[2]),
        pltpu.make_async_copy(b_hbm, b_ref, sems.at[3]),
    ]
    for copy in copies:
        copy.start()
    copies[0].wait()
    slots = pairs_ref.shape[1]
    row = pairs_ref[0:1, :]
    place = (row - base_ref[0]) * STEPS + pairs_ref[1:2, :] - row
    live = lax.broadcasted_iota(jnp.int32, (1, slots), 1) < count_ref[0]
    place = jnp.where(live, place, -1)
    hit = lax.broadcasted_iota(jnp.int32, (slots, slots), 0) == place
    found = jnp.sum(hit.astype(jnp.float32), axis=1, keepdims=True)
    listed_ref[...] = jnp.broadcast_to(found.astype(jnp.bfloat16)[:, :, None], listed_ref.shape)
    for copy in copies[1:]:
        copy.wait()
    leaves = order_ref.shape[0]
    n = b_ref.shape[0]
    sub = lax.broadcasted_iota(jnp.int32, (W, W), 0).astype(jnp.float32).astype(jnp.bfloat16)
    one, zero = jnp.ones((W, W), jnp.bfloat16), jnp.zeros((W, W), jnp.bfloat16)
    dot = functools.partial(jnp.dot, preferred_element_type=jnp.float32)
    top = lax.broadcasted_iota(jnp.int32, (8, W), 0) < 3
    pad = jnp.zeros((5, W), jnp.float32)
    wide = jnp.zeros((8, W), jnp.float32)
    for k in range(leaves):
        at = slice(k * W, (k + 1) * W)
        order = order_ref[k : k + 1, :].astype(jnp.float32).astype(jnp.bfloat16)
        sel = jnp.where(sub == jnp.broadcast_to(order, (W, W)), one, zero)
        raw = jnp.concatenate([coords_ref[:, at], pad], axis=0)
        parts = dot(jnp.concatenate(split3(raw), axis=0), sel)
        point = parts[0:8] + parts[8:16] + parts[16:24]
        got = point[0:3]
        center = jnp.broadcast_to(jnp.sum(point, axis=1, keepdims=True) * (1.0 / W), (8, W))
        pts_ref[k] = point
        center_ref[k] = center
        hi, mid, lo = split_rows(point, center, top, 1.0)
        square = jnp.where(top, 0.0, hi + mid + lo)
        first = center if k == 0 else first
        far_off = jnp.abs(point - first) * (SCALE * COMPACT / RANGE)
        wide = jnp.maximum(wide, jnp.maximum(square, far_off))
        unit = jnp.where(lax.broadcasted_iota(jnp.int32, (8, W), 0) == 3, 1.0, 0.0)
        stack = [hi, jnp.where(top, hi, mid), jnp.where(top, hi, lo)]
        stack += [jnp.where(top, mid, unit), jnp.where(top, mid, unit), jnp.where(top, lo, unit)]
        cols_ref[k] = jnp.transpose(jnp.concatenate(stack, axis=0)).astype(jnp.bfloat16)
        if k < REACH:
            edge_ref[0:n, at] = b_ref[:, at]
            edge_ref[n : n + 3, at] = got
    wide_ref[...] = wide
    load_values(v_ref, b_ref, leaves, 0)


def spread_rows(bc_ref, points):
    cols = jnp.transpose(points)
    for c in range(3):
        bc_ref[:, c * HALF : (c + 1) * HALF] = jnp.broadcast_to(cols[:, c : c + 1], (W, HALF))


def far_squares(bc_ref, other):
    def block(rows, h):
        u = None
        for c in range(3):
            b = jnp.broadcast_to(other[c : c + 1, h * HALF : (h + 1) * HALF], (CHUNK, HALF))
            d = bc_ref[rows, c * HALF : (c + 1) * HALF] - b
            u = d * d if u is None else u + d * d
        return u * (SCALE * SCALE)

    return block


def near_squares(cols, other, center):
    top = lax.broadcasted_iota(jnp.int32, (8, W), 0) < 3
    one = jnp.where(lax.broadcasted_iota(jnp.int32, (8, W), 0) == 3, 1.0, 0.0)
    hi, mid, lo = split_rows(other, center, top, -2.0)
    stack = [jnp.where(top, hi, one), jnp.where(top, mid, one), jnp.where(top, lo, one)]
    stack += [hi, mid, jnp.where(top, hi, lo)]
    rows = jnp.concatenate(stack, axis=0).astype(jnp.bfloat16)
    all_u = jnp.dot(cols, rows, preferred_element_type=jnp.float32)
    return lambda rows, h: all_u[rows, h * HALF : (h + 1) * HALF]


def make_tile(t_ref, block, same):
    for k in range(W // CHUNK):
        rows = slice(k * CHUNK, (k + 1) * CHUNK)
        lower = k * CHUNK >= HALF
        for h in range(2):
            if same and lower and h == 0:
                t_ref[0, rows, :] = jnp.zeros((CHUNK, HALF), jnp.bfloat16)
                t_ref[2, rows, :] = jnp.zeros((CHUNK, HALF), jnp.bfloat16)
                continue
            u = jnp.minimum(jnp.maximum(block(rows, h), TINY), KAPPA * KAPPA)
            q = u * lax.rsqrt(u)
            t = KAPPA - q
            e = jnp.exp2(t)
            t = t * t
            t = t * t
            x = ((q + KAPPA / 4.0) * (q + KAPPA / DECAY)) * (t * e)
            if same and lower == bool(h):
                x = x * 0.5
            hi, lo = split2(x)
            t_ref[h, rows, :] = hi
            t_ref[2 + h, rows, :] = lo


def product(t_ref, v, listed, transposed):
    hi = jnp.concatenate([t_ref[0], t_ref[1]], axis=1)
    lo = jnp.concatenate([t_ref[2], t_ref[3]], axis=1)
    dims = (((1,), (1 if transposed else 0,)), ((), ()))
    dot = functools.partial(lax.dot_general, dimension_numbers=dims, preferred_element_type=jnp.float32)
    n = v.shape[0] // 2
    keep = jnp.concatenate([listed, listed], axis=1)
    v = v * jnp.concatenate([keep, keep], axis=0)
    p = dot(v, hi)
    return p[:n] + p[n:] + dot(v[:n], lo)


def products(t_ref, vi, vj, listed):
    return product(t_ref, vj, listed, True), product(t_ref, vi, listed, False)


def put_rows(out_ref, acc_ref, first, leaves, own_ref=None):
    for k in range(leaves):
        at = slice(k * W, (k + 1) * W)
        x = acc_ref[first + k] * (1.0 / PEAK)
        out_ref[:, at] = x if own_ref is None else x + NUGGET * own_ref[:, at]


def evaluate_kernel(i0, i1, leaf_dev, last, listed_ref, pts_ref, cols_ref, v_ref, center_ref, wide_ref, *rest):
    rest = list(rest)
    far = i1 + REACH > leaf_dev
    shift_by = 0
    edge_ref = rest.pop(0) if far else None
    own_ref = rest.pop(0) if last else None
    prev_ref = rest.pop(0) if i0 else None
    tiles_ref = rest.pop(0)
    acc_ref = rest.pop(1 if last else 0)
    rows_ref = rest.pop(0) if last or far else None
    bc_ref = rest.pop(0)
    compact = jnp.max(wide_ref[...]) <= COMPACT
    if far:
        pts_all, v_all = rest
        n = v_ref.shape[1] // 2
        own = leaf_dev - i0
        pts_all[0:own] = pts_ref[i0:leaf_dev]
        v_all[0:own] = v_ref[i0:leaf_dev]
        first = center_ref[leaf_dev - 1, 0:3, :]
        pts_all[own:] = jnp.zeros_like(pts_all[own:])
        for k in range(REACH):
            got = edge_ref[n : n + 3, k * W : (k + 1) * W]
            pts_all[own + k, 0:3, :] = got
            far_off = jnp.abs(got - first) * (SCALE * COMPACT / RANGE)
            wide = far_off if k == 0 else jnp.maximum(wide, far_off)
        load_values(v_all, edge_ref, REACH, own)
        compact = compact & (jnp.max(wide) <= COMPACT)
        pts_ref, v_ref = pts_all, v_all
        shift_by = i0
    if i0:
        acc_ref[...] = prev_ref[...]
    else:
        acc_ref[...] = jnp.zeros_like(acc_ref)
    tiles_ref[0] = jnp.zeros_like(tiles_ref[0])

    def finish(i, slot):
        to_row, to_col = products(
            tiles_ref.at[slot], v_ref[i - shift_by], v_ref[i + REACH - shift_by], listed_ref[i * STEPS + REACH]
        )
        acc_ref[i] += to_row
        acc_ref[i + REACH] += to_col

    def near_leaf(i, _):
        slot = (i - i0) * STEPS
        cols = cols_ref[i]
        center = center_ref[i]
        vi = v_ref[i - shift_by]

        def make(d):
            block = near_squares(cols, pts_ref[i + d - shift_by], center)
            make_tile(tiles_ref.at[slot + (1 + d)], block, d == 0)

        make(0)
        finish(jnp.maximum(i - 1, i0), slot)
        total = None
        for d in range(REACH):
            make(d + 1)
            to_row, to_col = products(
                tiles_ref.at[slot + (1 + d)], vi, v_ref[i + d - shift_by], listed_ref[i * STEPS + d]
            )
            total = to_row if total is None else total + to_row
            acc_ref[i + d] += to_col
        acc_ref[i] += total
        return 0

    def far_leaf(i, _):
        slot = (i - i0) * STEPS
        spread_rows(bc_ref, pts_ref[i - shift_by])

        def step(d, _):
            t_ref = tiles_ref.at[slot + (1 + d)]
            block = far_squares(bc_ref, pts_ref.at[i + d - shift_by])
            lax.cond(d == 0, lambda: make_tile(t_ref, block, True), lambda: make_tile(t_ref, block, False))

            @pl.when(d < REACH)
            def _():
                to_row, to_col = products(
                    t_ref, v_ref[i - shift_by], v_ref[i + d - shift_by], listed_ref[i * STEPS + d]
                )
                acc_ref[i] += to_row
                acc_ref[i + d] += to_col

            return 0

        @pl.when(i > i0)
        def _():
            finish(i - 1, slot)

        return lax.fori_loop(0, STEPS, step, 0)

    @pl.when(compact)
    def _():
        lax.fori_loop(i0, i1, near_leaf, 0)

    @pl.when(jnp.logical_not(compact))
    def _():
        lax.fori_loop(i0, i1, far_leaf, 0)

    finish(i1 - 1, (i1 - i0) * STEPS)
    if far:
        put_rows(rows_ref, acc_ref, leaf_dev, REACH)
    if last:
        put_rows(rows_ref, acc_ref, 0, leaf_dev, own_ref)


def clear_or_copy(acc_ref, prev_ref):
    acc_ref[...] = jnp.zeros_like(acc_ref) if prev_ref is None else prev_ref[...]


def weighted(acc_ref, field_ref, first, leaves):
    total = acc_ref[first] * field_ref[:, 0:W]
    for k in range(1, leaves):
        total += acc_ref[first + k] * field_ref[:, k * W : (k + 1) * W]
    return total


def unrolled(start, stop, one):
    for i in range(start, stop):
        one(i, 0)


def apply_kernel(i0, i1, leaf_dev, last, listed_ref, tiles_ref, w_ref, *rest):
    rest = list(rest)
    if last:
        far_ref, extra_ref = rest.pop(0), rest.pop(0)
    prev_ref = rest.pop(0) if i0 else None
    acc_ref = rest.pop(0)
    dots_ref = rest.pop(0) if last else None
    v_ref = rest.pop(0)
    load_values(v_ref, w_ref, leaf_dev, 0)
    clear_or_copy(acc_ref, prev_ref)

    def one_leaf(i, _):
        slot = (i - i0) * STEPS
        vi = v_ref[i]
        total = None
        for d in range(STEPS):
            to_row, to_col = products(
                tiles_ref.at[slot + (1 + d)], vi, v_ref[i + d], listed_ref[i * STEPS + d]
            )
            total = to_row if total is None else total + to_row
            acc_ref[i + d] += to_col
        acc_ref[i] += total
        return 0

    unrolled(i0, i1, one_leaf)
    if last:
        total = weighted(acc_ref, w_ref, 0, leaf_dev) + weighted(acc_ref, far_ref, leaf_dev, REACH)
        dots_ref[...] = (total + extra_ref[...]) * (1.0 / PEAK)


def edge_kernel(i0, leaf_dev, listed_ref, tiles_ref, w_ref, far_ref, prev_ref, acc_ref, send_ref, dots_ref, v_ref, part_ref):
    held = leaf_dev - i0
    load_values(v_ref, w_ref, leaf_dev, 0)
    clear_or_copy(part_ref, None)

    def one_leaf(i, _):
        slot = (i - i0) * STEPS
        vi = v_ref[i]
        for d in range(STEPS):
            part_ref[i - i0 + d] += product(
                tiles_ref.at[slot + (1 + d)], vi, listed_ref[i * STEPS + d], False
            )
        return 0

    unrolled(i0, leaf_dev, one_leaf)
    dots_ref[...] = weighted(part_ref, w_ref.at[:, i0 * W :], 0, held) + weighted(part_ref, far_ref, held, REACH)
    acc_ref[...] = prev_ref[...]
    for k in range(held + REACH):
        acc_ref[i0 + k] += part_ref[k]
    put_rows(send_ref, acc_ref, leaf_dev, REACH)


def finish_kernel(
    i0, leaf_dev, listed_ref, tiles_hbm, w_ref, far_ref, prev_ref, rows_ref, v_ref, acc_ref, tiles_ref, sems
):
    copies = []
    for k in range(leaf_dev - i0):
        at = pl.ds(k * STEPS, STEPS)
        copies.append(pltpu.make_async_copy(tiles_hbm.at[pl.ds(k * STEPS + 1, STEPS)], tiles_ref.at[at], sems.at[k]))
    copies[0].start()
    load_values(v_ref, w_ref.at[:, i0 * W :], leaf_dev - i0, 0)
    load_values(v_ref, far_ref, REACH, leaf_dev - i0)
    acc_ref[...] = prev_ref[...]
    copies[1].start()
    for k, copy in enumerate(copies):
        copy.wait()
        if k + 2 < len(copies):
            copies[k + 2].start()
        total = None
        for d in range(STEPS):
            to_row = product(tiles_ref.at[k * STEPS + d], v_ref[k + d], listed_ref[(i0 + k) * STEPS + d], True)
            total = to_row if total is None else total + to_row
        acc_ref[i0 + k] += total
    put_rows(rows_ref, acc_ref, 0, leaf_dev, w_ref)


VM = pl.BlockSpec(memory_space=pltpu.VMEM)
SM = pl.BlockSpec(memory_space=pltpu.SMEM)
HBM = pl.BlockSpec(memory_space=pltpu.HBM)
PARAMS = pltpu.CompilerParams(vmem_limit_bytes=8 << 20)


def prepare_call(pairs, count, base, coords, order, b):
    leaves = order.shape[0]
    n = b.shape[0]
    return pl.pallas_call(
        prepare_kernel,
        out_shape=(
            jax.ShapeDtypeStruct((pairs.shape[1], 16, HALF), jnp.bfloat16),
            jax.ShapeDtypeStruct((leaves, 8, W), jnp.float32),
            jax.ShapeDtypeStruct((leaves, W, 8 * GROUPS), jnp.bfloat16),
            jax.ShapeDtypeStruct((leaves, 2 * n, W), jnp.bfloat16),
            jax.ShapeDtypeStruct((leaves, 8, W), jnp.float32),
            jax.ShapeDtypeStruct((8, W), jnp.float32),
            jax.ShapeDtypeStruct((n + 3, REACH * W), jnp.float32),
        ),
        in_specs=[SM, SM, HBM, HBM, HBM, HBM],
        out_specs=(VM,) * 7,
        scratch_shapes=[
            pltpu.VMEM(pairs.shape, jnp.int32),
            pltpu.VMEM(coords.shape, jnp.float32),
            pltpu.VMEM(order.shape, jnp.int32),
            pltpu.VMEM(b.shape, jnp.float32),
            pltpu.SemaphoreType.DMA((4,)),
        ],
        compiler_params=PARAMS,
        name="prepare",
    )(count, base, *(pltpu.with_memory_space_constraint(x, pltpu.HBM) for x in (pairs, coords, order, b)))


def shapes_out(leaf_dev, n, far, last):
    acc = (leaf_dev + REACH, n, W)
    rows = (n, (leaf_dev if last else REACH) * W)
    f32 = jnp.float32
    if last:
        return [jax.ShapeDtypeStruct(rows, f32)], [pltpu.VMEM(acc, f32)]
    return [jax.ShapeDtypeStruct(acc, f32)] + ([jax.ShapeDtypeStruct(rows, f32)] if far else []), []


def evaluate_call(i0, i1, leaf_dev, n, prepared, far, own, prev):
    tiles = (i1 - i0) * STEPS
    last = own is not None
    ops = [*prepared, *far, *([own] if last else []), *([] if prev is None else [prev])]
    outs, held_acc = shapes_out(leaf_dev, n, bool(far), last)
    scratch = [*held_acc, pltpu.VMEM((W, 3 * HALF), jnp.float32)]
    if far:
        held = leaf_dev - i0 + REACH
        scratch += [pltpu.VMEM((held, 8, W), jnp.float32), pltpu.VMEM((held, 2 * n, W), jnp.bfloat16)]
    outs = [jax.ShapeDtypeStruct((tiles + 1, 4, W, HALF), jnp.bfloat16), *outs]
    return pl.pallas_call(
        functools.partial(evaluate_kernel, i0, i1, leaf_dev, last),
        out_shape=outs,
        in_specs=[VM] * len(ops),
        out_specs=[VM] * len(outs),
        scratch_shapes=scratch,
        compiler_params=PARAMS,
        cost_estimate=pl.CostEstimate(flops=tiles << 28, transcendentals=tiles << 17, bytes_accessed=tiles << 18),
        name=f"evaluate_{i0}",
    )(*ops)


def small_call(kernel, name, outs, scratch, tiles, ops, in_hbm=()):
    return pl.pallas_call(
        kernel,
        out_shape=[jax.ShapeDtypeStruct(shape, jnp.float32) for shape in outs],
        in_specs=[HBM if k in in_hbm else VM for k in range(len(ops))],
        out_specs=[VM] * len(outs),
        scratch_shapes=scratch,
        compiler_params=pltpu.CompilerParams(vmem_limit_bytes=18 << 20) if in_hbm else PARAMS,
        cost_estimate=pl.CostEstimate(flops=tiles.shape[0] << 27, transcendentals=0, bytes_accessed=tiles.size * 2),
        name=name,
    )(*[pltpu.with_memory_space_constraint(x, pltpu.HBM) if k in in_hbm else x for k, x in enumerate(ops)])


def apply_call(i0, i1, leaf_dev, n, listed, tiles, own, last, prev):
    acc = (leaf_dev + REACH, n, W)
    ops = [listed, tiles, own, *last, *([] if prev is None else [prev])]
    return small_call(
        functools.partial(apply_kernel, i0, i1, leaf_dev, bool(last)),
        f"apply_{i0}",
        [acc, (n, W)] if last else [acc],
        [pltpu.VMEM((leaf_dev, 2 * n, W), jnp.bfloat16)],
        tiles,
        ops,
    )


def edge_call(i0, leaf_dev, n, listed, tiles, own, far, prev):
    acc = (leaf_dev + REACH, n, W)
    return small_call(
        functools.partial(edge_kernel, i0, leaf_dev),
        "apply_edge",
        [acc, (n, REACH * W), (n, W)],
        [
            pltpu.VMEM((leaf_dev, 2 * n, W), jnp.bfloat16),
            pltpu.VMEM((leaf_dev - i0 + REACH, n, W), jnp.float32),
        ],
        tiles,
        [listed, tiles, own, far, prev],
    )


def finish_call(i0, leaf_dev, n, listed, tiles, own, far, prev):
    acc = (leaf_dev + REACH, n, W)
    return small_call(
        functools.partial(finish_kernel, i0, leaf_dev),
        "finish",
        [own.shape],
        [
            pltpu.VMEM((leaf_dev - i0 + REACH, 2 * n, W), jnp.bfloat16),
            pltpu.VMEM(acc, jnp.float32),
            pltpu.VMEM((tiles.shape[0] - 1, *tiles.shape[1:]), jnp.bfloat16),
            pltpu.SemaphoreType.DMA((leaf_dev - i0,)),
        ],
        tiles,
        [listed, tiles, own, far, prev],
        in_hbm=(1,),
    )[0]


def shift(value, by):
    length = lax.axis_size("leaf")
    return lax.ppermute(value, "leaf", [(i, i + by) for i in range(length) if 0 <= i + by < length])


def sum_over_leaf(value):
    length = lax.axis_size("leaf")
    value = value + lax.ppermute(value, "leaf", [(i, i ^ 1) for i in range(length)])
    copies = jnp.broadcast_to(value.reshape(-1), (length // 2, value.size))
    groups = [[i for i in range(length) if i % 2 == c] for c in range(2)]
    got = lax.all_to_all(
        copies, "leaf", split_axis=0, concat_axis=0, tiled=True, axis_index_groups=groups
    )
    return jnp.sum(got, axis=0).reshape(value.shape)


def body(coords, site_order, leaf_pairs, pair_count, probes):
    leaf_dev, width = site_order.shape
    n = probes.shape[0]
    edge = REACH * width
    base = (lax.axis_index("leaf") * leaf_dev).astype(jnp.int32).reshape(1)
    *prepared, packed = prepare_call(leaf_pairs, pair_count, base, coords, site_order, probes)
    far = shift(packed, -1)
    cut0, cut1 = leaf_dev - REACH - 5, leaf_dev - REACH - 2
    evaluate = functools.partial(evaluate_call, leaf_dev=leaf_dev, n=n, prepared=prepared)
    tiles0, acc = evaluate(0, cut0, far=(), own=None, prev=None)
    tiles1, acc, send = evaluate(cut1, leaf_dev, far=(far,), own=None, prev=acc)
    back = shift(send, 1)
    tiles2, image = evaluate(cut0, cut1, far=(), own=probes, prev=acc)
    image = jnp.concatenate([image[:, :edge] + back, image[:, edge:]], axis=1)

    image_far = shift(image[:, :edge], -1)
    common = dict(leaf_dev=leaf_dev, n=n, listed=prepared[0], own=image)
    (acc,) = apply_call(0, cut0, tiles=tiles0, last=(), prev=None, **common)
    acc, send, edge_dots = edge_call(cut1, tiles=tiles1, far=image_far, prev=acc, **common)
    back = shift(send, 1)
    acc, dots = apply_call(cut0, cut1, tiles=tiles2, last=(image_far, edge_dots), prev=acc, **common)
    square = jnp.sum(image * image, axis=1)
    sums = jnp.stack(
        [
            jnp.sum(probes * probes, axis=1),
            jnp.sum(probes * image, axis=1),
            square,
            jnp.sum(dots, axis=1) + NUGGET * square,
        ]
    )
    image2 = finish_call(cut1, tiles=tiles1, far=image_far, prev=acc, **common)
    image2 = jnp.concatenate([image2[:, :edge] + back, image2[:, edge:]], axis=1)
    rr, bw, ww, wz = sum_over_leaf(sums)
    alpha = rr / bw
    rr1 = rr - 2.0 * alpha * bw + alpha * alpha * ww
    beta = rr1 / rr
    g = 1.0 + beta
    curve = g * g * bw - 2.0 * g * alpha * ww + alpha * alpha * wz
    alpha1 = rr1 / curve
    c = lambda x: x[:, None]
    direction1 = c(g) * probes - c(alpha) * image
    image1 = c(g) * image - c(alpha) * image2
    solution = c(alpha) * probes + c(alpha1) * direction1
    residual = probes - c(alpha) * image - c(alpha1) * image1
    return solution, residual


def solution(mesh):
    in_specs = (P(None, "leaf"), P("leaf", None), P(None, "leaf"), P("leaf"), P("probe", "leaf"))
    out_specs = (P("probe", "leaf"), P("probe", "leaf"))
    return jax.shard_map(body, mesh=mesh, in_specs=in_specs, out_specs=out_specs, check_vma=False)
```

```python
import functools
import math

import jax
import jax.numpy as jnp
from jax import lax
from jax.experimental import pallas as pl
from jax.experimental.pallas import tpu as pltpu
from jax.sharding import PartitionSpec as P

REACH = 5
STEPS = REACH + 1
UNIT = 0.025
LENGTH = 0.12
NUGGET = 0.5
W = 256
TAPER = REACH * UNIT
DECAY = math.sqrt(3.0) * TAPER / LENGTH
LOG2E = math.log2(math.e)
CHUNK = 16
HALF = W // 2
FLOOR_INV = 1e18
KAPPA = DECAY * LOG2E
PEAK = KAPPA**6 / (4.0 * DECAY) * 2.0**KAPPA
SCALE = KAPPA / TAPER
COMPACT = 20.0 * KAPPA * KAPPA
RANGE = 1e15
TINY = 1e-12
GROUPS = 6


def split2(x):
    hi = x.astype(jnp.bfloat16)
    lo = (x - hi.astype(jnp.float32)).astype(jnp.bfloat16)
    return hi, lo


def split3(x):
    hi = x.astype(jnp.bfloat16)
    rest = x - hi.astype(jnp.float32)
    mid = rest.astype(jnp.bfloat16)
    lo = (rest - mid.astype(jnp.float32)).astype(jnp.bfloat16)
    return hi, mid, lo


def load_values(v_ref, src_ref, leaves, first):
    n = v_ref.shape[1] // 2
    for k in range(leaves):
        hi, lo = split2(src_ref[0:n, k * W : (k + 1) * W])
        v_ref[first + k] = jnp.concatenate([hi, lo], axis=0)


def split_rows(point, center, top, weight):
    x = (point - center) * SCALE
    sq = x * x
    sq = sq[0:1] + sq[1:2] + sq[2:3]
    row = lax.broadcasted_iota(jnp.int32, x.shape, 0)
    x = jnp.where(top, x * weight, jnp.where(row == 3, sq, 0.0))
    hi = x.astype(jnp.bfloat16).astype(jnp.float32)
    rest = x - hi
    mid = rest.astype(jnp.bfloat16).astype(jnp.float32)
    return hi, mid, rest - mid


def prepare_kernel(
    count_ref, base_ref, pairs_hbm, coords_hbm, order_hbm, b_hbm,
    listed_ref, pts_ref, cols_ref, v_ref, center_ref, wide_ref, edge_ref,
    pairs_ref, coords_ref, order_ref, b_ref, sems,
):
    copies = [
        pltpu.make_async_copy(pairs_hbm, pairs_ref, sems.at[0]),
        pltpu.make_async_copy(coords_hbm, coords_ref, sems.at[1]),
        pltpu.make_async_copy(order_hbm, order_ref, sems.at[2]),
        pltpu.make_async_copy(b_hbm, b_ref, sems.at[3]),
    ]
    for copy in copies:
        copy.start()
    copies[0].wait()
    slots = pairs_ref.shape[1]
    row = pairs_ref[0:1, :]
    place = (row - base_ref[0]) * STEPS + pairs_ref[1:2, :] - row
    live = lax.broadcasted_iota(jnp.int32, (1, slots), 1) < count_ref[0]
    place = jnp.where(live, place, -1)
    hit = lax.broadcasted_iota(jnp.int32, (slots, slots), 0) == place
    found = jnp.sum(hit.astype(jnp.float32), axis=1, keepdims=True)
    listed_ref[...] = jnp.broadcast_to(found.astype(jnp.bfloat16)[:, :, None], listed_ref.shape)
    for copy in copies[1:]:
        copy.wait()
    leaves = order_ref.shape[0]
    n = b_ref.shape[0]
    sub = lax.broadcasted_iota(jnp.int32, (W, W), 0).astype(jnp.float32).astype(jnp.bfloat16)
    one, zero = jnp.ones((W, W), jnp.bfloat16), jnp.zeros((W, W), jnp.bfloat16)
    dot = functools.partial(jnp.dot, preferred_element_type=jnp.float32)
    top = lax.broadcasted_iota(jnp.int32, (8, W), 0) < 3
    pad = jnp.zeros((5, W), jnp.float32)
    wide = jnp.zeros((8, W), jnp.float32)
    for k in range(leaves):
        at = slice(k * W, (k + 1) * W)
        order = order_ref[k : k + 1, :].astype(jnp.float32).astype(jnp.bfloat16)
        sel = jnp.where(sub == jnp.broadcast_to(order, (W, W)), one, zero)
        raw = jnp.concatenate([coords_ref[:, at], pad], axis=0)
        parts = dot(jnp.concatenate(split3(raw), axis=0), sel)
        point = parts[0:8] + parts[8:16] + parts[16:24]
        got = point[0:3]
        center = jnp.broadcast_to(jnp.sum(point, axis=1, keepdims=True) * (1.0 / W), (8, W))
        pts_ref[k] = point
        center_ref[k] = center
        hi, mid, lo = split_rows(point, center, top, 1.0)
        square = jnp.where(top, 0.0, hi + mid + lo)
        first = center if k == 0 else first
        far_off = jnp.abs(point - first) * (SCALE * COMPACT / RANGE)
        wide = jnp.maximum(wide, jnp.maximum(square, far_off))
        unit = jnp.where(lax.broadcasted_iota(jnp.int32, (8, W), 0) == 3, 1.0, 0.0)
        stack = [hi, jnp.where(top, hi, mid), jnp.where(top, hi, lo)]
        stack += [jnp.where(top, mid, unit), jnp.where(top, mid, unit), jnp.where(top, lo, unit)]
        cols_ref[k] = jnp.transpose(jnp.concatenate(stack, axis=0)).astype(jnp.bfloat16)
        if k < REACH:
            edge_ref[0:n, at] = b_ref[:, at]
            edge_ref[n : n + 3, at] = got
    wide_ref[...] = wide
    load_values(v_ref, b_ref, leaves, 0)


def spread_rows(bc_ref, points):
    cols = jnp.transpose(points)
    for c in range(3):
        bc_ref[:, c * HALF : (c + 1) * HALF] = jnp.broadcast_to(cols[:, c : c + 1], (W, HALF))


def far_squares(bc_ref, other):
    def block(rows, h):
        u = None
        for c in range(3):
            b = jnp.broadcast_to(other[c : c + 1, h * HALF : (h + 1) * HALF], (CHUNK, HALF))
            d = bc_ref[rows, c * HALF : (c + 1) * HALF] - b
            u = d * d if u is None else u + d * d
        return u * (SCALE * SCALE)

    return block


def near_squares(cols, other, center):
    top = lax.broadcasted_iota(jnp.int32, (8, W), 0) < 3
    one = jnp.where(lax.broadcasted_iota(jnp.int32, (8, W), 0) == 3, 1.0, 0.0)
    hi, mid, lo = split_rows(other, center, top, -2.0)
    stack = [jnp.where(top, hi, one), jnp.where(top, mid, one), jnp.where(top, lo, one)]
    stack += [hi, mid, jnp.where(top, hi, lo)]
    rows = jnp.concatenate(stack, axis=0).astype(jnp.bfloat16)
    all_u = jnp.dot(cols, rows, preferred_element_type=jnp.float32)
    return lambda rows, h: all_u[rows, h * HALF : (h + 1) * HALF]


def make_tile(t_ref, block, same):
    for k in range(W // CHUNK):
        rows = slice(k * CHUNK, (k + 1) * CHUNK)
        lower = k * CHUNK >= HALF
        for h in range(2):
            if same and lower and h == 0:
                t_ref[0, rows, :] = jnp.zeros((CHUNK, HALF), jnp.bfloat16)
                t_ref[2, rows, :] = jnp.zeros((CHUNK, HALF), jnp.bfloat16)
                continue
            u = jnp.minimum(jnp.maximum(block(rows, h), TINY), KAPPA * KAPPA)
            q = u * lax.rsqrt(u)
            t = KAPPA - q
            e = jnp.exp2(t)
            t = t * t
            t = t * t
            x = ((q + KAPPA / 4.0) * (q + KAPPA / DECAY)) * (t * e)
            if same and lower == bool(h):
                x = x * 0.5
            hi, lo = split2(x)
            t_ref[h, rows, :] = hi
            t_ref[2 + h, rows, :] = lo


def product(t_ref, v, listed, transposed):
    hi = jnp.concatenate([t_ref[0], t_ref[1]], axis=1)
    lo = jnp.concatenate([t_ref[2], t_ref[3]], axis=1)
    dims = (((1,), (1 if transposed else 0,)), ((), ()))
    dot = functools.partial(lax.dot_general, dimension_numbers=dims, preferred_element_type=jnp.float32)
    n = v.shape[0] // 2
    keep = jnp.concatenate([listed, listed], axis=1)
    v = v * jnp.concatenate([keep, keep], axis=0)
    p = dot(v, hi)
    return p[:n] + p[n:] + dot(v[:n], lo)


def products(t_ref, vi, vj, listed):
    return product(t_ref, vj, listed, True), product(t_ref, vi, listed, False)


def put_rows(out_ref, acc_ref, first, leaves, own_ref=None):
    for k in range(leaves):
        at = slice(k * W, (k + 1) * W)
        x = acc_ref[first + k] * (1.0 / PEAK)
        out_ref[:, at] = x if own_ref is None else x + NUGGET * own_ref[:, at]


def unrolled(start, stop, one):
    for i in range(start, stop):
        one(i, 0)


def evaluate_kernel(i0, i1, leaf_dev, last, listed_ref, pts_ref, cols_ref, v_ref, center_ref, wide_ref, *rest):
    rest = list(rest)
    far = i1 + REACH > leaf_dev
    shift_by = 0
    edge_ref = rest.pop(0) if far else None
    own_ref = rest.pop(0) if last else None
    prev_ref = rest.pop(0) if i0 else None
    tiles_ref = rest.pop(0)
    acc_ref = rest.pop(1 if last else 0)
    rows_ref = rest.pop(0) if last or far else None
    bc_ref = rest.pop(0)
    compact = jnp.max(wide_ref[...]) <= COMPACT
    if far:
        pts_all, v_all = rest
        n = v_ref.shape[1] // 2
        own = leaf_dev - i0
        pts_all[0:own] = pts_ref[i0:leaf_dev]
        v_all[0:own] = v_ref[i0:leaf_dev]
        first = center_ref[leaf_dev - 1, 0:3, :]
        pts_all[own:] = jnp.zeros_like(pts_all[own:])
        for k in range(REACH):
            got = edge_ref[n : n + 3, k * W : (k + 1) * W]
            pts_all[own + k, 0:3, :] = got
            far_off = jnp.abs(got - first) * (SCALE * COMPACT / RANGE)
            wide = far_off if k == 0 else jnp.maximum(wide, far_off)
        load_values(v_all, edge_ref, REACH, own)
        compact = compact & (jnp.max(wide) <= COMPACT)
        pts_ref, v_ref = pts_all, v_all
        shift_by = i0
    if i0:
        acc_ref[...] = prev_ref[...]
    else:
        acc_ref[...] = jnp.zeros_like(acc_ref)

    def finish(i, slot):
        to_row, to_col = products(
            tiles_ref.at[slot], v_ref[i - shift_by], v_ref[i + REACH - shift_by], listed_ref[i * STEPS + REACH]
        )
        acc_ref[i] += to_row
        acc_ref[i + REACH] += to_col

    def near_leaf(i, _):
        slot = (i - i0) * STEPS
        cols = cols_ref[i]
        center = center_ref[i]
        vi = v_ref[i - shift_by]

        def make(d):
            block = near_squares(cols, pts_ref[i + d - shift_by], center)
            make_tile(tiles_ref.at[slot + (1 + d)], block, d == 0)

        make(0)
        if i > i0:
            finish(i - 1, slot)
        total = None
        for d in range(REACH):
            make(d + 1)
            to_row, to_col = products(
                tiles_ref.at[slot + (1 + d)], vi, v_ref[i + d - shift_by], listed_ref[i * STEPS + d]
            )
            total = to_row if total is None else total + to_row
            acc_ref[i + d] += to_col
        acc_ref[i] += total
        return 0

    def far_leaf(i, _):
        slot = (i - i0) * STEPS
        spread_rows(bc_ref, pts_ref[i - shift_by])

        def step(d, _):
            t_ref = tiles_ref.at[slot + (1 + d)]
            block = far_squares(bc_ref, pts_ref.at[i + d - shift_by])
            lax.cond(d == 0, lambda: make_tile(t_ref, block, True), lambda: make_tile(t_ref, block, False))

            @pl.when(d < REACH)
            def _():
                to_row, to_col = products(
                    t_ref, v_ref[i - shift_by], v_ref[i + d - shift_by], listed_ref[i * STEPS + d]
                )
                acc_ref[i] += to_row
                acc_ref[i + d] += to_col

            return 0

        @pl.when(i > i0)
        def _():
            finish(i - 1, slot)

        return lax.fori_loop(0, STEPS, step, 0)

    @pl.when(compact)
    def _():
        unrolled(i0, i1, near_leaf)

    @pl.when(jnp.logical_not(compact))
    def _():
        lax.fori_loop(i0, i1, far_leaf, 0)

    finish(i1 - 1, (i1 - i0) * STEPS)
    if far:
        put_rows(rows_ref, acc_ref, leaf_dev, REACH)
    if last:
        put_rows(rows_ref, acc_ref, 0, leaf_dev, own_ref)


def clear_or_copy(acc_ref, prev_ref):
    acc_ref[...] = jnp.zeros_like(acc_ref) if prev_ref is None else prev_ref[...]


def weighted(acc_ref, field_ref, first, leaves):
    total = acc_ref[first] * field_ref[:, 0:W]
    for k in range(1, leaves):
        total += acc_ref[first + k] * field_ref[:, k * W : (k + 1) * W]
    return total


def apply_kernel(i0, i1, leaf_dev, last, listed_ref, tiles_ref, w_ref, *rest):
    rest = list(rest)
    if last:
        far_ref, extra_ref = rest.pop(0), rest.pop(0)
    prev_ref = rest.pop(0) if i0 else None
    acc_ref = rest.pop(0)
    dots_ref = rest.pop(0) if last else None
    v_ref = rest.pop(0)
    load_values(v_ref, w_ref, leaf_dev, 0)
    clear_or_copy(acc_ref, prev_ref)

    def one_leaf(i, _):
        slot = (i - i0) * STEPS
        vi = v_ref[i]
        total = None
        for d in range(STEPS):
            to_row, to_col = products(
                tiles_ref.at[slot + (1 + d)], vi, v_ref[i + d], listed_ref[i * STEPS + d]
            )
            total = to_row if total is None else total + to_row
            acc_ref[i + d] += to_col
        acc_ref[i] += total
        return 0

    unrolled(i0, i1, one_leaf)
    if last:
        total = weighted(acc_ref, w_ref, 0, leaf_dev) + weighted(acc_ref, far_ref, leaf_dev, REACH)
        dots_ref[...] = (total + extra_ref[...]) * (1.0 / PEAK)


def edge_kernel(i0, leaf_dev, listed_ref, tiles_ref, w_ref, far_ref, prev_ref, acc_ref, send_ref, dots_ref, v_ref, part_ref):
    held = leaf_dev - i0
    load_values(v_ref, w_ref, leaf_dev, 0)
    clear_or_copy(part_ref, None)

    def one_leaf(i, _):
        slot = (i - i0) * STEPS
        vi = v_ref[i]
        for d in range(STEPS):
            part_ref[i - i0 + d] += product(
                tiles_ref.at[slot + (1 + d)], vi, listed_ref[i * STEPS + d], False
            )
        return 0

    unrolled(i0, leaf_dev, one_leaf)
    dots_ref[...] = weighted(part_ref, w_ref.at[:, i0 * W :], 0, held) + weighted(part_ref, far_ref, held, REACH)
    acc_ref[...] = prev_ref[...]
    for k in range(held + REACH):
        acc_ref[i0 + k] += part_ref[k]
    put_rows(send_ref, acc_ref, leaf_dev, REACH)


def finish_kernel(
    i0, leaf_dev, listed_ref, tiles_hbm, w_ref, far_ref, prev_ref, rows_ref, v_ref, acc_ref, tiles_ref, sems
):
    copies = []
    for k in range(leaf_dev - i0):
        at = pl.ds(k * STEPS, STEPS)
        copies.append(pltpu.make_async_copy(tiles_hbm.at[pl.ds(k * STEPS + 1, STEPS)], tiles_ref.at[at], sems.at[k]))
    copies[0].start()
    load_values(v_ref, w_ref.at[:, i0 * W :], leaf_dev - i0, 0)
    load_values(v_ref, far_ref, REACH, leaf_dev - i0)
    acc_ref[...] = prev_ref[...]
    copies[1].start()
    for k, copy in enumerate(copies):
        copy.wait()
        if k + 2 < len(copies):
            copies[k + 2].start()
        total = None
        for d in range(STEPS):
            to_row = product(tiles_ref.at[k * STEPS + d], v_ref[k + d], listed_ref[(i0 + k) * STEPS + d], True)
            total = to_row if total is None else total + to_row
        acc_ref[i0 + k] += total
    put_rows(rows_ref, acc_ref, 0, leaf_dev, w_ref)


VM = pl.BlockSpec(memory_space=pltpu.VMEM)
SM = pl.BlockSpec(memory_space=pltpu.SMEM)
HBM = pl.BlockSpec(memory_space=pltpu.HBM)
PARAMS = pltpu.CompilerParams(vmem_limit_bytes=8 << 20)


def prepare_call(pairs, count, base, coords, order, b):
    leaves = order.shape[0]
    n = b.shape[0]
    return pl.pallas_call(
        prepare_kernel,
        out_shape=(
            jax.ShapeDtypeStruct((pairs.shape[1], 16, HALF), jnp.bfloat16),
            jax.ShapeDtypeStruct((leaves, 8, W), jnp.float32),
            jax.ShapeDtypeStruct((leaves, W, 8 * GROUPS), jnp.bfloat16),
            jax.ShapeDtypeStruct((leaves, 2 * n, W), jnp.bfloat16),
            jax.ShapeDtypeStruct((leaves, 8, W), jnp.float32),
            jax.ShapeDtypeStruct((8, W), jnp.float32),
            jax.ShapeDtypeStruct((n + 3, REACH * W), jnp.float32),
        ),
        in_specs=[SM, SM, HBM, HBM, HBM, HBM],
        out_specs=(VM,) * 7,
        scratch_shapes=[
            pltpu.VMEM(pairs.shape, jnp.int32),
            pltpu.VMEM(coords.shape, jnp.float32),
            pltpu.VMEM(order.shape, jnp.int32),
            pltpu.VMEM(b.shape, jnp.float32),
            pltpu.SemaphoreType.DMA((4,)),
        ],
        compiler_params=PARAMS,
        name="prepare",
    )(count, base, *(pltpu.with_memory_space_constraint(x, pltpu.HBM) for x in (pairs, coords, order, b)))


def shapes_out(leaf_dev, n, far, last):
    acc = (leaf_dev + REACH, n, W)
    rows = (n, (leaf_dev if last else REACH) * W)
    f32 = jnp.float32
    if last:
        return [jax.ShapeDtypeStruct(rows, f32)], [pltpu.VMEM(acc, f32)]
    return [jax.ShapeDtypeStruct(acc, f32)] + ([jax.ShapeDtypeStruct(rows, f32)] if far else []), []


def evaluate_call(i0, i1, leaf_dev, n, prepared, far, own, prev):
    tiles = (i1 - i0) * STEPS
    last = own is not None
    ops = [*prepared, *far, *([own] if last else []), *([] if prev is None else [prev])]
    outs, held_acc = shapes_out(leaf_dev, n, bool(far), last)
    scratch = [*held_acc, pltpu.VMEM((W, 3 * HALF), jnp.float32)]
    if far:
        held = leaf_dev - i0 + REACH
        scratch += [pltpu.VMEM((held, 8, W), jnp.float32), pltpu.VMEM((held, 2 * n, W), jnp.bfloat16)]
    outs = [jax.ShapeDtypeStruct((tiles + 1, 4, W, HALF), jnp.bfloat16), *outs]
    return pl.pallas_call(
        functools.partial(evaluate_kernel, i0, i1, leaf_dev, last),
        out_shape=outs,
        in_specs=[VM] * len(ops),
        out_specs=[VM] * len(outs),
        scratch_shapes=scratch,
        compiler_params=PARAMS,
        cost_estimate=pl.CostEstimate(flops=tiles << 28, transcendentals=tiles << 17, bytes_accessed=tiles << 18),
        name=f"evaluate_{i0}",
    )(*ops)


def small_call(kernel, name, outs, scratch, tiles, ops, in_hbm=()):
    return pl.pallas_call(
        kernel,
        out_shape=[jax.ShapeDtypeStruct(shape, jnp.float32) for shape in outs],
        in_specs=[HBM if k in in_hbm else VM for k in range(len(ops))],
        out_specs=[VM] * len(outs),
        scratch_shapes=scratch,
        compiler_params=pltpu.CompilerParams(vmem_limit_bytes=18 << 20) if in_hbm else PARAMS,
        cost_estimate=pl.CostEstimate(flops=tiles.shape[0] << 27, transcendentals=0, bytes_accessed=tiles.size * 2),
        name=name,
    )(*[pltpu.with_memory_space_constraint(x, pltpu.HBM) if k in in_hbm else x for k, x in enumerate(ops)])


def apply_call(i0, i1, leaf_dev, n, listed, tiles, own, last, prev):
    acc = (leaf_dev + REACH, n, W)
    ops = [listed, tiles, own, *last, *([] if prev is None else [prev])]
    return small_call(
        functools.partial(apply_kernel, i0, i1, leaf_dev, bool(last)),
        f"apply_{i0}",
        [acc, (n, W)] if last else [acc],
        [pltpu.VMEM((leaf_dev, 2 * n, W), jnp.bfloat16)],
        tiles,
        ops,
    )


def edge_call(i0, leaf_dev, n, listed, tiles, own, far, prev):
    acc = (leaf_dev + REACH, n, W)
    return small_call(
        functools.partial(edge_kernel, i0, leaf_dev),
        "apply_edge",
        [acc, (n, REACH * W), (n, W)],
        [
            pltpu.VMEM((leaf_dev, 2 * n, W), jnp.bfloat16),
            pltpu.VMEM((leaf_dev - i0 + REACH, n, W), jnp.float32),
        ],
        tiles,
        [listed, tiles, own, far, prev],
    )


def finish_call(i0, leaf_dev, n, listed, tiles, own, far, prev):
    acc = (leaf_dev + REACH, n, W)
    return small_call(
        functools.partial(finish_kernel, i0, leaf_dev),
        "finish",
        [own.shape],
        [
            pltpu.VMEM((leaf_dev - i0 + REACH, 2 * n, W), jnp.bfloat16),
            pltpu.VMEM(acc, jnp.float32),
            pltpu.VMEM((tiles.shape[0] - 1, *tiles.shape[1:]), jnp.bfloat16),
            pltpu.SemaphoreType.DMA((leaf_dev - i0,)),
        ],
        tiles,
        [listed, tiles, own, far, prev],
        in_hbm=(1,),
    )[0]


def shift(value, by):
    length = lax.axis_size("leaf")
    return lax.ppermute(value, "leaf", [(i, i + by) for i in range(length) if 0 <= i + by < length])


def sum_over_leaf(value):
    length = lax.axis_size("leaf")
    value = value + lax.ppermute(value, "leaf", [(i, i ^ 1) for i in range(length)])
    copies = jnp.broadcast_to(value.reshape(-1), (length // 2, value.size))
    groups = [[i for i in range(length) if i % 2 == c] for c in range(2)]
    got = lax.all_to_all(
        copies, "leaf", split_axis=0, concat_axis=0, tiled=True, axis_index_groups=groups
    )
    return jnp.sum(got, axis=0).reshape(value.shape)


def body(coords, site_order, leaf_pairs, pair_count, probes):
    leaf_dev, width = site_order.shape
    n = probes.shape[0]
    edge = REACH * width
    base = (lax.axis_index("leaf") * leaf_dev).astype(jnp.int32).reshape(1)
    *prepared, packed = prepare_call(leaf_pairs, pair_count, base, coords, site_order, probes)
    far = shift(packed, -1)
    cut0, cut1 = leaf_dev - REACH - 5, leaf_dev - REACH - 2
    evaluate = functools.partial(evaluate_call, leaf_dev=leaf_dev, n=n, prepared=prepared)
    tiles0, acc = evaluate(0, cut0, far=(), own=None, prev=None)
    tiles1, acc, send = evaluate(cut1, leaf_dev, far=(far,), own=None, prev=acc)
    back = shift(send, 1)
    tiles2, image = evaluate(cut0, cut1, far=(), own=probes, prev=acc)
    image = jnp.concatenate([image[:, :edge] + back, image[:, edge:]], axis=1)

    image_far = shift(image[:, :edge], -1)
    common = dict(leaf_dev=leaf_dev, n=n, listed=prepared[0], own=image)
    (acc,) = apply_call(0, cut0, tiles=tiles0, last=(), prev=None, **common)
    acc, send, edge_dots = edge_call(cut1, tiles=tiles1, far=image_far, prev=acc, **common)
    back = shift(send, 1)
    acc, dots = apply_call(cut0, cut1, tiles=tiles2, last=(image_far, edge_dots), prev=acc, **common)
    square = jnp.sum(image * image, axis=1)
    sums = jnp.stack(
        [
            jnp.sum(probes * probes, axis=1),
            jnp.sum(probes * image, axis=1),
            square,
            jnp.sum(dots, axis=1) + NUGGET * square,
        ]
    )
    image2 = finish_call(cut1, tiles=tiles1, far=image_far, prev=acc, **common)
    image2 = jnp.concatenate([image2[:, :edge] + back, image2[:, edge:]], axis=1)
    rr, bw, ww, wz = sum_over_leaf(sums)
    alpha = rr / bw
    rr1 = rr - 2.0 * alpha * bw + alpha * alpha * ww
    beta = rr1 / rr
    g = 1.0 + beta
    curve = g * g * bw - 2.0 * g * alpha * ww + alpha * alpha * wz
    alpha1 = rr1 / curve
    c = lambda x: x[:, None]
    direction1 = c(g) * probes - c(alpha) * image
    image1 = c(g) * image - c(alpha) * image2
    solution = c(alpha) * probes + c(alpha1) * direction1
    residual = probes - c(alpha) * image - c(alpha1) * image1
    return solution, residual


def solution(mesh):
    in_specs = (P(None, "leaf"), P("leaf", None), P(None, "leaf"), P("leaf"), P("probe", "leaf"))
    out_specs = (P("probe", "leaf"), P("probe", "leaf"))
    return jax.shard_map(body, mesh=mesh, in_specs=in_specs, out_specs=out_specs, check_vma=False)
```

```python
import functools
import math

import jax
import jax.numpy as jnp
from jax import lax
from jax.experimental import pallas as pl
from jax.experimental.pallas import tpu as pltpu
from jax.sharding import PartitionSpec as P

REACH = 5
STEPS = REACH + 1
UNIT = 0.025
LENGTH = 0.12
NUGGET = 0.5
W = 256
TAPER = REACH * UNIT
DECAY = math.sqrt(3.0) * TAPER / LENGTH
LOG2E = math.log2(math.e)
CHUNK = 16
HALF = W // 2
FLOOR_INV = 1e18
KAPPA = DECAY * LOG2E
PEAK = KAPPA**6 / (4.0 * DECAY) * 2.0**KAPPA
SCALE = KAPPA / TAPER
COMPACT = 20.0 * KAPPA * KAPPA
RANGE = 1e15
TINY = 1e-12
GROUPS = 6


def split2(x):
    hi = x.astype(jnp.bfloat16)
    lo = (x - hi.astype(jnp.float32)).astype(jnp.bfloat16)
    return hi, lo


def split3(x):
    hi = x.astype(jnp.bfloat16)
    rest = x - hi.astype(jnp.float32)
    mid = rest.astype(jnp.bfloat16)
    lo = (rest - mid.astype(jnp.float32)).astype(jnp.bfloat16)
    return hi, mid, lo


def load_values(v_ref, src_ref, leaves, first):
    n = v_ref.shape[1] // 2
    for k in range(leaves):
        hi, lo = split2(src_ref[0:n, k * W : (k + 1) * W])
        v_ref[first + k] = jnp.concatenate([hi, lo], axis=0)


def split_rows(point, center, top, weight):
    x = (point - center) * SCALE
    sq = x * x
    sq = sq[0:1] + sq[1:2] + sq[2:3]
    row = lax.broadcasted_iota(jnp.int32, x.shape, 0)
    x = jnp.where(top, x * weight, jnp.where(row == 3, sq, 0.0))
    hi = x.astype(jnp.bfloat16).astype(jnp.float32)
    rest = x - hi
    mid = rest.astype(jnp.bfloat16).astype(jnp.float32)
    return hi, mid, rest - mid


def prepare_kernel(
    count_ref, base_ref, pairs_hbm, coords_hbm, order_hbm, b_hbm,
    listed_ref, pts_ref, cols_ref, v_ref, center_ref, wide_ref, edge_ref,
    pairs_ref, coords_ref, order_ref, b_ref, sems,
):
    copies = [
        pltpu.make_async_copy(pairs_hbm, pairs_ref, sems.at[0]),
        pltpu.make_async_copy(coords_hbm, coords_ref, sems.at[1]),
        pltpu.make_async_copy(order_hbm, order_ref, sems.at[2]),
        pltpu.make_async_copy(b_hbm, b_ref, sems.at[3]),
    ]
    for copy in copies:
        copy.start()
    copies[0].wait()
    slots = pairs_ref.shape[1]
    row = pairs_ref[0:1, :]
    place = (row - base_ref[0]) * STEPS + pairs_ref[1:2, :] - row
    live = lax.broadcasted_iota(jnp.int32, (1, slots), 1) < count_ref[0]
    place = jnp.where(live, place, -1)
    hit = lax.broadcasted_iota(jnp.int32, (slots, slots), 0) == place
    found = jnp.sum(hit.astype(jnp.float32), axis=1, keepdims=True)
    listed_ref[...] = jnp.broadcast_to(found.astype(jnp.bfloat16)[:, :, None], listed_ref.shape)
    for copy in copies[1:]:
        copy.wait()
    leaves = order_ref.shape[0]
    n = b_ref.shape[0]
    sub = lax.broadcasted_iota(jnp.int32, (W, W), 0).astype(jnp.float32).astype(jnp.bfloat16)
    one, zero = jnp.ones((W, W), jnp.bfloat16), jnp.zeros((W, W), jnp.bfloat16)
    dot = functools.partial(jnp.dot, preferred_element_type=jnp.float32)
    top = lax.broadcasted_iota(jnp.int32, (8, W), 0) < 3
    pad = jnp.zeros((5, W), jnp.float32)
    wide = jnp.zeros((8, W), jnp.float32)
    for k in range(leaves):
        at = slice(k * W, (k + 1) * W)
        order = order_ref[k : k + 1, :].astype(jnp.float32).astype(jnp.bfloat16)
        sel = jnp.where(sub == jnp.broadcast_to(order, (W, W)), one, zero)
        raw = jnp.concatenate([coords_ref[:, at], pad], axis=0)
        parts = dot(jnp.concatenate(split3(raw), axis=0), sel)
        point = parts[0:8] + parts[8:16] + parts[16:24]
        got = point[0:3]
        center = jnp.broadcast_to(jnp.sum(point, axis=1, keepdims=True) * (1.0 / W), (8, W))
        pts_ref[k] = point
        center_ref[k] = center
        hi, mid, lo = split_rows(point, center, top, 1.0)
        square = jnp.where(top, 0.0, hi + mid + lo)
        first = center if k == 0 else first
        far_off = jnp.abs(point - first) * (SCALE * COMPACT / RANGE)
        wide = jnp.maximum(wide, jnp.maximum(square, far_off))
        unit = jnp.where(lax.broadcasted_iota(jnp.int32, (8, W), 0) == 3, 1.0, 0.0)
        stack = [hi, jnp.where(top, hi, mid), jnp.where(top, hi, lo)]
        stack += [jnp.where(top, mid, unit), jnp.where(top, mid, unit), jnp.where(top, lo, unit)]
        cols_ref[k] = jnp.transpose(jnp.concatenate(stack, axis=0)).astype(jnp.bfloat16)
        if k < REACH:
            edge_ref[0:n, at] = b_ref[:, at]
            edge_ref[n : n + 3, at] = got
    wide_ref[...] = wide
    load_values(v_ref, b_ref, leaves, 0)


def spread_rows(bc_ref, points):
    cols = jnp.transpose(points)
    for c in range(3):
        bc_ref[:, c * HALF : (c + 1) * HALF] = jnp.broadcast_to(cols[:, c : c + 1], (W, HALF))


def far_squares(bc_ref, other):
    def block(rows, h):
        u = None
        for c in range(3):
            b = jnp.broadcast_to(other[c : c + 1, h * HALF : (h + 1) * HALF], (CHUNK, HALF))
            d = bc_ref[rows, c * HALF : (c + 1) * HALF] - b
            u = d * d if u is None else u + d * d
        return u * (SCALE * SCALE)

    return block


def near_squares(cols, other, center):
    top = lax.broadcasted_iota(jnp.int32, (8, W), 0) < 3
    one = jnp.where(lax.broadcasted_iota(jnp.int32, (8, W), 0) == 3, 1.0, 0.0)
    hi, mid, lo = split_rows(other, center, top, -2.0)
    stack = [jnp.where(top, hi, one), jnp.where(top, mid, one), jnp.where(top, lo, one)]
    stack += [hi, mid, jnp.where(top, hi, lo)]
    rows = jnp.concatenate(stack, axis=0).astype(jnp.bfloat16)
    all_u = jnp.dot(cols, rows, preferred_element_type=jnp.float32)
    return lambda rows, h: all_u[rows, h * HALF : (h + 1) * HALF]


def make_tile(t_ref, block, same):
    for k in range(W // CHUNK):
        rows = slice(k * CHUNK, (k + 1) * CHUNK)
        lower = k * CHUNK >= HALF
        for h in range(2):
            if same and lower and h == 0:
                t_ref[0, rows, :] = jnp.zeros((CHUNK, HALF), jnp.bfloat16)
                t_ref[2, rows, :] = jnp.zeros((CHUNK, HALF), jnp.bfloat16)
                continue
            u = jnp.minimum(jnp.maximum(block(rows, h), TINY), KAPPA * KAPPA)
            q = u * lax.rsqrt(u)
            t = KAPPA - q
            e = jnp.exp2(t)
            t = t * t
            t = t * t
            x = ((q + KAPPA / 4.0) * (q + KAPPA / DECAY)) * (t * e)
            if same and lower == bool(h):
                x = x * 0.5
            hi, lo = split2(x)
            t_ref[h, rows, :] = hi
            t_ref[2 + h, rows, :] = lo


def product(t_ref, v, listed, transposed):
    hi = jnp.concatenate([t_ref[0], t_ref[1]], axis=1)
    lo = jnp.concatenate([t_ref[2], t_ref[3]], axis=1)
    dims = (((1,), (1 if transposed else 0,)), ((), ()))
    dot = functools.partial(lax.dot_general, dimension_numbers=dims, preferred_element_type=jnp.float32)
    n = v.shape[0] // 2
    keep = jnp.concatenate([listed, listed], axis=1)
    v = v * jnp.concatenate([keep, keep], axis=0)
    p = dot(v, hi)
    return p[:n] + p[n:] + dot(v[:n], lo)


def products(t_ref, vi, vj, listed):
    return product(t_ref, vj, listed, True), product(t_ref, vi, listed, False)


def put_rows(out_ref, acc_ref, first, leaves, own_ref=None):
    for k in range(leaves):
        at = slice(k * W, (k + 1) * W)
        x = acc_ref[first + k] * (1.0 / PEAK)
        out_ref[:, at] = x if own_ref is None else x + NUGGET * own_ref[:, at]


def evaluate_kernel(i0, i1, leaf_dev, last, listed_ref, pts_ref, cols_ref, v_ref, center_ref, wide_ref, *rest):
    rest = list(rest)
    far = i1 + REACH > leaf_dev
    shift_by = 0
    edge_ref = rest.pop(0) if far else None
    own_ref = rest.pop(0) if last else None
    prev_ref = rest.pop(0) if i0 else None
    tiles_ref = rest.pop(0)
    acc_ref = rest.pop(1 if last else 0)
    rows_ref = rest.pop(0) if last or far else None
    bc_ref = rest.pop(0)
    compact = jnp.max(wide_ref[...]) <= COMPACT
    if far:
        pts_all, v_all = rest
        n = v_ref.shape[1] // 2
        own = leaf_dev - i0
        pts_all[0:own] = pts_ref[i0:leaf_dev]
        v_all[0:own] = v_ref[i0:leaf_dev]
        first = center_ref[leaf_dev - 1, 0:3, :]
        pts_all[own:] = jnp.zeros_like(pts_all[own:])
        for k in range(REACH):
            got = edge_ref[n : n + 3, k * W : (k + 1) * W]
            pts_all[own + k, 0:3, :] = got
            far_off = jnp.abs(got - first) * (SCALE * COMPACT / RANGE)
            wide = far_off if k == 0 else jnp.maximum(wide, far_off)
        load_values(v_all, edge_ref, REACH, own)
        compact = compact & (jnp.max(wide) <= COMPACT)
        pts_ref, v_ref = pts_all, v_all
        shift_by = i0
    if i0:
        acc_ref[...] = prev_ref[...]
    else:
        acc_ref[...] = jnp.zeros_like(acc_ref)
    tiles_ref[0] = jnp.zeros_like(tiles_ref[0])

    def finish(i, slot):
        to_row, to_col = products(
            tiles_ref.at[slot], v_ref[i - shift_by], v_ref[i + REACH - shift_by], listed_ref[i * STEPS + REACH]
        )
        acc_ref[i] += to_row
        acc_ref[i + REACH] += to_col

    def near_leaf(i, _):
        slot = (i - i0) * STEPS
        cols = cols_ref[i]
        center = center_ref[i]
        vi = v_ref[i - shift_by]

        def make(d):
            block = near_squares(cols, pts_ref[i + d - shift_by], center)
            make_tile(tiles_ref.at[slot + (1 + d)], block, d == 0)

        make(0)
        finish(jnp.maximum(i - 1, i0), slot)
        total = None
        for d in range(REACH):
            make(d + 1)
            to_row, to_col = products(
                tiles_ref.at[slot + (1 + d)], vi, v_ref[i + d - shift_by], listed_ref[i * STEPS + d]
            )
            total = to_row if total is None else total + to_row
            acc_ref[i + d] += to_col
        acc_ref[i] += total
        return 0

    def far_leaf(i, _):
        slot = (i - i0) * STEPS
        spread_rows(bc_ref, pts_ref[i - shift_by])

        def step(d, _):
            t_ref = tiles_ref.at[slot + (1 + d)]
            block = far_squares(bc_ref, pts_ref.at[i + d - shift_by])
            lax.cond(d == 0, lambda: make_tile(t_ref, block, True), lambda: make_tile(t_ref, block, False))

            @pl.when(d < REACH)
            def _():
                to_row, to_col = products(
                    t_ref, v_ref[i - shift_by], v_ref[i + d - shift_by], listed_ref[i * STEPS + d]
                )
                acc_ref[i] += to_row
                acc_ref[i + d] += to_col

            return 0

        @pl.when(i > i0)
        def _():
            finish(i - 1, slot)

        return lax.fori_loop(0, STEPS, step, 0)

    @pl.when(compact)
    def _():
        lax.fori_loop(i0, i1, near_leaf, 0)

    @pl.when(jnp.logical_not(compact))
    def _():
        lax.fori_loop(i0, i1, far_leaf, 0)

    finish(i1 - 1, (i1 - i0) * STEPS)
    if far:
        put_rows(rows_ref, acc_ref, leaf_dev, REACH)
    if last:
        put_rows(rows_ref, acc_ref, 0, leaf_dev, own_ref)


def clear_or_copy(acc_ref, prev_ref):
    acc_ref[...] = jnp.zeros_like(acc_ref) if prev_ref is None else prev_ref[...]


def weighted(acc_ref, field_ref, first, leaves):
    total = acc_ref[first] * field_ref[:, 0:W]
    for k in range(1, leaves):
        total += acc_ref[first + k] * field_ref[:, k * W : (k + 1) * W]
    return total


def unrolled(start, stop, one):
    for i in range(start, stop):
        one(i, 0)


def apply_kernel(i0, i1, leaf_dev, last, listed_ref, tiles_ref, w_ref, *rest):
    rest = list(rest)
    if last:
        far_ref, extra_ref = rest.pop(0), rest.pop(0)
    prev_ref = rest.pop(0) if i0 else None
    acc_ref = rest.pop(0)
    dots_ref = rest.pop(0) if last else None
    v_ref = rest.pop(0)
    load_values(v_ref, w_ref, leaf_dev, 0)
    clear_or_copy(acc_ref, prev_ref)

    def one_leaf(i, _):
        slot = (i - i0) * STEPS
        vi = v_ref[i]
        total = None
        for d in range(STEPS):
            to_row, to_col = products(
                tiles_ref.at[slot + (1 + d)], vi, v_ref[i + d], listed_ref[i * STEPS + d]
            )
            total = to_row if total is None else total + to_row
            acc_ref[i + d] += to_col
        acc_ref[i] += total
        return 0

    unrolled(i0, i1, one_leaf)
    if last:
        total = weighted(acc_ref, w_ref, 0, leaf_dev) + weighted(acc_ref, far_ref, leaf_dev, REACH)
        dots_ref[...] = (total + extra_ref[...]) * (1.0 / PEAK)


def edge_kernel(i0, leaf_dev, listed_ref, tiles_ref, w_ref, far_ref, prev_ref, acc_ref, send_ref, dots_ref, v_ref, part_ref):
    held = leaf_dev - i0
    load_values(v_ref, w_ref, leaf_dev, 0)
    clear_or_copy(part_ref, None)

    def one_leaf(i, _):
        slot = (i - i0) * STEPS
        vi = v_ref[i]
        for d in range(STEPS):
            part_ref[i - i0 + d] += product(
                tiles_ref.at[slot + (1 + d)], vi, listed_ref[i * STEPS + d], False
            )
        return 0

    unrolled(i0, leaf_dev, one_leaf)
    dots_ref[...] = weighted(part_ref, w_ref.at[:, i0 * W :], 0, held) + weighted(part_ref, far_ref, held, REACH)
    acc_ref[...] = prev_ref[...]
    for k in range(held + REACH):
        acc_ref[i0 + k] += part_ref[k]
    put_rows(send_ref, acc_ref, leaf_dev, REACH)


def finish_kernel(
    i0, leaf_dev, listed_ref, tiles_hbm, w_ref, far_ref, prev_ref, rows_ref, v_ref, acc_ref, tiles_ref, sems
):
    copies = []
    for k in range(leaf_dev - i0):
        at = pl.ds(k * STEPS, STEPS)
        copies.append(pltpu.make_async_copy(tiles_hbm.at[pl.ds(k * STEPS + 1, STEPS)], tiles_ref.at[at], sems.at[k]))
    copies[0].start()
    load_values(v_ref, w_ref.at[:, i0 * W :], leaf_dev - i0, 0)
    load_values(v_ref, far_ref, REACH, leaf_dev - i0)
    acc_ref[...] = prev_ref[...]
    copies[1].start()
    for k, copy in enumerate(copies):
        copy.wait()
        if k + 2 < len(copies):
            copies[k + 2].start()
        total = None
        for d in range(STEPS):
            to_row = product(tiles_ref.at[k * STEPS + d], v_ref[k + d], listed_ref[(i0 + k) * STEPS + d], True)
            total = to_row if total is None else total + to_row
        acc_ref[i0 + k] += total
    put_rows(rows_ref, acc_ref, 0, leaf_dev, w_ref)


VM = pl.BlockSpec(memory_space=pltpu.VMEM)
SM = pl.BlockSpec(memory_space=pltpu.SMEM)
HBM = pl.BlockSpec(memory_space=pltpu.HBM)
PARAMS = pltpu.CompilerParams(vmem_limit_bytes=8 << 20)


def prepare_call(pairs, count, base, coords, order, b):
    leaves = order.shape[0]
    n = b.shape[0]
    return pl.pallas_call(
        prepare_kernel,
        out_shape=(
            jax.ShapeDtypeStruct((pairs.shape[1], 16, HALF), jnp.bfloat16),
            jax.ShapeDtypeStruct((leaves, 8, W), jnp.float32),
            jax.ShapeDtypeStruct((leaves, W, 8 * GROUPS), jnp.bfloat16),
            jax.ShapeDtypeStruct((leaves, 2 * n, W), jnp.bfloat16),
            jax.ShapeDtypeStruct((leaves, 8, W), jnp.float32),
            jax.ShapeDtypeStruct((8, W), jnp.float32),
            jax.ShapeDtypeStruct((n + 3, REACH * W), jnp.float32),
        ),
        in_specs=[SM, SM, HBM, HBM, HBM, HBM],
        out_specs=(VM,) * 7,
        scratch_shapes=[
            pltpu.VMEM(pairs.shape, jnp.int32),
            pltpu.VMEM(coords.shape, jnp.float32),
            pltpu.VMEM(order.shape, jnp.int32),
            pltpu.VMEM(b.shape, jnp.float32),
            pltpu.SemaphoreType.DMA((4,)),
        ],
        compiler_params=PARAMS,
        name="prepare",
    )(count, base, *(pltpu.with_memory_space_constraint(x, pltpu.HBM) for x in (pairs, coords, order, b)))


def shapes_out(leaf_dev, n, far, last):
    acc = (leaf_dev + REACH, n, W)
    rows = (n, (leaf_dev if last else REACH) * W)
    f32 = jnp.float32
    if last:
        return [jax.ShapeDtypeStruct(rows, f32)], [pltpu.VMEM(acc, f32)]
    return [jax.ShapeDtypeStruct(acc, f32)] + ([jax.ShapeDtypeStruct(rows, f32)] if far else []), []


def evaluate_call(i0, i1, leaf_dev, n, prepared, far, own, prev):
    tiles = (i1 - i0) * STEPS
    last = own is not None
    ops = [*prepared, *far, *([own] if last else []), *([] if prev is None else [prev])]
    outs, held_acc = shapes_out(leaf_dev, n, bool(far), last)
    scratch = [*held_acc, pltpu.VMEM((W, 3 * HALF), jnp.float32)]
    if far:
        held = leaf_dev - i0 + REACH
        scratch += [pltpu.VMEM((held, 8, W), jnp.float32), pltpu.VMEM((held, 2 * n, W), jnp.bfloat16)]
    outs = [jax.ShapeDtypeStruct((tiles + 1, 4, W, HALF), jnp.bfloat16), *outs]
    return pl.pallas_call(
        functools.partial(evaluate_kernel, i0, i1, leaf_dev, last),
        out_shape=outs,
        in_specs=[VM] * len(ops),
        out_specs=[VM] * len(outs),
        scratch_shapes=scratch,
        compiler_params=PARAMS,
        cost_estimate=pl.CostEstimate(flops=tiles << 28, transcendentals=tiles << 17, bytes_accessed=tiles << 18),
        name=f"evaluate_{i0}",
    )(*ops)


def small_call(kernel, name, outs, scratch, tiles, ops, in_hbm=()):
    return pl.pallas_call(
        kernel,
        out_shape=[jax.ShapeDtypeStruct(shape, jnp.float32) for shape in outs],
        in_specs=[HBM if k in in_hbm else VM for k in range(len(ops))],
        out_specs=[VM] * len(outs),
        scratch_shapes=scratch,
        compiler_params=pltpu.CompilerParams(vmem_limit_bytes=18 << 20) if in_hbm else PARAMS,
        cost_estimate=pl.CostEstimate(flops=tiles.shape[0] << 27, transcendentals=0, bytes_accessed=tiles.size * 2),
        name=name,
    )(*[pltpu.with_memory_space_constraint(x, pltpu.HBM) if k in in_hbm else x for k, x in enumerate(ops)])


def apply_call(i0, i1, leaf_dev, n, listed, tiles, own, last, prev):
    acc = (leaf_dev + REACH, n, W)
    ops = [listed, tiles, own, *last, *([] if prev is None else [prev])]
    return small_call(
        functools.partial(apply_kernel, i0, i1, leaf_dev, bool(last)),
        f"apply_{i0}",
        [acc, (n, W)] if last else [acc],
        [pltpu.VMEM((leaf_dev, 2 * n, W), jnp.bfloat16)],
        tiles,
        ops,
    )


def edge_call(i0, leaf_dev, n, listed, tiles, own, far, prev):
    acc = (leaf_dev + REACH, n, W)
    return small_call(
        functools.partial(edge_kernel, i0, leaf_dev),
        "apply_edge",
        [acc, (n, REACH * W), (n, W)],
        [
            pltpu.VMEM((leaf_dev, 2 * n, W), jnp.bfloat16),
            pltpu.VMEM((leaf_dev - i0 + REACH, n, W), jnp.float32),
        ],
        tiles,
        [listed, tiles, own, far, prev],
    )


def finish_call(i0, leaf_dev, n, listed, tiles, own, far, prev):
    acc = (leaf_dev + REACH, n, W)
    return small_call(
        functools.partial(finish_kernel, i0, leaf_dev),
        "finish",
        [own.shape],
        [
            pltpu.VMEM((leaf_dev - i0 + REACH, 2 * n, W), jnp.bfloat16),
            pltpu.VMEM(acc, jnp.float32),
            pltpu.VMEM((tiles.shape[0] - 1, *tiles.shape[1:]), jnp.bfloat16),
            pltpu.SemaphoreType.DMA((leaf_dev - i0,)),
        ],
        tiles,
        [listed, tiles, own, far, prev],
        in_hbm=(1,),
    )[0]


def add_edge_kernel(rows_ref, back_ref, out_ref):
    edge = back_ref.shape[1]
    out_ref[:, 0:edge] = rows_ref[:, 0:edge] + back_ref[...]
    out_ref[:, edge:] = rows_ref[:, edge:]


def add_edge_call(rows, back):
    return pl.pallas_call(
        add_edge_kernel,
        out_shape=jax.ShapeDtypeStruct(rows.shape, jnp.float32),
        in_specs=[VM, VM],
        out_specs=VM,
        compiler_params=PARAMS,
        name="add_edge",
    )(rows, back)


def shift(value, by):
    length = lax.axis_size("leaf")
    return lax.ppermute(value, "leaf", [(i, i + by) for i in range(length) if 0 <= i + by < length])


def sum_over_leaf(value, later, beside):
    length = lax.axis_size("leaf")
    value = value + lax.ppermute(value, "leaf", [(i, i ^ 1) for i in range(length)])
    copies = jnp.broadcast_to(value.reshape(-1), (length // 2, value.size))
    copies, later = lax.optimization_barrier((copies, later))
    groups = [[i for i in range(length) if i % 2 == c] for c in range(2)]
    got = lax.all_to_all(
        copies, "leaf", split_axis=0, concat_axis=0, tiled=True, axis_index_groups=groups
    )
    got, done = lax.optimization_barrier((got, beside(later)))
    return jnp.sum(got, axis=0).reshape(value.shape), done


def body(coords, site_order, leaf_pairs, pair_count, probes):
    leaf_dev, width = site_order.shape
    n = probes.shape[0]
    edge = REACH * width
    base = (lax.axis_index("leaf") * leaf_dev).astype(jnp.int32).reshape(1)
    *prepared, packed = prepare_call(leaf_pairs, pair_count, base, coords, site_order, probes)
    far = shift(packed, -1)
    cut0, cut1 = leaf_dev - REACH - 5, leaf_dev - REACH - 2
    evaluate = functools.partial(evaluate_call, leaf_dev=leaf_dev, n=n, prepared=prepared)
    tiles0, acc = evaluate(0, cut0, far=(), own=None, prev=None)
    tiles1, acc, send = evaluate(cut1, leaf_dev, far=(far,), own=None, prev=acc)
    back = shift(send, 1)
    tiles2, image = evaluate(cut0, cut1, far=(), own=probes, prev=acc)
    image = jnp.concatenate([image[:, :edge] + back, image[:, edge:]], axis=1)

    image_far = shift(image[:, :edge], -1)
    common = dict(leaf_dev=leaf_dev, n=n, listed=prepared[0], own=image)
    (acc,) = apply_call(0, cut0, tiles=tiles0, last=(), prev=None, **common)
    acc, send, edge_dots = edge_call(cut1, tiles=tiles1, far=image_far, prev=acc, **common)
    acc, dots = apply_call(cut0, cut1, tiles=tiles2, last=(image_far, edge_dots), prev=acc, **common)
    square = jnp.sum(image * image, axis=1)
    sums = jnp.stack(
        [
            jnp.sum(probes * probes, axis=1),
            jnp.sum(probes * image, axis=1),
            square,
            jnp.sum(dots, axis=1) + NUGGET * square,
        ]
    )

    def beside(send):
        rows = finish_call(cut1, tiles=tiles1, far=image_far, prev=acc, **common)
        return add_edge_call(rows, shift(send, 1))

    (rr, bw, ww, wz), image2 = sum_over_leaf(sums, send, beside)
    alpha = rr / bw
    rr1 = rr - 2.0 * alpha * bw + alpha * alpha * ww
    beta = rr1 / rr
    g = 1.0 + beta
    curve = g * g * bw - 2.0 * g * alpha * ww + alpha * alpha * wz
    alpha1 = rr1 / curve
    c = lambda x: x[:, None]
    direction1 = c(g) * probes - c(alpha) * image
    image1 = c(g) * image - c(alpha) * image2
    solution = c(alpha) * probes + c(alpha1) * direction1
    residual = probes - c(alpha) * image - c(alpha1) * image1
    return solution, residual


def solution(mesh):
    in_specs = (P(None, "leaf"), P("leaf", None), P(None, "leaf"), P("leaf"), P("probe", "leaf"))
    out_specs = (P("probe", "leaf"), P("probe", "leaf"))
    return jax.shard_map(body, mesh=mesh, in_specs=in_specs, out_specs=out_specs, check_vma=False)
```

```python
import functools
import math

import jax
import jax.numpy as jnp
from jax import lax
from jax.experimental import pallas as pl
from jax.experimental.pallas import tpu as pltpu
from jax.sharding import PartitionSpec as P

REACH = 5
STEPS = REACH + 1
UNIT = 0.025
LENGTH = 0.12
NUGGET = 0.5
W = 256
TAPER = REACH * UNIT
DECAY = math.sqrt(3.0) * TAPER / LENGTH
LOG2E = math.log2(math.e)
CHUNK = 16
HALF = W // 2
FLOOR_INV = 1e18
KAPPA = DECAY * LOG2E
PEAK = KAPPA**6 / (4.0 * DECAY) * 2.0**KAPPA
SCALE = KAPPA / TAPER
COMPACT = 20.0 * KAPPA * KAPPA
RANGE = 1e15
TINY = 1e-12
GROUPS = 6


def split2(x):
    hi = x.astype(jnp.bfloat16)
    lo = (x - hi.astype(jnp.float32)).astype(jnp.bfloat16)
    return hi, lo


def split3(x):
    hi = x.astype(jnp.bfloat16)
    rest = x - hi.astype(jnp.float32)
    mid = rest.astype(jnp.bfloat16)
    lo = (rest - mid.astype(jnp.float32)).astype(jnp.bfloat16)
    return hi, mid, lo


def load_values(v_ref, src_ref, leaves, first):
    n = v_ref.shape[1] // 2
    for k in range(leaves):
        hi, lo = split2(src_ref[0:n, k * W : (k + 1) * W])
        v_ref[first + k] = jnp.concatenate([hi, lo], axis=0)


def split_rows(point, center, top, weight):
    x = (point - center) * SCALE
    sq = x * x
    sq = sq[0:1] + sq[1:2] + sq[2:3]
    row = lax.broadcasted_iota(jnp.int32, x.shape, 0)
    x = jnp.where(top, x * weight, jnp.where(row == 3, sq, 0.0))
    hi = x.astype(jnp.bfloat16).astype(jnp.float32)
    rest = x - hi
    mid = rest.astype(jnp.bfloat16).astype(jnp.float32)
    return hi, mid, rest - mid


def prepare_kernel(
    count_ref, base_ref, pairs_hbm, coords_hbm, order_hbm, b_hbm,
    listed_ref, pts_ref, cols_ref, v_ref, center_ref, wide_ref, edge_ref,
    pairs_ref, coords_ref, order_ref, b_ref, sems,
):
    copies = [
        pltpu.make_async_copy(pairs_hbm, pairs_ref, sems.at[0]),
        pltpu.make_async_copy(coords_hbm, coords_ref, sems.at[1]),
        pltpu.make_async_copy(order_hbm, order_ref, sems.at[2]),
        pltpu.make_async_copy(b_hbm, b_ref, sems.at[3]),
    ]
    for copy in copies:
        copy.start()
    copies[0].wait()
    slots = pairs_ref.shape[1]
    row = pairs_ref[0:1, :]
    place = (row - base_ref[0]) * STEPS + pairs_ref[1:2, :] - row
    live = lax.broadcasted_iota(jnp.int32, (1, slots), 1) < count_ref[0]
    place = jnp.where(live, place, -1)
    hit = lax.broadcasted_iota(jnp.int32, (slots, slots), 0) == place
    found = jnp.sum(hit.astype(jnp.float32), axis=1, keepdims=True)
    listed_ref[...] = jnp.broadcast_to(found.astype(jnp.bfloat16)[:, :, None], listed_ref.shape)
    for copy in copies[1:]:
        copy.wait()
    leaves = order_ref.shape[0]
    n = b_ref.shape[0]
    sub = lax.broadcasted_iota(jnp.int32, (W, W), 0).astype(jnp.float32).astype(jnp.bfloat16)
    one, zero = jnp.ones((W, W), jnp.bfloat16), jnp.zeros((W, W), jnp.bfloat16)
    dot = functools.partial(jnp.dot, preferred_element_type=jnp.float32)
    top = lax.broadcasted_iota(jnp.int32, (8, W), 0) < 3
    pad = jnp.zeros((5, W), jnp.float32)
    wide = jnp.zeros((8, W), jnp.float32)
    for k in range(leaves):
        at = slice(k * W, (k + 1) * W)
        order = order_ref[k : k + 1, :].astype(jnp.float32).astype(jnp.bfloat16)
        sel = jnp.where(sub == jnp.broadcast_to(order, (W, W)), one, zero)
        raw = jnp.concatenate([coords_ref[:, at], pad], axis=0)
        parts = dot(jnp.concatenate(split3(raw), axis=0), sel)
        point = parts[0:8] + parts[8:16] + parts[16:24]
        got = point[0:3]
        center = jnp.broadcast_to(jnp.sum(point, axis=1, keepdims=True) * (1.0 / W), (8, W))
        pts_ref[k] = point
        center_ref[k] = center
        hi, mid, lo = split_rows(point, center, top, 1.0)
        square = jnp.where(top, 0.0, hi + mid + lo)
        first = center if k == 0 else first
        far_off = jnp.abs(point - first) * (SCALE * COMPACT / RANGE)
        wide = jnp.maximum(wide, jnp.maximum(square, far_off))
        unit = jnp.where(lax.broadcasted_iota(jnp.int32, (8, W), 0) == 3, 1.0, 0.0)
        stack = [hi, jnp.where(top, hi, mid), jnp.where(top, hi, lo)]
        stack += [jnp.where(top, mid, unit), jnp.where(top, mid, unit), jnp.where(top, lo, unit)]
        cols_ref[k] = jnp.transpose(jnp.concatenate(stack, axis=0)).astype(jnp.bfloat16)
        if k < REACH:
            edge_ref[0:n, at] = b_ref[:, at]
            edge_ref[n : n + 3, at] = got
    wide_ref[...] = wide
    load_values(v_ref, b_ref, leaves, 0)


def spread_rows(bc_ref, points):
    cols = jnp.transpose(points)
    for c in range(3):
        bc_ref[:, c * HALF : (c + 1) * HALF] = jnp.broadcast_to(cols[:, c : c + 1], (W, HALF))


def far_squares(bc_ref, other):
    def block(rows, h):
        u = None
        for c in range(3):
            b = jnp.broadcast_to(other[c : c + 1, h * HALF : (h + 1) * HALF], (CHUNK, HALF))
            d = bc_ref[rows, c * HALF : (c + 1) * HALF] - b
            u = d * d if u is None else u + d * d
        return u * (SCALE * SCALE)

    return block


def near_squares(cols, other, center):
    top = lax.broadcasted_iota(jnp.int32, (8, W), 0) < 3
    one = jnp.where(lax.broadcasted_iota(jnp.int32, (8, W), 0) == 3, 1.0, 0.0)
    hi, mid, lo = split_rows(other, center, top, -2.0)
    stack = [jnp.where(top, hi, one), jnp.where(top, mid, one), jnp.where(top, lo, one)]
    stack += [hi, mid, jnp.where(top, hi, lo)]
    rows = jnp.concatenate(stack, axis=0).astype(jnp.bfloat16)
    all_u = jnp.dot(cols, rows, preferred_element_type=jnp.float32)
    return lambda rows, h: all_u[rows, h * HALF : (h + 1) * HALF]


def make_tile(t_ref, block, same):
    for k in range(W // CHUNK):
        rows = slice(k * CHUNK, (k + 1) * CHUNK)
        lower = k * CHUNK >= HALF
        for h in range(2):
            if same and lower and h == 0:
                t_ref[0, rows, :] = jnp.zeros((CHUNK, HALF), jnp.bfloat16)
                t_ref[2, rows, :] = jnp.zeros((CHUNK, HALF), jnp.bfloat16)
                continue
            u = jnp.minimum(jnp.maximum(block(rows, h), TINY), KAPPA * KAPPA)
            q = u * lax.rsqrt(u)
            t = KAPPA - q
            e = jnp.exp2(t)
            t = t * t
            t = t * t
            x = ((q + KAPPA / 4.0) * (q + KAPPA / DECAY)) * (t * e)
            if same and lower == bool(h):
                x = x * 0.5
            hi, lo = split2(x)
            t_ref[h, rows, :] = hi
            t_ref[2 + h, rows, :] = lo


def product(t_ref, v, listed, transposed):
    hi = jnp.concatenate([t_ref[0], t_ref[1]], axis=1)
    lo = jnp.concatenate([t_ref[2], t_ref[3]], axis=1)
    dims = (((1,), (1 if transposed else 0,)), ((), ()))
    dot = functools.partial(lax.dot_general, dimension_numbers=dims, preferred_element_type=jnp.float32)
    n = v.shape[0] // 2
    keep = jnp.concatenate([listed, listed], axis=1)
    v = v * jnp.concatenate([keep, keep], axis=0)
    p = dot(v, hi)
    return p[:n] + p[n:] + dot(v[:n], lo)


def products(t_ref, vi, vj, listed):
    return product(t_ref, vj, listed, True), product(t_ref, vi, listed, False)


def put_rows(out_ref, acc_ref, first, leaves, own_ref=None):
    for k in range(leaves):
        at = slice(k * W, (k + 1) * W)
        x = acc_ref[first + k] * (1.0 / PEAK)
        out_ref[:, at] = x if own_ref is None else x + NUGGET * own_ref[:, at]


def evaluate_kernel(i0, i1, leaf_dev, last, listed_ref, pts_ref, cols_ref, v_ref, center_ref, wide_ref, *rest):
    rest = list(rest)
    far = i1 + REACH > leaf_dev
    shift_by = 0
    edge_ref = rest.pop(0) if far else None
    own_ref = rest.pop(0) if last else None
    prev_ref = rest.pop(0) if i0 else None
    tiles_ref = rest.pop(0)
    acc_ref = rest.pop(1 if last else 0)
    rows_ref = rest.pop(0) if last or far else None
    bc_ref = rest.pop(0)
    compact = jnp.max(wide_ref[...]) <= COMPACT
    if far:
        pts_all, v_all = rest
        n = v_ref.shape[1] // 2
        own = leaf_dev - i0
        pts_all[0:own] = pts_ref[i0:leaf_dev]
        v_all[0:own] = v_ref[i0:leaf_dev]
        first = center_ref[leaf_dev - 1, 0:3, :]
        pts_all[own:] = jnp.zeros_like(pts_all[own:])
        for k in range(REACH):
            got = edge_ref[n : n + 3, k * W : (k + 1) * W]
            pts_all[own + k, 0:3, :] = got
            far_off = jnp.abs(got - first) * (SCALE * COMPACT / RANGE)
            wide = far_off if k == 0 else jnp.maximum(wide, far_off)
        load_values(v_all, edge_ref, REACH, own)
        compact = compact & (jnp.max(wide) <= COMPACT)
        pts_ref, v_ref = pts_all, v_all
        shift_by = i0
    if i0:
        acc_ref[...] = prev_ref[...]
    else:
        acc_ref[...] = jnp.zeros_like(acc_ref)
    tiles_ref[0] = jnp.zeros_like(tiles_ref[0])

    def finish(i, slot):
        to_row, to_col = products(
            tiles_ref.at[slot], v_ref[i - shift_by], v_ref[i + REACH - shift_by], listed_ref[i * STEPS + REACH]
        )
        acc_ref[i] += to_row
        acc_ref[i + REACH] += to_col

    def near_leaf(i, _):
        slot = (i - i0) * STEPS
        cols = cols_ref[i]
        center = center_ref[i]
        vi = v_ref[i - shift_by]

        def make(d):
            block = near_squares(cols, pts_ref[i + d - shift_by], center)
            make_tile(tiles_ref.at[slot + (1 + d)], block, d == 0)

        make(0)
        finish(jnp.maximum(i - 1, i0), slot)
        total = None
        for d in range(REACH):
            make(d + 1)
            to_row, to_col = products(
                tiles_ref.at[slot + (1 + d)], vi, v_ref[i + d - shift_by], listed_ref[i * STEPS + d]
            )
            total = to_row if total is None else total + to_row
            acc_ref[i + d] += to_col
        acc_ref[i] += total
        return 0

    def far_leaf(i, _):
        slot = (i - i0) * STEPS
        spread_rows(bc_ref, pts_ref[i - shift_by])

        def step(d, _):
            t_ref = tiles_ref.at[slot + (1 + d)]
            block = far_squares(bc_ref, pts_ref.at[i + d - shift_by])
            lax.cond(d == 0, lambda: make_tile(t_ref, block, True), lambda: make_tile(t_ref, block, False))

            @pl.when(d < REACH)
            def _():
                to_row, to_col = products(
                    t_ref, v_ref[i - shift_by], v_ref[i + d - shift_by], listed_ref[i * STEPS + d]
                )
                acc_ref[i] += to_row
                acc_ref[i + d] += to_col

            return 0

        @pl.when(i > i0)
        def _():
            finish(i - 1, slot)

        return lax.fori_loop(0, STEPS, step, 0)

    @pl.when(compact)
    def _():
        lax.fori_loop(i0, i1, near_leaf, 0)

    @pl.when(jnp.logical_not(compact))
    def _():
        lax.fori_loop(i0, i1, far_leaf, 0)

    finish(i1 - 1, (i1 - i0) * STEPS)
    if far:
        put_rows(rows_ref, acc_ref, leaf_dev, REACH)
    if last:
        put_rows(rows_ref, acc_ref, 0, leaf_dev, own_ref)


def clear_or_copy(acc_ref, prev_ref):
    acc_ref[...] = jnp.zeros_like(acc_ref) if prev_ref is None else prev_ref[...]


def weighted(acc_ref, field_ref, first, leaves):
    total = acc_ref[first] * field_ref[:, 0:W]
    for k in range(1, leaves):
        total += acc_ref[first + k] * field_ref[:, k * W : (k + 1) * W]
    return total


def unrolled(start, stop, one):
    for i in range(start, stop):
        one(i, 0)


def apply_kernel(i0, i1, leaf_dev, last, listed_ref, tiles_ref, w_ref, *rest):
    rest = list(rest)
    if last:
        far_ref, extra_ref = rest.pop(0), rest.pop(0)
    prev_ref = rest.pop(0) if i0 else None
    acc_ref = rest.pop(0)
    dots_ref = rest.pop(0) if last else None
    v_ref = rest.pop(0)
    load_values(v_ref, w_ref, leaf_dev, 0)
    clear_or_copy(acc_ref, prev_ref)

    def one_leaf(i, _):
        slot = (i - i0) * STEPS
        vi = v_ref[i]
        total = None
        for d in range(STEPS):
            to_row, to_col = products(
                tiles_ref.at[slot + (1 + d)], vi, v_ref[i + d], listed_ref[i * STEPS + d]
            )
            total = to_row if total is None else total + to_row
            acc_ref[i + d] += to_col
        acc_ref[i] += total
        return 0

    unrolled(i0, i1, one_leaf)
    if last:
        total = weighted(acc_ref, w_ref, 0, leaf_dev) + weighted(acc_ref, far_ref, leaf_dev, REACH)
        dots_ref[...] = (total + extra_ref[...]) * (1.0 / PEAK)


def edge_kernel(i0, leaf_dev, listed_ref, tiles_ref, w_ref, far_ref, prev_ref, acc_ref, send_ref, dots_ref, v_ref, part_ref):
    held = leaf_dev - i0
    load_values(v_ref, w_ref, leaf_dev, 0)
    clear_or_copy(part_ref, None)

    def one_leaf(i, _):
        slot = (i - i0) * STEPS
        vi = v_ref[i]
        for d in range(STEPS):
            part_ref[i - i0 + d] += product(
                tiles_ref.at[slot + (1 + d)], vi, listed_ref[i * STEPS + d], False
            )
        return 0

    unrolled(i0, leaf_dev, one_leaf)
    dots_ref[...] = weighted(part_ref, w_ref.at[:, i0 * W :], 0, held) + weighted(part_ref, far_ref, held, REACH)
    acc_ref[...] = prev_ref[...]
    for k in range(held + REACH):
        acc_ref[i0 + k] += part_ref[k]
    put_rows(send_ref, acc_ref, leaf_dev, REACH)


def finish_kernel(
    i0, leaf_dev, listed_ref, tiles_hbm, w_ref, far_ref, prev_ref, rows_ref, v_ref, acc_ref, tiles_ref, sems
):
    copies = []
    for k in range(leaf_dev - i0):
        at = pl.ds(k * STEPS, STEPS)
        copies.append(pltpu.make_async_copy(tiles_hbm.at[pl.ds(k * STEPS + 1, STEPS)], tiles_ref.at[at], sems.at[k]))
    copies[0].start()
    load_values(v_ref, w_ref.at[:, i0 * W :], leaf_dev - i0, 0)
    load_values(v_ref, far_ref, REACH, leaf_dev - i0)
    acc_ref[...] = prev_ref[...]
    copies[1].start()
    for k, copy in enumerate(copies):
        copy.wait()
        if k + 2 < len(copies):
            copies[k + 2].start()
        total = None
        for d in range(STEPS):
            to_row = product(tiles_ref.at[k * STEPS + d], v_ref[k + d], listed_ref[(i0 + k) * STEPS + d], True)
            total = to_row if total is None else total + to_row
        acc_ref[i0 + k] += total
    put_rows(rows_ref, acc_ref, 0, leaf_dev, w_ref)


VM = pl.BlockSpec(memory_space=pltpu.VMEM)
SM = pl.BlockSpec(memory_space=pltpu.SMEM)
HBM = pl.BlockSpec(memory_space=pltpu.HBM)
PARAMS = pltpu.CompilerParams(vmem_limit_bytes=8 << 20)


def prepare_call(pairs, count, base, coords, order, b):
    leaves = order.shape[0]
    n = b.shape[0]
    return pl.pallas_call(
        prepare_kernel,
        out_shape=(
            jax.ShapeDtypeStruct((pairs.shape[1], 16, HALF), jnp.bfloat16),
            jax.ShapeDtypeStruct((leaves, 8, W), jnp.float32),
            jax.ShapeDtypeStruct((leaves, W, 8 * GROUPS), jnp.bfloat16),
            jax.ShapeDtypeStruct((leaves, 2 * n, W), jnp.bfloat16),
            jax.ShapeDtypeStruct((leaves, 8, W), jnp.float32),
            jax.ShapeDtypeStruct((8, W), jnp.float32),
            jax.ShapeDtypeStruct((n + 3, REACH * W), jnp.float32),
        ),
        in_specs=[SM, SM, HBM, HBM, HBM, HBM],
        out_specs=(VM,) * 7,
        scratch_shapes=[
            pltpu.VMEM(pairs.shape, jnp.int32),
            pltpu.VMEM(coords.shape, jnp.float32),
            pltpu.VMEM(order.shape, jnp.int32),
            pltpu.VMEM(b.shape, jnp.float32),
            pltpu.SemaphoreType.DMA((4,)),
        ],
        compiler_params=PARAMS,
        name="prepare",
    )(count, base, *(pltpu.with_memory_space_constraint(x, pltpu.HBM) for x in (pairs, coords, order, b)))


def shapes_out(leaf_dev, n, far, last):
    acc = (leaf_dev + REACH, n, W)
    rows = (n, (leaf_dev if last else REACH) * W)
    f32 = jnp.float32
    if last:
        return [jax.ShapeDtypeStruct(rows, f32)], [pltpu.VMEM(acc, f32)]
    return [jax.ShapeDtypeStruct(acc, f32)] + ([jax.ShapeDtypeStruct(rows, f32)] if far else []), []


def evaluate_call(i0, i1, leaf_dev, n, prepared, far, own, prev):
    tiles = (i1 - i0) * STEPS
    last = own is not None
    ops = [*prepared, *far, *([own] if last else []), *([] if prev is None else [prev])]
    outs, held_acc = shapes_out(leaf_dev, n, bool(far), last)
    scratch = [*held_acc, pltpu.VMEM((W, 3 * HALF), jnp.float32)]
    if far:
        held = leaf_dev - i0 + REACH
        scratch += [pltpu.VMEM((held, 8, W), jnp.float32), pltpu.VMEM((held, 2 * n, W), jnp.bfloat16)]
    outs = [jax.ShapeDtypeStruct((tiles + 1, 4, W, HALF), jnp.bfloat16), *outs]
    return pl.pallas_call(
        functools.partial(evaluate_kernel, i0, i1, leaf_dev, last),
        out_shape=outs,
        in_specs=[VM] * len(ops),
        out_specs=[VM] * len(outs),
        scratch_shapes=scratch,
        compiler_params=PARAMS,
        cost_estimate=pl.CostEstimate(flops=tiles << 28, transcendentals=tiles << 17, bytes_accessed=tiles << 18),
        name=f"evaluate_{i0}",
    )(*ops)


def small_call(kernel, name, outs, scratch, tiles, ops, in_hbm=()):
    return pl.pallas_call(
        kernel,
        out_shape=[jax.ShapeDtypeStruct(shape, jnp.float32) for shape in outs],
        in_specs=[HBM if k in in_hbm else VM for k in range(len(ops))],
        out_specs=[VM] * len(outs),
        scratch_shapes=scratch,
        compiler_params=pltpu.CompilerParams(vmem_limit_bytes=18 << 20) if in_hbm else PARAMS,
        cost_estimate=pl.CostEstimate(flops=tiles.shape[0] << 27, transcendentals=0, bytes_accessed=tiles.size * 2),
        name=name,
    )(*[pltpu.with_memory_space_constraint(x, pltpu.HBM) if k in in_hbm else x for k, x in enumerate(ops)])


def apply_call(i0, i1, leaf_dev, n, listed, tiles, own, last, prev):
    acc = (leaf_dev + REACH, n, W)
    ops = [listed, tiles, own, *last, *([] if prev is None else [prev])]
    return small_call(
        functools.partial(apply_kernel, i0, i1, leaf_dev, bool(last)),
        f"apply_{i0}",
        [acc, (n, W)] if last else [acc],
        [pltpu.VMEM((leaf_dev, 2 * n, W), jnp.bfloat16)],
        tiles,
        ops,
    )


def edge_call(i0, leaf_dev, n, listed, tiles, own, far, prev):
    acc = (leaf_dev + REACH, n, W)
    return small_call(
        functools.partial(edge_kernel, i0, leaf_dev),
        "apply_edge",
        [acc, (n, REACH * W), (n, W)],
        [
            pltpu.VMEM((leaf_dev, 2 * n, W), jnp.bfloat16),
            pltpu.VMEM((leaf_dev - i0 + REACH, n, W), jnp.float32),
        ],
        tiles,
        [listed, tiles, own, far, prev],
    )


def finish_call(i0, leaf_dev, n, listed, tiles, own, far, prev):
    acc = (leaf_dev + REACH, n, W)
    return small_call(
        functools.partial(finish_kernel, i0, leaf_dev),
        "finish",
        [own.shape],
        [
            pltpu.VMEM((leaf_dev - i0 + REACH, 2 * n, W), jnp.bfloat16),
            pltpu.VMEM(acc, jnp.float32),
            pltpu.VMEM((tiles.shape[0] - 1, *tiles.shape[1:]), jnp.bfloat16),
            pltpu.SemaphoreType.DMA((leaf_dev - i0,)),
        ],
        tiles,
        [listed, tiles, own, far, prev],
        in_hbm=(1,),
    )[0]


def add_edge_kernel(rows_ref, back_ref, out_ref):
    edge = back_ref.shape[1]
    out_ref[:, 0:edge] = rows_ref[:, 0:edge] + back_ref[...]
    out_ref[:, edge:] = rows_ref[:, edge:]


def add_edge_call(rows, back):
    return pl.pallas_call(
        add_edge_kernel,
        out_shape=jax.ShapeDtypeStruct(rows.shape, jnp.float32),
        in_specs=[VM, VM],
        out_specs=VM,
        compiler_params=PARAMS,
        name="add_edge",
    )(rows, back)


def shift(value, by):
    length = lax.axis_size("leaf")
    return lax.ppermute(value, "leaf", [(i, i + by) for i in range(length) if 0 <= i + by < length])


def sum_over_leaf(value, later, beside):
    length = lax.axis_size("leaf")
    value = value + lax.ppermute(value, "leaf", [(i, i ^ 1) for i in range(length)])
    copies = jnp.broadcast_to(value.reshape(-1), (length // 2, value.size))
    copies, later = lax.optimization_barrier((copies, later))
    groups = [[i for i in range(length) if i % 2 == c] for c in range(2)]
    got = lax.all_to_all(
        copies, "leaf", split_axis=0, concat_axis=0, tiled=True, axis_index_groups=groups
    )
    got, done = lax.optimization_barrier((got, beside(later)))
    return jnp.sum(got, axis=0).reshape(value.shape), done


def body(coords, site_order, leaf_pairs, pair_count, probes):
    leaf_dev, width = site_order.shape
    n = probes.shape[0]
    edge = REACH * width
    base = (lax.axis_index("leaf") * leaf_dev).astype(jnp.int32).reshape(1)
    *prepared, packed = prepare_call(leaf_pairs, pair_count, base, coords, site_order, probes)
    far = shift(packed, -1)
    cut0, cut1 = leaf_dev - REACH - 5, leaf_dev - REACH - 1
    evaluate = functools.partial(evaluate_call, leaf_dev=leaf_dev, n=n, prepared=prepared)
    tiles0, acc = evaluate(0, cut0, far=(), own=None, prev=None)
    tiles1, acc, send = evaluate(cut1, leaf_dev, far=(far,), own=None, prev=acc)
    back = shift(send, 1)
    tiles2, image = evaluate(cut0, cut1, far=(), own=probes, prev=acc)
    image = jnp.concatenate([image[:, :edge] + back, image[:, edge:]], axis=1)

    image_far = shift(image[:, :edge], -1)
    common = dict(leaf_dev=leaf_dev, n=n, listed=prepared[0], own=image)
    (acc,) = apply_call(0, cut0, tiles=tiles0, last=(), prev=None, **common)
    acc, send, edge_dots = edge_call(cut1, tiles=tiles1, far=image_far, prev=acc, **common)
    acc, dots = apply_call(cut0, cut1, tiles=tiles2, last=(image_far, edge_dots), prev=acc, **common)
    square = jnp.sum(image * image, axis=1)
    sums = jnp.stack(
        [
            jnp.sum(probes * probes, axis=1),
            jnp.sum(probes * image, axis=1),
            square,
            jnp.sum(dots, axis=1) + NUGGET * square,
        ]
    )

    def beside(send):
        rows = finish_call(cut1, tiles=tiles1, far=image_far, prev=acc, **common)
        return add_edge_call(rows, shift(send, 1))

    (rr, bw, ww, wz), image2 = sum_over_leaf(sums, send, beside)
    alpha = rr / bw
    rr1 = rr - 2.0 * alpha * bw + alpha * alpha * ww
    beta = rr1 / rr
    g = 1.0 + beta
    curve = g * g * bw - 2.0 * g * alpha * ww + alpha * alpha * wz
    alpha1 = rr1 / curve
    c = lambda x: x[:, None]
    direction1 = c(g) * probes - c(alpha) * image
    image1 = c(g) * image - c(alpha) * image2
    solution = c(alpha) * probes + c(alpha1) * direction1
    residual = probes - c(alpha) * image - c(alpha1) * image1
    return solution, residual


def solution(mesh):
    in_specs = (P(None, "leaf"), P("leaf", None), P(None, "leaf"), P("leaf"), P("probe", "leaf"))
    out_specs = (P("probe", "leaf"), P("probe", "leaf"))
    return jax.shard_map(body, mesh=mesh, in_specs=in_specs, out_specs=out_specs, check_vma=False)
```

```python
import functools
import math

import jax
import jax.numpy as jnp
from jax import lax
from jax.experimental import pallas as pl
from jax.experimental.pallas import tpu as pltpu
from jax.sharding import PartitionSpec as P

REACH = 5
STEPS = REACH + 1
UNIT = 0.025
LENGTH = 0.12
NUGGET = 0.5
W = 256
TAPER = REACH * UNIT
DECAY = math.sqrt(3.0) * TAPER / LENGTH
LOG2E = math.log2(math.e)
CHUNK = 16
HALF = W // 2
FLOOR_INV = 1e18
KAPPA = DECAY * LOG2E
PEAK = KAPPA**6 / (4.0 * DECAY) * 2.0**KAPPA
SCALE = KAPPA / TAPER
COMPACT = 20.0 * KAPPA * KAPPA
RANGE = 1e15
TINY = 1e-12
GROUPS = 6


def split2(x):
    hi = x.astype(jnp.bfloat16)
    lo = (x - hi.astype(jnp.float32)).astype(jnp.bfloat16)
    return hi, lo


def split3(x):
    hi = x.astype(jnp.bfloat16)
    rest = x - hi.astype(jnp.float32)
    mid = rest.astype(jnp.bfloat16)
    lo = (rest - mid.astype(jnp.float32)).astype(jnp.bfloat16)
    return hi, mid, lo


def load_values(v_ref, src_ref, leaves, first):
    n = v_ref.shape[1] // 2
    for k in range(leaves):
        hi, lo = split2(src_ref[0:n, k * W : (k + 1) * W])
        v_ref[first + k] = jnp.concatenate([hi, lo], axis=0)


def split_rows(point, center, top, weight):
    x = (point - center) * SCALE
    sq = x * x
    sq = sq[0:1] + sq[1:2] + sq[2:3]
    row = lax.broadcasted_iota(jnp.int32, x.shape, 0)
    x = jnp.where(top, x * weight, jnp.where(row == 3, sq, 0.0))
    hi = x.astype(jnp.bfloat16).astype(jnp.float32)
    rest = x - hi
    mid = rest.astype(jnp.bfloat16).astype(jnp.float32)
    return hi, mid, rest - mid


def prepare_kernel(
    count_ref, base_ref, pairs_hbm, coords_hbm, order_hbm, b_hbm,
    listed_ref, pts_ref, cols_ref, v_ref, center_ref, wide_ref, edge_ref,
    pairs_ref, coords_ref, order_ref, b_ref, sems,
):
    copies = [
        pltpu.make_async_copy(pairs_hbm, pairs_ref, sems.at[0]),
        pltpu.make_async_copy(coords_hbm, coords_ref, sems.at[1]),
        pltpu.make_async_copy(order_hbm, order_ref, sems.at[2]),
        pltpu.make_async_copy(b_hbm, b_ref, sems.at[3]),
    ]
    for copy in copies:
        copy.start()
    copies[0].wait()
    slots = pairs_ref.shape[1]
    row = pairs_ref[0:1, :]
    place = (row - base_ref[0]) * STEPS + pairs_ref[1:2, :] - row
    live = lax.broadcasted_iota(jnp.int32, (1, slots), 1) < count_ref[0]
    place = jnp.where(live, place, -1)
    hit = lax.broadcasted_iota(jnp.int32, (slots, slots), 0) == place
    found = jnp.sum(hit.astype(jnp.float32), axis=1, keepdims=True)
    listed_ref[...] = jnp.broadcast_to(found.astype(jnp.bfloat16)[:, :, None], listed_ref.shape)
    for copy in copies[1:]:
        copy.wait()
    leaves = order_ref.shape[0]
    n = b_ref.shape[0]
    sub = lax.broadcasted_iota(jnp.int32, (W, W), 0).astype(jnp.float32).astype(jnp.bfloat16)
    one, zero = jnp.ones((W, W), jnp.bfloat16), jnp.zeros((W, W), jnp.bfloat16)
    dot = functools.partial(jnp.dot, preferred_element_type=jnp.float32)
    top = lax.broadcasted_iota(jnp.int32, (8, W), 0) < 3
    pad = jnp.zeros((5, W), jnp.float32)
    wide = jnp.zeros((8, W), jnp.float32)
    for k in range(leaves):
        at = slice(k * W, (k + 1) * W)
        order = order_ref[k : k + 1, :].astype(jnp.float32).astype(jnp.bfloat16)
        sel = jnp.where(sub == jnp.broadcast_to(order, (W, W)), one, zero)
        raw = jnp.concatenate([coords_ref[:, at], pad], axis=0)
        parts = dot(jnp.concatenate(split3(raw), axis=0), sel)
        point = parts[0:8] + parts[8:16] + parts[16:24]
        got = point[0:3]
        center = jnp.broadcast_to(jnp.sum(point, axis=1, keepdims=True) * (1.0 / W), (8, W))
        pts_ref[k] = point
        center_ref[k] = center
        hi, mid, lo = split_rows(point, center, top, 1.0)
        square = jnp.where(top, 0.0, hi + mid + lo)
        first = center if k == 0 else first
        far_off = jnp.abs(point - first) * (SCALE * COMPACT / RANGE)
        wide = jnp.maximum(wide, jnp.maximum(square, far_off))
        unit = jnp.where(lax.broadcasted_iota(jnp.int32, (8, W), 0) == 3, 1.0, 0.0)
        stack = [hi, jnp.where(top, hi, mid), jnp.where(top, hi, lo)]
        stack += [jnp.where(top, mid, unit), jnp.where(top, mid, unit), jnp.where(top, lo, unit)]
        cols_ref[k] = jnp.transpose(jnp.concatenate(stack, axis=0)).astype(jnp.bfloat16)
        if k < REACH:
            edge_ref[0:n, at] = b_ref[:, at]
            edge_ref[n : n + 3, at] = got
    wide_ref[...] = wide
    load_values(v_ref, b_ref, leaves, 0)


def spread_rows(bc_ref, points):
    cols = jnp.transpose(points)
    for c in range(3):
        bc_ref[:, c * HALF : (c + 1) * HALF] = jnp.broadcast_to(cols[:, c : c + 1], (W, HALF))


def far_squares(bc_ref, other):
    def block(rows, h):
        u = None
        for c in range(3):
            b = jnp.broadcast_to(other[c : c + 1, h * HALF : (h + 1) * HALF], (CHUNK, HALF))
            d = bc_ref[rows, c * HALF : (c + 1) * HALF] - b
            u = d * d if u is None else u + d * d
        return u * (SCALE * SCALE)

    return block


def near_squares(cols, other, center):
    top = lax.broadcasted_iota(jnp.int32, (8, W), 0) < 3
    one = jnp.where(lax.broadcasted_iota(jnp.int32, (8, W), 0) == 3, 1.0, 0.0)
    hi, mid, lo = split_rows(other, center, top, -2.0)
    stack = [jnp.where(top, hi, one), jnp.where(top, mid, one), jnp.where(top, lo, one)]
    stack += [hi, mid, jnp.where(top, hi, lo)]
    rows = jnp.concatenate(stack, axis=0).astype(jnp.bfloat16)
    all_u = jnp.dot(cols, rows, preferred_element_type=jnp.float32)
    return lambda rows, h: all_u[rows, h * HALF : (h + 1) * HALF]


def make_tile(t_ref, block, same):
    for k in range(W // CHUNK):
        rows = slice(k * CHUNK, (k + 1) * CHUNK)
        lower = k * CHUNK >= HALF
        for h in range(2):
            if same and lower and h == 0:
                t_ref[0, rows, :] = jnp.zeros((CHUNK, HALF), jnp.bfloat16)
                t_ref[2, rows, :] = jnp.zeros((CHUNK, HALF), jnp.bfloat16)
                continue
            u = jnp.minimum(jnp.maximum(block(rows, h), TINY), KAPPA * KAPPA)
            q = u * lax.rsqrt(u)
            t = KAPPA - q
            e = jnp.exp2(t)
            t = t * t
            t = t * t
            x = ((q + KAPPA / 4.0) * (q + KAPPA / DECAY)) * (t * e)
            if same and lower == bool(h):
                x = x * 0.5
            hi, lo = split2(x)
            t_ref[h, rows, :] = hi
            t_ref[2 + h, rows, :] = lo


def product(t_ref, v, listed, transposed):
    hi = jnp.concatenate([t_ref[0], t_ref[1]], axis=1)
    lo = jnp.concatenate([t_ref[2], t_ref[3]], axis=1)
    dims = (((1,), (1 if transposed else 0,)), ((), ()))
    dot = functools.partial(lax.dot_general, dimension_numbers=dims, preferred_element_type=jnp.float32)
    n = v.shape[0] // 2
    keep = jnp.concatenate([listed, listed], axis=1)
    v = v * jnp.concatenate([keep, keep], axis=0)
    p = dot(v, hi)
    return p[:n] + p[n:] + dot(v[:n], lo)


def products(t_ref, vi, vj, listed):
    return product(t_ref, vj, listed, True), product(t_ref, vi, listed, False)


def put_rows(out_ref, acc_ref, first, leaves, own_ref=None):
    for k in range(leaves):
        at = slice(k * W, (k + 1) * W)
        x = acc_ref[first + k] * (1.0 / PEAK)
        out_ref[:, at] = x if own_ref is None else x + NUGGET * own_ref[:, at]


def evaluate_kernel(i0, i1, leaf_dev, last, listed_ref, pts_ref, cols_ref, v_ref, center_ref, wide_ref, *rest):
    rest = list(rest)
    far = i1 + REACH > leaf_dev
    shift_by = 0
    edge_ref = rest.pop(0) if far else None
    own_ref = rest.pop(0) if last else None
    prev_ref = rest.pop(0) if i0 else None
    tiles_ref = rest.pop(0)
    acc_ref = rest.pop(1 if last else 0)
    rows_ref = rest.pop(0) if last or far else None
    bc_ref = rest.pop(0)
    compact = jnp.max(wide_ref[...]) <= COMPACT
    if far:
        pts_all, v_all = rest
        n = v_ref.shape[1] // 2
        own = leaf_dev - i0
        pts_all[0:own] = pts_ref[i0:leaf_dev]
        v_all[0:own] = v_ref[i0:leaf_dev]
        first = center_ref[leaf_dev - 1, 0:3, :]
        pts_all[own:] = jnp.zeros_like(pts_all[own:])
        for k in range(REACH):
            got = edge_ref[n : n + 3, k * W : (k + 1) * W]
            pts_all[own + k, 0:3, :] = got
            far_off = jnp.abs(got - first) * (SCALE * COMPACT / RANGE)
            wide = far_off if k == 0 else jnp.maximum(wide, far_off)
        load_values(v_all, edge_ref, REACH, own)
        compact = compact & (jnp.max(wide) <= COMPACT)
        pts_ref, v_ref = pts_all, v_all
        shift_by = i0
    if i0:
        acc_ref[...] = prev_ref[...]
    else:
        acc_ref[...] = jnp.zeros_like(acc_ref)
    tiles_ref[0] = jnp.zeros_like(tiles_ref[0])

    def finish(i, slot):
        to_row, to_col = products(
            tiles_ref.at[slot], v_ref[i - shift_by], v_ref[i + REACH - shift_by], listed_ref[i * STEPS + REACH]
        )
        acc_ref[i] += to_row
        acc_ref[i + REACH] += to_col

    def near_leaf(i, _):
        slot = (i - i0) * STEPS
        cols = cols_ref[i]
        center = center_ref[i]
        vi = v_ref[i - shift_by]

        def make(d):
            block = near_squares(cols, pts_ref[i + d - shift_by], center)
            make_tile(tiles_ref.at[slot + (1 + d)], block, d == 0)

        make(0)
        finish(jnp.maximum(i - 1, i0), slot)
        total = None
        for d in range(REACH):
            make(d + 1)
            to_row, to_col = products(
                tiles_ref.at[slot + (1 + d)], vi, v_ref[i + d - shift_by], listed_ref[i * STEPS + d]
            )
            total = to_row if total is None else total + to_row
            acc_ref[i + d] += to_col
        acc_ref[i] += total
        return 0

    def far_leaf(i, _):
        slot = (i - i0) * STEPS
        spread_rows(bc_ref, pts_ref[i - shift_by])

        def step(d, _):
            t_ref = tiles_ref.at[slot + (1 + d)]
            block = far_squares(bc_ref, pts_ref.at[i + d - shift_by])
            lax.cond(d == 0, lambda: make_tile(t_ref, block, True), lambda: make_tile(t_ref, block, False))

            @pl.when(d < REACH)
            def _():
                to_row, to_col = products(
                    t_ref, v_ref[i - shift_by], v_ref[i + d - shift_by], listed_ref[i * STEPS + d]
                )
                acc_ref[i] += to_row
                acc_ref[i + d] += to_col

            return 0

        @pl.when(i > i0)
        def _():
            finish(i - 1, slot)

        return lax.fori_loop(0, STEPS, step, 0)

    @pl.when(compact)
    def _():
        lax.fori_loop(i0, i1, near_leaf, 0)

    @pl.when(jnp.logical_not(compact))
    def _():
        lax.fori_loop(i0, i1, far_leaf, 0)

    finish(i1 - 1, (i1 - i0) * STEPS)
    if far:
        put_rows(rows_ref, acc_ref, leaf_dev, REACH)
    if last:
        put_rows(rows_ref, acc_ref, 0, leaf_dev, own_ref)


def clear_or_copy(acc_ref, prev_ref):
    acc_ref[...] = jnp.zeros_like(acc_ref) if prev_ref is None else prev_ref[...]


def weighted(acc_ref, field_ref, first, leaves):
    total = acc_ref[first] * field_ref[:, 0:W]
    for k in range(1, leaves):
        total += acc_ref[first + k] * field_ref[:, k * W : (k + 1) * W]
    return total


def unrolled(start, stop, one):
    for i in range(start, stop):
        one(i, 0)


def apply_kernel(i0, i1, leaf_dev, last, listed_ref, tiles_ref, w_ref, *rest):
    rest = list(rest)
    if last:
        far_ref, extra_ref = rest.pop(0), rest.pop(0)
    prev_ref = rest.pop(0) if i0 else None
    acc_ref = rest.pop(0)
    dots_ref = rest.pop(0) if last else None
    v_ref = rest.pop(0)
    load_values(v_ref, w_ref, leaf_dev, 0)
    clear_or_copy(acc_ref, prev_ref)

    def one_leaf(i, _):
        slot = (i - i0) * STEPS
        vi = v_ref[i]
        total = None
        for d in range(STEPS):
            to_row, to_col = products(
                tiles_ref.at[slot + (1 + d)], vi, v_ref[i + d], listed_ref[i * STEPS + d]
            )
            total = to_row if total is None else total + to_row
            acc_ref[i + d] += to_col
        acc_ref[i] += total
        return 0

    unrolled(i0, i1, one_leaf)
    if last:
        total = weighted(acc_ref, w_ref, 0, leaf_dev) + weighted(acc_ref, far_ref, leaf_dev, REACH)
        dots_ref[...] = (total + extra_ref[...]) * (1.0 / PEAK)


def edge_kernel(i0, leaf_dev, listed_ref, tiles_ref, w_ref, far_ref, prev_ref, acc_ref, send_ref, dots_ref, v_ref, part_ref):
    held = leaf_dev - i0
    load_values(v_ref, w_ref, leaf_dev, 0)
    clear_or_copy(part_ref, None)

    def one_leaf(i, _):
        slot = (i - i0) * STEPS
        vi = v_ref[i]
        for d in range(STEPS):
            part_ref[i - i0 + d] += product(
                tiles_ref.at[slot + (1 + d)], vi, listed_ref[i * STEPS + d], False
            )
        return 0

    unrolled(i0, leaf_dev, one_leaf)
    dots_ref[...] = weighted(part_ref, w_ref.at[:, i0 * W :], 0, held) + weighted(part_ref, far_ref, held, REACH)
    acc_ref[...] = prev_ref[...]
    for k in range(held + REACH):
        acc_ref[i0 + k] += part_ref[k]
    put_rows(send_ref, acc_ref, leaf_dev, REACH)


def finish_kernel(
    i0, leaf_dev, listed_ref, tiles_hbm, w_ref, far_ref, prev_ref, rows_ref, v_ref, acc_ref, tiles_ref, sems
):
    copies = []
    for k in range(leaf_dev - i0):
        at = pl.ds(k * STEPS, STEPS)
        copies.append(pltpu.make_async_copy(tiles_hbm.at[pl.ds(k * STEPS + 1, STEPS)], tiles_ref.at[at], sems.at[k]))
    copies[0].start()
    load_values(v_ref, w_ref.at[:, i0 * W :], leaf_dev - i0, 0)
    load_values(v_ref, far_ref, REACH, leaf_dev - i0)
    acc_ref[...] = prev_ref[...]
    copies[1].start()
    for k, copy in enumerate(copies):
        copy.wait()
        if k + 2 < len(copies):
            copies[k + 2].start()
        total = None
        for d in range(STEPS):
            to_row = product(tiles_ref.at[k * STEPS + d], v_ref[k + d], listed_ref[(i0 + k) * STEPS + d], True)
            total = to_row if total is None else total + to_row
        acc_ref[i0 + k] += total
    put_rows(rows_ref, acc_ref, 0, leaf_dev, w_ref)


VM = pl.BlockSpec(memory_space=pltpu.VMEM)
SM = pl.BlockSpec(memory_space=pltpu.SMEM)
HBM = pl.BlockSpec(memory_space=pltpu.HBM)
PARAMS = pltpu.CompilerParams(vmem_limit_bytes=8 << 20)


def prepare_call(pairs, count, base, coords, order, b):
    leaves = order.shape[0]
    n = b.shape[0]
    return pl.pallas_call(
        prepare_kernel,
        out_shape=(
            jax.ShapeDtypeStruct((pairs.shape[1], 16, HALF), jnp.bfloat16),
            jax.ShapeDtypeStruct((leaves, 8, W), jnp.float32),
            jax.ShapeDtypeStruct((leaves, W, 8 * GROUPS), jnp.bfloat16),
            jax.ShapeDtypeStruct((leaves, 2 * n, W), jnp.bfloat16),
            jax.ShapeDtypeStruct((leaves, 8, W), jnp.float32),
            jax.ShapeDtypeStruct((8, W), jnp.float32),
            jax.ShapeDtypeStruct((n + 3, REACH * W), jnp.float32),
        ),
        in_specs=[SM, SM, HBM, HBM, HBM, HBM],
        out_specs=(VM,) * 7,
        scratch_shapes=[
            pltpu.VMEM(pairs.shape, jnp.int32),
            pltpu.VMEM(coords.shape, jnp.float32),
            pltpu.VMEM(order.shape, jnp.int32),
            pltpu.VMEM(b.shape, jnp.float32),
            pltpu.SemaphoreType.DMA((4,)),
        ],
        compiler_params=PARAMS,
        name="prepare",
    )(count, base, *(pltpu.with_memory_space_constraint(x, pltpu.HBM) for x in (pairs, coords, order, b)))


def shapes_out(leaf_dev, n, far, last):
    acc = (leaf_dev + REACH, n, W)
    rows = (n, (leaf_dev if last else REACH) * W)
    f32 = jnp.float32
    if last:
        return [jax.ShapeDtypeStruct(rows, f32)], [pltpu.VMEM(acc, f32)]
    return [jax.ShapeDtypeStruct(acc, f32)] + ([jax.ShapeDtypeStruct(rows, f32)] if far else []), []


def evaluate_call(i0, i1, leaf_dev, n, prepared, far, own, prev):
    tiles = (i1 - i0) * STEPS
    last = own is not None
    ops = [*prepared, *far, *([own] if last else []), *([] if prev is None else [prev])]
    outs, held_acc = shapes_out(leaf_dev, n, bool(far), last)
    scratch = [*held_acc, pltpu.VMEM((W, 3 * HALF), jnp.float32)]
    if far:
        held = leaf_dev - i0 + REACH
        scratch += [pltpu.VMEM((held, 8, W), jnp.float32), pltpu.VMEM((held, 2 * n, W), jnp.bfloat16)]
    outs = [jax.ShapeDtypeStruct((tiles + 1, 4, W, HALF), jnp.bfloat16), *outs]
    return pl.pallas_call(
        functools.partial(evaluate_kernel, i0, i1, leaf_dev, last),
        out_shape=outs,
        in_specs=[VM] * len(ops),
        out_specs=[VM] * len(outs),
        scratch_shapes=scratch,
        compiler_params=PARAMS,
        cost_estimate=pl.CostEstimate(flops=tiles << 28, transcendentals=tiles << 17, bytes_accessed=tiles << 18),
        name=f"evaluate_{i0}",
    )(*ops)


def small_call(kernel, name, outs, scratch, tiles, ops, in_hbm=()):
    return pl.pallas_call(
        kernel,
        out_shape=[jax.ShapeDtypeStruct(shape, jnp.float32) for shape in outs],
        in_specs=[HBM if k in in_hbm else VM for k in range(len(ops))],
        out_specs=[VM] * len(outs),
        scratch_shapes=scratch,
        compiler_params=pltpu.CompilerParams(vmem_limit_bytes=18 << 20) if in_hbm else PARAMS,
        cost_estimate=pl.CostEstimate(flops=tiles.shape[0] << 27, transcendentals=0, bytes_accessed=tiles.size * 2),
        name=name,
    )(*[pltpu.with_memory_space_constraint(x, pltpu.HBM) if k in in_hbm else x for k, x in enumerate(ops)])


def apply_call(i0, i1, leaf_dev, n, listed, tiles, own, last, prev):
    acc = (leaf_dev + REACH, n, W)
    ops = [listed, tiles, own, *last, *([] if prev is None else [prev])]
    return small_call(
        functools.partial(apply_kernel, i0, i1, leaf_dev, bool(last)),
        f"apply_{i0}",
        [acc, (n, W)] if last else [acc],
        [pltpu.VMEM((leaf_dev, 2 * n, W), jnp.bfloat16)],
        tiles,
        ops,
    )


def edge_call(i0, leaf_dev, n, listed, tiles, own, far, prev):
    acc = (leaf_dev + REACH, n, W)
    return small_call(
        functools.partial(edge_kernel, i0, leaf_dev),
        "apply_edge",
        [acc, (n, REACH * W), (n, W)],
        [
            pltpu.VMEM((leaf_dev, 2 * n, W), jnp.bfloat16),
            pltpu.VMEM((leaf_dev - i0 + REACH, n, W), jnp.float32),
        ],
        tiles,
        [listed, tiles, own, far, prev],
    )


def finish_call(i0, leaf_dev, n, listed, tiles, own, far, prev):
    acc = (leaf_dev + REACH, n, W)
    return small_call(
        functools.partial(finish_kernel, i0, leaf_dev),
        "finish",
        [own.shape],
        [
            pltpu.VMEM((leaf_dev - i0 + REACH, 2 * n, W), jnp.bfloat16),
            pltpu.VMEM(acc, jnp.float32),
            pltpu.VMEM((tiles.shape[0] - 1, *tiles.shape[1:]), jnp.bfloat16),
            pltpu.SemaphoreType.DMA((leaf_dev - i0,)),
        ],
        tiles,
        [listed, tiles, own, far, prev],
        in_hbm=(1,),
    )[0]


def add_edge_kernel(rows_ref, back_ref, out_ref):
    edge = back_ref.shape[1]
    out_ref[:, 0:edge] = rows_ref[:, 0:edge] + back_ref[...]
    out_ref[:, edge:] = rows_ref[:, edge:]


def add_edge_call(rows, back):
    return pl.pallas_call(
        add_edge_kernel,
        out_shape=jax.ShapeDtypeStruct(rows.shape, jnp.float32),
        in_specs=[VM, VM],
        out_specs=VM,
        compiler_params=PARAMS,
        name="add_edge",
    )(rows, back)


def shift(value, by):
    length = lax.axis_size("leaf")
    return lax.ppermute(value, "leaf", [(i, i + by) for i in range(length) if 0 <= i + by < length])


def sum_over_leaf(value, later, beside):
    length = lax.axis_size("leaf")
    value = value + lax.ppermute(value, "leaf", [(i, i ^ 1) for i in range(length)])
    copies = jnp.broadcast_to(value.reshape(-1), (length // 2, value.size))
    copies, later = lax.optimization_barrier((copies, later))
    groups = [[i for i in range(length) if i % 2 == c] for c in range(2)]
    got = lax.all_to_all(
        copies, "leaf", split_axis=0, concat_axis=0, tiled=True, axis_index_groups=groups
    )
    got, done = lax.optimization_barrier((got, beside(later)))
    return jnp.sum(got, axis=0).reshape(value.shape), done


def body(coords, site_order, leaf_pairs, pair_count, probes):
    leaf_dev, width = site_order.shape
    n = probes.shape[0]
    edge = REACH * width
    base = (lax.axis_index("leaf") * leaf_dev).astype(jnp.int32).reshape(1)
    *prepared, packed = prepare_call(leaf_pairs, pair_count, base, coords, site_order, probes)
    far = shift(packed, -1)
    cut0, cut1 = leaf_dev - REACH - 5, leaf_dev - REACH
    evaluate = functools.partial(evaluate_call, leaf_dev=leaf_dev, n=n, prepared=prepared)
    tiles0, acc = evaluate(0, cut0, far=(), own=None, prev=None)
    tiles1, acc, send = evaluate(cut1, leaf_dev, far=(far,), own=None, prev=acc)
    back = shift(send, 1)
    tiles2, image = evaluate(cut0, cut1, far=(), own=probes, prev=acc)
    image = jnp.concatenate([image[:, :edge] + back, image[:, edge:]], axis=1)

    image_far = shift(image[:, :edge], -1)
    common = dict(leaf_dev=leaf_dev, n=n, listed=prepared[0], own=image)
    (acc,) = apply_call(0, cut0, tiles=tiles0, last=(), prev=None, **common)
    acc, send, edge_dots = edge_call(cut1, tiles=tiles1, far=image_far, prev=acc, **common)
    acc, dots = apply_call(cut0, cut1, tiles=tiles2, last=(image_far, edge_dots), prev=acc, **common)
    square = jnp.sum(image * image, axis=1)
    sums = jnp.stack(
        [
            jnp.sum(probes * probes, axis=1),
            jnp.sum(probes * image, axis=1),
            square,
            jnp.sum(dots, axis=1) + NUGGET * square,
        ]
    )

    def beside(send):
        rows = finish_call(cut1, tiles=tiles1, far=image_far, prev=acc, **common)
        return add_edge_call(rows, shift(send, 1))

    (rr, bw, ww, wz), image2 = sum_over_leaf(sums, send, beside)
    alpha = rr / bw
    rr1 = rr - 2.0 * alpha * bw + alpha * alpha * ww
    beta = rr1 / rr
    g = 1.0 + beta
    curve = g * g * bw - 2.0 * g * alpha * ww + alpha * alpha * wz
    alpha1 = rr1 / curve
    c = lambda x: x[:, None]
    direction1 = c(g) * probes - c(alpha) * image
    image1 = c(g) * image - c(alpha) * image2
    solution = c(alpha) * probes + c(alpha1) * direction1
    residual = probes - c(alpha) * image - c(alpha1) * image1
    return solution, residual


def solution(mesh):
    in_specs = (P(None, "leaf"), P("leaf", None), P(None, "leaf"), P("leaf"), P("probe", "leaf"))
    out_specs = (P("probe", "leaf"), P("probe", "leaf"))
    return jax.shard_map(body, mesh=mesh, in_specs=in_specs, out_specs=out_specs, check_vma=False)
```
